32 devices in a mesh: grp: 2 (over x), chol: 16 (over z, y, core).
Axes of the slice: x: 2, y: 2, z: 4, core: 2. Of those that a mesh axis runs over, the one named last changes fastest.
Arguments:
- walkers: bfloat16 [1024, 64, 256], P(('grp', 'chol')), parts along dimension 0, may hold values from -6 to 6
- fields: bfloat16 [1024, 1024], P(('grp', 'chol')), parts along dimension 0, may hold values from -6 to 6
- chol_vectors: bfloat16 [1024, 256, 256], P(None, 'chol'), may hold values from -0.375 to 0.375
- rotated: bfloat16 [1024, 64, 256], P(None, 'chol'), may hold values from -0.046875 to 0.046875
- send_walker: int32 [32, 16, 2], P(('grp', 'chol')), parts along dimension 0, may hold values from -1 to 31, as said below
- slot_row: int32 [1024], P(('grp', 'chol')), parts along dimension 0, may hold values from 0 to 31, as said below
Outputs:
- new_walkers: bfloat16 [1024, 64, 256], P(('grp', 'chol')), parts along dimension 0
- force_bias: float32 [1024, 1024], P(('grp', 'chol')), parts along dimension 0
The draws below stay inside these ranges and needn't reach their ends.
There are 2 independent parts, one for each index of `grp`. The reference program is written for one: setup_inputs(seed, part) draws one part's arguments, and reference() takes and returns one part's arrays. A program takes and returns all parts, laid end to end along the dimension named above; an argument that names none is the same for every part. Nothing has to cross between parts.
Inputs may be any that keep to these rules, and one draw needn't show every extreme that they name: `send_walker`: entry [s, d, c] is the index, among the 32 walkers of block s, of the walker that block s sends as its c-th one to block d, or -1 where it sends none; indices of one [s, d] row come first, -1 after. Some pair of blocks uses all 2 entries. `slot_row`: for every slot of block d, s * 2 + c names a valid entry [s, d, c] of send_walker, and every valid entry is named by exactly one slot of block d.
All inputs are finite; a program needn't handle non-finite values.
Results may differ from the reference program's by a relative error of at most 0.0075.
Values may be sent and summed in bfloat16 or wider, within the bound.
A program may use at most 64 MiB of HBM per device.

```python
import math
import jax
import jax.numpy as jnp
from jax import lax

M = 256
N = 64
NCHOL = 1024
CAP = 2
W_DEV = 32
BLOCKS = 16
WALKERS = 512


def branch_plan(key):
    base = jax.random.fold_in(key, 4111)
    offset = jax.random.randint(jax.random.fold_in(base, 1), (), 0, BLOCKS)
    dest_keys = jax.random.split(jax.random.fold_in(base, 2), BLOCKS)

    def one_dest(dest_key, dest):
        key_a, key_b, key_c = jax.random.split(dest_key, 3)
        doubled = (dest + offset) % BLOCKS
        order = jax.random.permutation(key_a, 2 * (BLOCKS - 1)) % (BLOCKS - 1)
        others = jnp.where(order >= doubled, order + 1, order)[:W_DEV - 2]
        sources = jnp.concatenate([jnp.stack([doubled, doubled]), others]).astype(jnp.int32)
        sources = sources[jax.random.permutation(key_b, W_DEV)]
        walker_index = jax.random.randint(key_c, (W_DEV,), 0, W_DEV).astype(jnp.int32)
        positions = jnp.arange(W_DEV, dtype=jnp.int32)
        same = (sources[:, None] == sources[None, :]) & (positions[None, :] < positions[:, None])
        rank = jnp.sum(same.astype(jnp.int32), axis=1).astype(jnp.int32)
        return (sources, rank, walker_index)
    sources, rank, walker_index = jax.vmap(one_dest)(dest_keys, jnp.arange(BLOCKS, dtype=jnp.int32))
    dest_grid = jnp.broadcast_to(jnp.arange(BLOCKS, dtype=jnp.int32)[:, None], (BLOCKS, W_DEV))
    table = jnp.full((BLOCKS, BLOCKS, CAP), -1, jnp.int32)
    table = table.at[sources.reshape(-1), dest_grid.reshape(-1), rank.reshape(-1)].set(walker_index.reshape(-1))
    rows = (sources * CAP + rank).reshape(-1).astype(jnp.int32)
    return (table, rows)


def draw_send_walker(key, part):
    return branch_plan(key)[0]


def draw_slot_row(key, part):
    return branch_plan(key)[1]


def block_scale(rng, shape, pieces, least, largest):
    loudness = 1.0
    for axis_at, blocks in pieces:
        steps = jax.random.uniform(jax.random.fold_in(jax.random.fold_in(rng, 6), axis_at), (blocks,), jnp.float32, least / len(pieces), largest / len(pieces))
        loudness = loudness * jnp.repeat(jnp.exp(steps), shape[axis_at] // blocks).reshape((-1,) + (1,) * (len(shape) - 1 - axis_at))
    return loudness


def bell_draw(key, shape, spread, bound, pieces=(), kind=jnp.bfloat16):
    array = jax.random.normal(key, shape, jnp.float32) * spread
    if len(pieces) > 0:
        array = block_scale(key, shape, pieces, -0.22, 0.18) * array
    return jnp.clip(array, min=-bound, max=bound).astype(kind)


def setup_inputs(seed: int = 0, part: int = 0) -> dict:
    key_list = jax.random.split(jax.random.key(seed), 7)
    part_splits = jax.random.split(jax.random.fold_in(key_list[6], part), 7)
    walkers = bell_draw(part_splits[0], (WALKERS, N, M), 1.0, 6.0, ((0, 16),))
    fields = bell_draw(part_splits[1], (WALKERS, NCHOL), 1.0, 6.0, ((0, 16),))
    chol_vectors = bell_draw(key_list[2], (NCHOL, M, M), M ** -0.5, 0.375, ((1, 16),))
    rotated = bell_draw(key_list[3], (NCHOL, N, M), (N * M) ** -0.5, 0.046875, ((1, 16),))
    send_walker = draw_send_walker(jax.random.fold_in(jax.random.fold_in(key_list[6], part), 71), part)
    slot_row = draw_slot_row(jax.random.fold_in(jax.random.fold_in(key_list[6], part), 71), part)
    return dict(walkers=walkers, fields=fields, chol_vectors=chol_vectors, rotated=rotated, send_walker=send_walker, slot_row=slot_row)


field_scale = 1.5

def reference(walkers, fields, chol_vectors, rotated, send_walker, slot_row):
    dest = jnp.arange(WALKERS, dtype=jnp.int32) // W_DEV
    source = (slot_row // CAP).astype(jnp.int32)
    rank = (slot_row % CAP).astype(jnp.int32)
    local_index = send_walker[source, dest, rank].astype(jnp.int32)
    parent = (source * W_DEV + local_index).astype(jnp.int32)
    branched = walkers[parent]
    chol_flat = chol_vectors.reshape(NCHOL, M * M)
    rot_flat = rotated.reshape(NCHOL, N * M)
    scale = field_scale / math.sqrt(NCHOL)

    def propagate(blocks):
        field_rows, phi_block = blocks
        operator = (jnp.dot(field_rows, chol_flat, preferred_element_type=jnp.float32) * scale).astype(jnp.bfloat16)
        operator = operator.reshape(W_DEV, M, M)
        total = phi_block.astype(jnp.float32)
        term = phi_block
        for degree in range(1, 6):
            product = jnp.einsum('waj,wij->wai', term.astype(jnp.float32), operator.astype(jnp.float32))
            term = (product / degree).astype(jnp.bfloat16)
            total = total + term.astype(jnp.float32)
        new_block = total.astype(jnp.bfloat16)
        bias = lax.dot_general(new_block.reshape(W_DEV, N * M), rot_flat, (((1,), (1,)), ((), ())), preferred_element_type=jnp.float32)
        return (new_block, bias)
    new_all, bias_all = lax.map(propagate, (fields.reshape(BLOCKS, W_DEV, NCHOL), branched.reshape(BLOCKS, W_DEV, N, M)))
    return (new_all.reshape(WALKERS, N, M), bias_all.reshape(WALKERS, NCHOL))
```

```python
import functools
import math

import jax
import jax.numpy as jnp
from jax import lax
from jax.experimental import pallas as pl
from jax.experimental.pallas import tpu as pltpu
from jax.sharding import PartitionSpec as P

field_scale = 1.5
chunk_slots = 16
degrees = 5
unfold_depth = 64
MESH = pl.DeviceIdType.MESH


def stride_of(blocks):
    return next(h for h in (7, 5, 3, 1) if math.gcd(h, blocks) == 1)


def unfold(source, scratch, target):
    depth, rows, orbitals = source.shape
    step = scratch.shape[1] // rows

    def body(b, carry):
        first = pl.multiple_of(b * step, step)
        block = source[pl.ds(first, step)].astype(jnp.float32).reshape(step * rows, orbitals)
        for h in range(orbitals // 128):
            scratch[h] = block[:, h * 128 : (h + 1) * 128]
        for r in range(rows):
            for h in range(orbitals // 128):
                low = r * orbitals + h * 128
                target[pl.ds(first, step), low : low + 128] = scratch[
                    h, pl.ds(r, step, stride=rows), :
                ].astype(jnp.bfloat16)
        return carry

    lax.fori_loop(0, depth // step, body, 0)


def exchange(me, blocks, send, recv, chunk, send_sem, recv_sem, place=lambda d: d, land=lambda d: d):
    hop = stride_of(blocks)

    def step(k, carry):
        peer = lax.rem(me + k * hop, blocks)
        pltpu.make_async_remote_copy(
            src_ref=send.at[chunk, place(peer)],
            dst_ref=recv.at[chunk, land(me)],
            send_sem=send_sem.at[chunk],
            recv_sem=recv_sem.at[chunk],
            device_id={"chol": peer},
            device_id_type=MESH,
        ).start()
        return carry

    lax.fori_loop(1, blocks, step, 0)
    recv[chunk, land(me)] = send[chunk, place(me)]


def arrived(blocks, recv, chunk, sem):
    whole = recv.at[chunk, pl.ds(0, blocks - 1)]
    pltpu.make_async_copy(whole, whole, sem.at[chunk]).wait()


def kernel(
    dims,
    send_walker,
    slot_row,
    walkers,
    fields,
    chol_hbm,
    rotated_raw,
    new_walkers,
    force_bias,
    chol_raw,
    chol_wide,
    chol,
    rotated_wide,
    rotated,
    all_fields,
    br_send,
    br_recv,
    op_send,
    op_recv,
    op_rows,
    totals,
    nw_send,
    nw_recv,
    pair_send,
    pair_recv,
    pair_own,
    fb_send,
    fb_recv,
    send_sems,
    recv_sems,
    field_sems,
    load_sem,
    op_sems,
):
    blocks, chunks, width, cap, rows, elec = dims
    slots, electrons, orbitals = walkers.shape
    nchol = rotated.shape[0]
    halves = orbitals // 128
    me = lax.axis_index("chol")
    pairs = blocks // 2
    core, pair = lax.rem(me, 2), me // 2
    groups = math.gcd(4, blocks)
    share_of = blocks // groups
    hop = stride_of(blocks)
    load = pltpu.make_async_copy(chol_hbm, chol_raw, load_sem)
    load.start()

    barrier = pltpu.get_barrier_semaphore()

    def greet(k, carry):
        pl.semaphore_signal(
            barrier, inc=1, device_id={"chol": lax.rem(me + k, blocks)}, device_id_type=MESH
        )
        return carry

    lax.fori_loop(1, blocks, greet, 0)

    def pick(d, carry):
        for c in range(cap):
            br_send[0, d, c] = walkers[jnp.maximum(send_walker[d * cap + c], 0)]
        return carry

    lax.fori_loop(0, blocks, pick, 0)
    pl.semaphore_wait(barrier, blocks - 1)

    def share(k, carry):
        pltpu.make_async_remote_copy(
            src_ref=fields,
            dst_ref=all_fields.at[core, pair],
            send_sem=field_sems.at[0],
            recv_sem=field_sems.at[1],
            device_id={"chol": lax.rem(pair + k, pairs) * 2 + core},
            device_id_type=MESH,
        ).start()
        return carry

    lax.fori_loop(1, pairs, share, 0)
    all_fields[core, pair] = fields[...]
    load.wait()
    unfold(chol_raw, chol_wide, chol)
    same_core = all_fields.at[core, pl.ds(0, pairs - 1)]
    pltpu.make_async_copy(same_core, same_core, field_sems.at[1]).wait()
    across = pltpu.make_async_remote_copy(
        src_ref=all_fields.at[core],
        dst_ref=all_fields.at[core],
        send_sem=field_sems.at[2],
        recv_sem=field_sems.at[3],
        device_id={"chol": pair * 2 + 1 - core},
        device_id_type=MESH,
    )
    across.start()
    exchange(me, blocks, br_send, br_recv, 0, send_sems.at[0], recv_sems.at[0])

    across.wait_recv()
    scale = field_scale / math.sqrt(nchol)
    cols = rows * orbitals
    tile = min(512, cols)

    @pl.loop(0, cols // tile)
    def _(n):
        at = pl.ds(pl.multiple_of(n * tile, tile), tile)
        left = all_fields[...].reshape(blocks * slots, nchol)
        part = jnp.dot(left, chol[:, at], preferred_element_type=jnp.float32) * scale
        part = part.astype(jnp.bfloat16).reshape(blocks, chunks, width, tile)
        for q in range(chunks):
            op_send[q, :, :, at] = part[:, q]

    def send_operators(q):
        for group in range(groups):
            def step(k, carry):
                peer = lax.rem(me + k * hop, blocks)
                pltpu.make_async_remote_copy(
                    src_ref=op_send.at[q, place(peer)],
                    dst_ref=op_recv.at[q, me],
                    send_sem=send_sems.at[1, q],
                    recv_sem=op_sems.at[q, group],
                    device_id={"chol": peer},
                    device_id_type=MESH,
                ).start()
                return carry

            lax.fori_loop(max(1, group * share_of), (group + 1) * share_of, step, 0)
        op_recv[q, me] = op_send[q, place(me)]

    def place(d):
        return lax.rem(d, 2) * pairs + d // 2

    def taylor(q):
        def spread(k, carry):
            s = lax.rem(me + (blocks - k) * hop, blocks)
            block = op_recv[q, s].astype(jnp.float32)
            for r in range(rows):
                for h in range(halves):
                    low = r * orbitals + h * 128
                    op_rows[h, pl.ds(s * rows + r, width, stride=orbitals), :] = block[
                        :, low : low + 128
                    ]
            return carry

        for group in range(groups):
            count = share_of - 1 if group == 0 else share_of
            whole = op_recv.at[q, pl.ds(0, count)]
            pltpu.make_async_copy(whole, whole, op_sems.at[q, group]).wait()
            lax.fori_loop(group * share_of, (group + 1) * share_of, spread, 0)
        group = 4

        @pl.loop(0, width // group)
        def _(g):
            ops, terms, sums = [], [], []
            for u in range(group):
                w = g * group + u
                first = pl.ds(pl.multiple_of(w * orbitals, orbitals), orbitals)
                ops.append(
                    jnp.concatenate([op_rows[h, first, :] for h in range(halves)], axis=1).astype(
                        jnp.bfloat16
                    )
                )
                row = slot_row[q * width + w]
                terms.append(br_recv[0, row // cap, row % cap])
                sums.append(terms[u].astype(jnp.float32))
            for degree in range(1, degrees + 1):
                for u in range(group):
                    product = lax.dot_general(
                        terms[u],
                        ops[u],
                        (((1,), (1,)), ((), ())),
                        preferred_element_type=jnp.float32,
                    )
                    terms[u] = (product * (1.0 / degree)).astype(jnp.bfloat16)
                    sums[u] = sums[u] + terms[u].astype(jnp.float32)
            for u in range(group):
                w = g * group + u
                new_walkers[q * width + w] = sums[u].astype(jnp.bfloat16)
                place = pl.ds(pl.multiple_of(w * electrons, electrons), electrons)
                for h in range(halves):
                    totals[h, place, :] = sums[u][:, h * 128 : (h + 1) * 128]

        def turn(d, carry):
            for e in range(elec):
                for h in range(halves):
                    low = e * orbitals + h * 128
                    nw_send[q, d, :, low : low + 128] = totals[
                        h, pl.ds(d * elec + e, width, stride=electrons), :
                    ].astype(jnp.bfloat16)
            return carry

        lax.fori_loop(0, blocks, turn, 0)
        exchange(me, blocks, nw_send, nw_recv, q, send_sems.at[2], recv_sems.at[2], land=place)

    def partial(q, half, target):
        left = nw_recv[q, pl.ds(half * pairs, pairs)].reshape(pairs * width, elec * orbitals)
        step = min(256, nchol)

        @pl.loop(0, nchol // step)
        def _(n):
            at = pl.ds(pl.multiple_of(n * step, step), step)
            target[:, at] = lax.dot_general(
                left, rotated[at, :], (((1,), (1,)), ((), ())), preferred_element_type=jnp.float32
            )

    def bias(q):
        partial(q, 1 - core, pair_send.at[q])
        across = pltpu.make_async_remote_copy(
            src_ref=pair_send.at[q],
            dst_ref=pair_recv.at[q],
            send_sem=send_sems.at[4, q],
            recv_sem=recv_sems.at[4, q],
            device_id={"chol": pair * 2 + 1 - core},
            device_id_type=MESH,
        )
        across.start()
        partial(q, core, pair_own)
        across.wait_recv()
        both = (pair_own[...] + pair_recv[q]).astype(jnp.bfloat16)
        fb_send[q] = both.reshape(pairs, width, nchol)

        def step(k, carry):
            peer = lax.rem(pair + k, pairs)
            pltpu.make_async_remote_copy(
                src_ref=fb_send.at[q, peer],
                dst_ref=fb_recv.at[q, pair],
                send_sem=send_sems.at[3, q],
                recv_sem=recv_sems.at[3, q],
                device_id={"chol": peer * 2 + core},
                device_id_type=MESH,
            ).start()
            return carry

        lax.fori_loop(1, pairs, step, 0)
        fb_recv[q, pair] = fb_send[q, pair]

    def finish(q):
        force_bias[q * width : (q + 1) * width, :] = lax.fori_loop(
            1,
            pairs,
            lambda s, acc: acc + fb_recv[q, s].astype(jnp.float32),
            fb_recv[q, 0].astype(jnp.float32),
        )

    for q in range(min(2, chunks)):
        send_operators(q)
    unfold(rotated_raw, rotated_wide, rotated)
    arrived(blocks, br_recv, 0, recv_sems.at[0])
    for q in range(chunks + 2):
        if q < chunks:
            if q + 2 < chunks:
                send_operators(q + 2)
            taylor(q)
        if 1 <= q <= chunks:
            arrived(blocks, nw_recv, q - 1, recv_sems.at[2])
            bias(q - 1)
        if q >= 2:
            arrived(pairs, fb_recv, q - 2, recv_sems.at[3])
            finish(q - 2)
    arrived(blocks, br_send, 0, send_sems.at[0])
    across.wait_send()
    pltpu.make_async_copy(same_core, same_core, field_sems.at[0]).wait()
    for q in range(chunks):
        arrived(blocks, op_send, q, send_sems.at[1])
        arrived(blocks, nw_send, q, send_sems.at[2])
        arrived(pairs, fb_send, q, send_sems.at[3])
        pltpu.make_async_copy(pair_send.at[q], pair_send.at[q], send_sems.at[4, q]).wait()


def shards(blocks, walkers, fields, chol_vectors, rotated, send_walker, slot_row):
    slots, electrons, orbitals = walkers.shape
    nchol, rows, _ = chol_vectors.shape
    elec = rotated.shape[1]
    cap = send_walker.shape[-1]
    width = min(chunk_slots, slots)
    chunks = slots // width
    dims = (blocks, chunks, width, cap, rows, elec)
    bf16, f32 = jnp.bfloat16, jnp.float32
    vmem, smem = (pl.BlockSpec(memory_space=m) for m in (pltpu.VMEM, pltpu.SMEM))
    return pl.pallas_call(
        functools.partial(kernel, dims),
        out_shape=(
            jax.ShapeDtypeStruct(walkers.shape, bf16),
            jax.ShapeDtypeStruct((slots, nchol), f32),
        ),
        in_specs=[smem, smem, vmem, vmem, pl.BlockSpec(memory_space=pl.ANY), vmem],
        out_specs=(vmem, vmem),
        scratch_shapes=[
            pltpu.VMEM(chol_vectors.shape, bf16),
            pltpu.VMEM((orbitals // 128, rows * unfold_depth, 128), f32),
            pltpu.VMEM((nchol, rows * orbitals), bf16),
            pltpu.VMEM((orbitals // 128, elec * unfold_depth, 128), f32),
            pltpu.VMEM((nchol, elec * orbitals), bf16),
            pltpu.VMEM((2, blocks // 2, slots, nchol), bf16),
            pltpu.VMEM((1, blocks, cap, electrons, orbitals), bf16),
            pltpu.VMEM((1, blocks, cap, electrons, orbitals), bf16),
            pltpu.VMEM((chunks, blocks, width, rows * orbitals), bf16),
            pltpu.VMEM((chunks, blocks, width, rows * orbitals), bf16),
            pltpu.VMEM((orbitals // 128, width * orbitals, 128), f32),
            pltpu.VMEM((orbitals // 128, width * electrons, 128), f32),
            pltpu.VMEM((chunks, blocks, width, elec * orbitals), bf16),
            pltpu.VMEM((chunks, blocks, width, elec * orbitals), bf16),
            pltpu.VMEM((chunks, blocks // 2 * width, nchol), f32),
            pltpu.VMEM((chunks, blocks // 2 * width, nchol), f32),
            pltpu.VMEM((blocks // 2 * width, nchol), f32),
            pltpu.VMEM((chunks, blocks // 2, width, nchol), bf16),
            pltpu.VMEM((chunks, blocks // 2, width, nchol), bf16),
            pltpu.SemaphoreType.DMA((5, chunks)),
            pltpu.SemaphoreType.DMA((5, chunks)),
            pltpu.SemaphoreType.DMA((4,)),
            pltpu.SemaphoreType.DMA,
            pltpu.SemaphoreType.DMA((chunks, math.gcd(4, blocks))),
        ],
        compiler_params=pltpu.CompilerParams(
            collective_id=0, has_side_effects=True, vmem_limit_bytes=60 * 1024 * 1024
        ),
    )(
        send_walker.reshape(-1),
        slot_row,
        walkers,
        fields,
        chol_vectors,
        rotated,
    )


def strided_relay(source, scratch, target, start, count):
    rows, orbitals = source.shape[1:]
    step = min(scratch.shape[1] // rows, count)

    def body(b, carry):
        first = pl.multiple_of(start + b * step, step)
        block = source[pl.ds(first, step)].astype(jnp.float32).reshape(step * rows, orbitals)
        for h in range(orbitals // 128):
            scratch[h, : step * rows] = block[:, h * 128 : (h + 1) * 128]
        for r in range(rows):
            for h in range(orbitals // 128):
                low = r * orbitals + h * 128
                target[pl.ds(first, step), low : low + 128] = scratch[
                    h, pl.ds(r, step, stride=rows), :
                ].astype(jnp.bfloat16)
        return carry

    lax.fori_loop(0, count // step, body, 0)


def parent_kernel(
    dims,
    send_walker,
    slot_row,
    fields,
    walkers_hbm,
    chol_hbm,
    rotated_hbm,
    new_walkers,
    force_bias,
    walkers,
    chol_raw,
    chol_wide,
    chol,
    rotated_raw,
    rotated_wide,
    rotated,
    all_fields,
    left,
    op_wide,
    op_send,
    op_recv,
    totals,
    nw_full,
    nw_send,
    nw_recv,
    part,
    pair_recv,
    fb_send,
    fb_recv,
    fb_total,
    fw_wide,
    fw_send,
    fw_recv,
    fw_rows,
    branch,
    load_sems,
    field_send,
    field_core,
    field_line,
    field_row,
    op_sent,
    op_got,
    nw_sent,
    nw_got,
    br_sent,
    br_got,
    pair_sent,
    pair_got,
    fb_sent,
    fb_got,
    fw_sent,
    fw_got,
):
    blocks, cap, rows, elec = dims
    slots, nchol = fields.shape
    electrons, orbitals = walkers.shape[1:]
    halves = orbitals // 128
    me = lax.axis_index("chol")
    pairs, lines, half = blocks // 2, blocks // 4, blocks // 2
    core, pair = lax.rem(me, 2), me // 2
    line, across = pair // 2, lax.rem(pair, 2)
    side, local = me // half, lax.rem(me, half)
    away = 1 - side
    near = electrons // 2
    bf16, f32 = jnp.bfloat16, jnp.float32

    def wait(ref, sem):
        pltpu.make_async_copy(ref, ref, sem).wait()

    def send(src, dst, sent, got, peer):
        pltpu.make_async_remote_copy(
            src_ref=src,
            dst_ref=dst,
            send_sem=sent,
            recv_sem=got,
            device_id={"chol": peer},
            device_id_type=MESH,
        ).start()

    def far_then_near(far, close):
        def first(t, carry):
            far(away * half + lax.rem(local + t, half))
            return carry

        def second(t, carry):
            close(side * half + lax.rem(local + t, half))
            return carry

        lax.fori_loop(0, half, first, 0)
        lax.fori_loop(1, half, second, 0)

    def row_of(d):
        return lax.rem(d, 2) * pairs + d // 2

    pieces = 4
    span = nchol // pieces
    chol_loads = [
        pltpu.make_async_copy(
            chol_hbm.at[pl.ds(p * span, span)], chol_raw.at[pl.ds(p * span, span)], load_sems.at[p]
        )
        for p in range(pieces)
    ]
    for load in chol_loads:
        load.start()
    walker_load = pltpu.make_async_copy(walkers_hbm, walkers, load_sems.at[pieces])
    rotated_load = pltpu.make_async_copy(rotated_hbm, rotated_raw, load_sems.at[pieces + 1])
    walker_load.start()
    rotated_load.start()

    barrier = pltpu.get_barrier_semaphore()

    def greet(k, carry):
        pl.semaphore_signal(
            barrier, inc=1, device_id={"chol": lax.rem(me + k, blocks)}, device_id_type=MESH
        )
        return carry

    lax.fori_loop(1, blocks, greet, 0)

    order = lax.broadcasted_iota(jnp.int32, (slots, slots), 0)
    place = lax.broadcasted_iota(jnp.int32, (slots, slots), 1)
    chosen = jnp.zeros((slots, slots), f32)
    for p in range(slots):
        entry = slot_row[p]
        target = lax.rem(entry, cap) * blocks + entry // cap
        chosen = jnp.where((place == p) & (order == target), 1.0, chosen)
    all_fields[pair, core] = jnp.dot(
        chosen.astype(bf16), fields[...], preferred_element_type=f32
    ).astype(bf16)

    for p in range(pieces):
        chol_loads[p].wait()
        strided_relay(chol_raw, chol_wide, chol, p * span, span)

    scale = field_scale / math.sqrt(nchol)
    cols = rows * orbitals
    tile = min(512, cols)
    deep = tile // orbitals

    def operators(m):
        @pl.loop(0, cols // tile)
        def _(n):
            at = pl.ds(pl.multiple_of(n * tile, tile), tile)
            out = jnp.dot(left[:m], chol[:, at], preferred_element_type=f32) * scale
            for i in range(deep):
                for h in range(halves):
                    low = i * orbitals + h * 128
                    op_wide[h, pl.ds(n * deep + i, m, stride=rows), :] = out[:, low : low + 128]

    def packed(w):
        first = pl.ds(pl.multiple_of(w * rows, rows), rows)
        return jnp.concatenate([op_wide[h, first, :] for h in range(halves)], axis=1).astype(bf16)

    def chip_operators(which):
        left[:slots] = all_fields[pair, which]
        operators(slots)

        def pack(s, carry):
            for c in range(cap):
                op_send[0, which, c, s] = packed(c * blocks + s)
            return carry

        lax.fori_loop(0, blocks, pack, 0)

    def send_chip_operators(which):
        def to(s):
            send(
                op_send.at[0, which, :, s],
                op_recv.at[:, me, 0, which],
                op_sent.at[cap],
                op_got.at[cap],
                s,
            )

        far_then_near(to, to)
        for c in range(cap):
            op_recv[c, me, 0, which] = op_send[0, which, c, me]

    def other_operators(c, first, count):
        for k in range(count):
            chip = lax.rem(pair + first + k, pairs)
            for q in range(2):
                low = (k * 2 + q) * blocks
                left[low : low + blocks] = all_fields[chip, q, c * blocks : (c + 1) * blocks]
        operators(count * 2 * blocks)

        def pack(s, carry):
            for k in range(count):
                for q in range(2):
                    op_send[first + k, q, c, s] = packed((k * 2 + q) * blocks + s)
            return carry

        lax.fori_loop(0, blocks, pack, 0)

        def to(s):
            send(
                op_send.at[pl.ds(first, count), :, c, s],
                op_recv.at[c, me, pl.ds(first, count)],
                op_sent.at[c],
                op_got.at[c],
                s,
            )

        far_then_near(to, to)
        for k in range(count):
            for q in range(2):
                op_recv[c, me, first + k, q] = op_send[first + k, q, c, me]

    chip_operators(core)
    pl.semaphore_wait(barrier, blocks - 1)

    partner = pair * 2 + 1 - core
    beside = (line * 2 + 1 - across) * 2 + core

    def line_at(j):
        return lax.rem(line + lines - j, lines)

    own = all_fields.at[pair, core]
    send(own, own, field_send.at[0], field_core.at[0], partner)
    for j in range(1, lines):
        peer = (lax.rem(line + j, lines) * 2 + across) * 2 + core
        send(own, own, field_send.at[2], field_line.at[j], peer)
    send(own, own, field_send.at[1], field_row.at[0], beside)
    send_chip_operators(core)

    twin = all_fields.at[pair, 1 - core]
    wait(twin, field_core.at[0])
    chip_operators(1 - core)
    send_chip_operators(1 - core)
    for j in range(1, lines):
        held = all_fields.at[line_at(j) * 2 + across, core]
        wait(held, field_line.at[j])
        send(held, held, field_send.at[1], field_row.at[j], beside)
        send(held, held, field_send.at[0], field_core.at[1], partner)
    for j in range(lines):
        held = all_fields.at[line_at(j) * 2 + 1 - across, core]
        wait(held, field_row.at[j])
        send(held, held, field_send.at[0], field_core.at[1], partner)
    wait(all_fields.at[pl.ds(0, pairs - 1), 0], field_core.at[1])

    split = pairs // 2
    for c in range(cap):
        other_operators(c, 1, split)
        other_operators(c, 1 + split, pairs - 1 - split)

    rotated_load.wait()
    strided_relay(rotated_raw, rotated_wide, rotated, 0, nchol)
    walker_load.wait()

    def taylor(c):
        group = 4

        @pl.loop(0, blocks // group)
        def _(g):
            ops, terms, sums = [], [], []
            for u in range(group):
                r = g * group + u
                chip, q = lax.rem(r, pairs), r // pairs
                ops.append(
                    jnp.concatenate(
                        [
                            op_recv[c, o, lax.rem(chip + pairs - o // 2, pairs), q]
                            for o in range(blocks)
                        ],
                        axis=0,
                    )
                )
                entry = jnp.maximum(send_walker[(chip * 2 + q) * cap + c], 0)
                terms.append(walkers[entry])
                sums.append(terms[u].astype(f32))
            for degree in range(1, degrees + 1):
                for u in range(group):
                    product = lax.dot_general(
                        terms[u], ops[u], (((1,), (1,)), ((), ())), preferred_element_type=f32
                    )
                    terms[u] = (product * (1.0 / degree)).astype(bf16)
                    sums[u] = sums[u] + terms[u].astype(f32)
            for u in range(group):
                r = g * group + u
                nw_full[c, r] = sums[u].astype(bf16)
                at = pl.ds(pl.multiple_of(r * electrons, electrons), electrons)
                for h in range(halves):
                    totals[h, at, :] = sums[u][:, h * 128 : (h + 1) * 128]

        def turn(o, carry):
            for e in range(elec):
                for h in range(halves):
                    low = e * orbitals + h * 128
                    nw_send[c, o, :, low : low + 128] = totals[
                        h, pl.ds(o * elec + e, blocks, stride=electrons), :
                    ].astype(bf16)
            return carry

        lax.fori_loop(0, blocks, turn, 0)

        def to_owner(o):
            send(nw_send.at[c, o], nw_recv.at[c, me], nw_sent.at[c], nw_got.at[c], o)

        far_then_near(to_owner, to_owner)
        nw_recv[c, me] = nw_send[c, me]
        mine = pl.ds(pl.multiple_of(side * near, near), near)

        def to_far(d):
            send(
                nw_full.at[c, row_of(d), mine],
                branch.at[c, me, mine],
                br_sent.at[0],
                br_got.at[0],
                d,
            )

        def to_close(d):
            send(nw_full.at[c, row_of(d)], branch.at[c, me], br_sent.at[0], br_got.at[0], d)

        far_then_near(to_far, to_close)
        branch[c, me] = nw_full[c, row_of(me)]

    def bias(c):
        rows_in = nw_recv[c].reshape(blocks * blocks, elec * orbitals)
        step = min(256, nchol)

        @pl.loop(0, nchol // step)
        def _(n):
            at = pl.ds(pl.multiple_of(n * step, step), step)
            out = lax.dot_general(
                rows_in, rotated[at, :], (((1,), (1,)), ((), ())), preferred_element_type=f32
            ).reshape(blocks, 2, pairs, step)
            for q in range(2):
                mine = out[:, q].reshape(blocks * pairs, step)
                for h in range(step // 128):
                    part[c, q, n * (step // 128) + h] = mine[:, h * 128 : (h + 1) * 128]

        send(part.at[c, 1 - core], pair_recv.at[c], pair_sent.at[c], pair_got.at[c], partner)

    def reduce(c):
        wait(pair_recv.at[c], pair_got.at[c])

        def pick(chip, carry):
            at = pl.ds(chip, blocks, stride=pairs)
            for h in range(nchol // 128):
                both = part[c, core, h, at, :] + pair_recv[c, h, at, :]
                fb_send[c, chip, :, h * 128 : (h + 1) * 128] = both.astype(bf16)
            return carry

        lax.fori_loop(0, pairs, pick, 0)

        def step(k, carry):
            chip = lax.rem(pair + pairs // 2 + k, pairs)

            @pl.when(chip != pair)
            def _():
                send(
                    fb_send.at[c, chip],
                    fb_recv.at[c, pair],
                    fb_sent.at[c],
                    fb_got.at[c],
                    chip * 2 + core,
                )

            return carry

        lax.fori_loop(0, pairs, step, 0)
        fb_recv[c, pair] = fb_send[c, pair]

    def finish(c):
        wait(fb_recv.at[c, pl.ds(0, pairs - 1)], fb_got.at[c])
        fb_total[c] = lax.fori_loop(
            1,
            pairs,
            lambda s, acc: acc + fb_recv[c, s].astype(f32),
            fb_recv[c, 0].astype(f32),
        )

    def forward():
        count = half * blocks
        for c in range(cap):
            block = nw_recv[c, pl.ds(away * half, half)].astype(f32)
            block = block.reshape(count, elec * orbitals)
            for h in range(elec * orbitals // 128):
                fw_wide[h, c * count : (c + 1) * count] = block[:, h * 128 : (h + 1) * 128]

        def gather(t, carry):
            at = pl.ds(row_of(side * half + t), cap * half, stride=blocks)
            for h in range(elec * orbitals // 128):
                fw_send[t, :, h * 128 : (h + 1) * 128] = fw_wide[h, at, :].astype(bf16)
            return carry

        lax.fori_loop(0, half, gather, 0)

        def step(k, carry):
            t = lax.rem(local + k, half)
            send(fw_send.at[t], fw_recv.at[local], fw_sent.at[0], fw_got.at[0], side * half + t)
            return carry

        lax.fori_loop(1, half, step, 0)
        fw_recv[local] = fw_send[local]

    def collect():
        wait(fw_recv.at[pl.ds(0, half - 1)], fw_got.at[0])

        def fold(o, carry):
            block = fw_recv[o].astype(f32)
            for e in range(elec):
                for h in range(halves):
                    low = e * orbitals + h * 128
                    fw_rows[h, pl.ds(o * elec + e, cap * half, stride=near), :] = block[
                        :, low : low + 128
                    ]
            return carry

        lax.fori_loop(0, half, fold, 0)
        wait(branch.at[:, pl.ds(0, half - 1 + half // 2)], br_got.at[0])

        def put(s, carry):
            for c in range(cap):
                at = pl.ds(pl.multiple_of((c * half + s) * near, near), near)
                value = jnp.concatenate([fw_rows[h, at, :] for h in range(halves)], axis=1)
                mine = pl.ds(pl.multiple_of(side * near, near), near)
                branch[c, away * half + s, mine] = value.astype(bf16)
            return carry

        lax.fori_loop(0, half, put, 0)

        def walker_out(p, carry):
            entry = slot_row[p]
            new_walkers[p] = branch[lax.rem(entry, cap), entry // cap]
            return carry

        lax.fori_loop(0, slots, walker_out, 0)

    wait(op_recv.at[:, pl.ds(0, blocks - 1), 0], op_got.at[cap])
    for c in range(cap):
        wait(op_recv.at[c, pl.ds(0, blocks - 1), pl.ds(1, pairs - 1)], op_got.at[c])
        taylor(c)
    for c in range(cap):
        wait(nw_recv.at[c, pl.ds(0, blocks - 1)], nw_got.at[c])
        bias(c)
        if c == cap - 1:
            forward()
        reduce(c)
    collect()
    for c in range(cap):
        finish(c)

    def bias_out(p, carry):
        entry = slot_row[p]
        force_bias[pl.ds(p, 1), :] = fb_total[lax.rem(entry, cap), pl.ds(entry // cap, 1), :]
        return carry

    lax.fori_loop(0, slots, bias_out, 0)

    wait(all_fields.at[:, 0], field_send.at[0])
    wait(all_fields.at[pl.ds(0, lines), 0], field_send.at[1])
    wait(all_fields.at[pl.ds(0, lines - 1), 0], field_send.at[2])
    wait(op_recv.at[:, pl.ds(0, blocks - 1), 0], op_sent.at[cap])
    wait(branch.at[:, pl.ds(0, half - 1 + half // 2)], br_sent.at[0])
    wait(fw_send.at[pl.ds(0, half - 1)], fw_sent.at[0])
    for c in range(cap):
        wait(op_recv.at[c, pl.ds(0, blocks - 1), pl.ds(1, pairs - 1)], op_sent.at[c])
        wait(nw_send.at[c, pl.ds(0, blocks - 1)], nw_sent.at[c])
        wait(pair_recv.at[c], pair_sent.at[c])
        wait(fb_send.at[c, pl.ds(0, pairs - 1)], fb_sent.at[c])


def parent_shards(blocks, walkers, fields, chol_vectors, rotated, send_walker, slot_row):
    slots, electrons, orbitals = walkers.shape
    nchol, rows, _ = chol_vectors.shape
    elec = rotated.shape[1]
    cap = send_walker.shape[-1]
    bf16, f32 = jnp.bfloat16, jnp.float32
    pairs, lines, half = blocks // 2, blocks // 4, blocks // 2
    halves, near = orbitals // 128, electrons // 2
    most = max(pairs // 2 * 2 * blocks, slots)
    wide = elec * orbitals
    vmem, smem, anywhere = (
        pl.BlockSpec(memory_space=m) for m in (pltpu.VMEM, pltpu.SMEM, pl.ANY)
    )
    dma = pltpu.SemaphoreType.DMA
    return pl.pallas_call(
        functools.partial(parent_kernel, (blocks, cap, rows, elec)),
        out_shape=(
            jax.ShapeDtypeStruct(walkers.shape, bf16),
            jax.ShapeDtypeStruct((slots, nchol), f32),
        ),
        in_specs=[smem, smem, vmem, anywhere, anywhere, anywhere],
        out_specs=(vmem, vmem),
        scratch_shapes=[
            pltpu.VMEM(walkers.shape, bf16),
            pltpu.VMEM(chol_vectors.shape, bf16),
            pltpu.VMEM((halves, rows * unfold_depth, 128), f32),
            pltpu.VMEM((nchol, rows * orbitals), bf16),
            pltpu.VMEM(rotated.shape, bf16),
            pltpu.VMEM((halves, elec * unfold_depth, 128), f32),
            pltpu.VMEM((nchol, wide), bf16),
            pltpu.VMEM((pairs, 2, slots, nchol), bf16),
            pltpu.VMEM((most, nchol), bf16),
            pltpu.VMEM((halves, most * rows, 128), f32),
            pltpu.VMEM((pairs, 2, cap, blocks, rows, orbitals), bf16),
            pltpu.VMEM((cap, blocks, pairs, 2, rows, orbitals), bf16),
            pltpu.VMEM((halves, blocks * electrons, 128), f32),
            pltpu.VMEM((cap, blocks, electrons, orbitals), bf16),
            pltpu.VMEM((cap, blocks, blocks, wide), bf16),
            pltpu.VMEM((cap, blocks, blocks, wide), bf16),
            pltpu.VMEM((cap, 2, nchol // 128, blocks * pairs, 128), f32),
            pltpu.VMEM((cap, nchol // 128, blocks * pairs, 128), f32),
            pltpu.VMEM((cap, pairs, blocks, nchol), bf16),
            pltpu.VMEM((cap, pairs, blocks, nchol), bf16),
            pltpu.VMEM((cap, blocks, nchol), f32),
            pltpu.VMEM((wide // 128, cap * half * blocks, 128), f32),
            pltpu.VMEM((half, cap * half, wide), bf16),
            pltpu.VMEM((half, cap * half, wide), bf16),
            pltpu.VMEM((halves, cap * half * near, 128), f32),
            pltpu.VMEM((cap, blocks, electrons, orbitals), bf16),
            dma((6,)),
            dma((3,)),
            dma((2,)),
            dma((lines,)),
            dma((lines,)),
            dma((cap + 1,)),
            dma((cap + 1,)),
            dma((cap,)),
            dma((cap,)),
            dma((1,)),
            dma((1,)),
            dma((cap,)),
            dma((cap,)),
            dma((cap,)),
            dma((cap,)),
            dma((1,)),
            dma((1,)),
        ],
        compiler_params=pltpu.CompilerParams(
            collective_id=1, has_side_effects=True, vmem_limit_bytes=60 * 1024 * 1024
        ),
    )(send_walker.reshape(-1), slot_row, fields, walkers, chol_vectors, rotated)


def plan(blocks, walkers, fields, chol_vectors, rotated, send_walker, slot_row):
    every_entry = blocks * send_walker.shape[-1] == walkers.shape[0]
    step = parent_shards if every_entry and blocks % 8 == 0 else shards
    return step(blocks, walkers, fields, chol_vectors, rotated, send_walker, slot_row)


def solution(mesh):
    in_specs = (
        P(("grp", "chol"), None, None),
        P(("grp", "chol"), None),
        P(None, "chol", None),
        P(None, "chol", None),
        P(("grp", "chol"), None, None),
        P(("grp", "chol")),
    )
    out_specs = (P(("grp", "chol"), None, None), P(("grp", "chol"), None))
    return jax.shard_map(
        functools.partial(plan, mesh.shape["chol"]),
        mesh=mesh,
        in_specs=in_specs,
        out_specs=out_specs,
        check_vma=False,
    )
```

```python
import functools
import math

import jax
import jax.numpy as jnp
from jax import lax
from jax.experimental import pallas as pl
from jax.experimental.pallas import tpu as pltpu
from jax.sharding import PartitionSpec as P

field_scale = 1.5
chunk_slots = 16
degrees = 5
unfold_depth = 64
MESH = pl.DeviceIdType.MESH


def stride_of(blocks):
    return next(h for h in (7, 5, 3, 1) if math.gcd(h, blocks) == 1)


def unfold(source, scratch, target):
    depth, rows, orbitals = source.shape
    step = scratch.shape[1] // rows

    def body(b, carry):
        first = pl.multiple_of(b * step, step)
        block = source[pl.ds(first, step)].astype(jnp.float32).reshape(step * rows, orbitals)
        for h in range(orbitals // 128):
            scratch[h] = block[:, h * 128 : (h + 1) * 128]
        for r in range(rows):
            for h in range(orbitals // 128):
                low = r * orbitals + h * 128
                target[pl.ds(first, step), low : low + 128] = scratch[
                    h, pl.ds(r, step, stride=rows), :
                ].astype(jnp.bfloat16)
        return carry

    lax.fori_loop(0, depth // step, body, 0)


def exchange(me, blocks, send, recv, chunk, send_sem, recv_sem, place=lambda d: d, land=lambda d: d):
    hop = stride_of(blocks)

    def step(k, carry):
        peer = lax.rem(me + k * hop, blocks)
        pltpu.make_async_remote_copy(
            src_ref=send.at[chunk, place(peer)],
            dst_ref=recv.at[chunk, land(me)],
            send_sem=send_sem.at[chunk],
            recv_sem=recv_sem.at[chunk],
            device_id={"chol": peer},
            device_id_type=MESH,
        ).start()
        return carry

    lax.fori_loop(1, blocks, step, 0)
    recv[chunk, land(me)] = send[chunk, place(me)]


def arrived(blocks, recv, chunk, sem):
    whole = recv.at[chunk, pl.ds(0, blocks - 1)]
    pltpu.make_async_copy(whole, whole, sem.at[chunk]).wait()


def kernel(
    dims,
    send_walker,
    slot_row,
    walkers,
    fields,
    chol_hbm,
    rotated_raw,
    new_walkers,
    force_bias,
    chol_raw,
    chol_wide,
    chol,
    rotated_wide,
    rotated,
    all_fields,
    br_send,
    br_recv,
    op_send,
    op_recv,
    op_rows,
    totals,
    nw_send,
    nw_recv,
    pair_send,
    pair_recv,
    pair_own,
    fb_send,
    fb_recv,
    send_sems,
    recv_sems,
    field_sems,
    load_sem,
    op_sems,
):
    blocks, chunks, width, cap, rows, elec = dims
    slots, electrons, orbitals = walkers.shape
    nchol = rotated.shape[0]
    halves = orbitals // 128
    me = lax.axis_index("chol")
    pairs = blocks // 2
    core, pair = lax.rem(me, 2), me // 2
    groups = math.gcd(4, blocks)
    share_of = blocks // groups
    hop = stride_of(blocks)
    load = pltpu.make_async_copy(chol_hbm, chol_raw, load_sem)
    load.start()

    barrier = pltpu.get_barrier_semaphore()

    def greet(k, carry):
        pl.semaphore_signal(
            barrier, inc=1, device_id={"chol": lax.rem(me + k, blocks)}, device_id_type=MESH
        )
        return carry

    lax.fori_loop(1, blocks, greet, 0)

    def pick(d, carry):
        for c in range(cap):
            br_send[0, d, c] = walkers[jnp.maximum(send_walker[d * cap + c], 0)]
        return carry

    lax.fori_loop(0, blocks, pick, 0)
    pl.semaphore_wait(barrier, blocks - 1)

    def share(k, carry):
        pltpu.make_async_remote_copy(
            src_ref=fields,
            dst_ref=all_fields.at[core, pair],
            send_sem=field_sems.at[0],
            recv_sem=field_sems.at[1],
            device_id={"chol": lax.rem(pair + k, pairs) * 2 + core},
            device_id_type=MESH,
        ).start()
        return carry

    lax.fori_loop(1, pairs, share, 0)
    all_fields[core, pair] = fields[...]
    load.wait()
    unfold(chol_raw, chol_wide, chol)
    same_core = all_fields.at[core, pl.ds(0, pairs - 1)]
    pltpu.make_async_copy(same_core, same_core, field_sems.at[1]).wait()
    across = pltpu.make_async_remote_copy(
        src_ref=all_fields.at[core],
        dst_ref=all_fields.at[core],
        send_sem=field_sems.at[2],
        recv_sem=field_sems.at[3],
        device_id={"chol": pair * 2 + 1 - core},
        device_id_type=MESH,
    )
    across.start()
    exchange(me, blocks, br_send, br_recv, 0, send_sems.at[0], recv_sems.at[0])

    across.wait_recv()
    scale = field_scale / math.sqrt(nchol)
    cols = rows * orbitals
    tile = min(512, cols)

    @pl.loop(0, cols // tile)
    def _(n):
        at = pl.ds(pl.multiple_of(n * tile, tile), tile)
        left = all_fields[...].reshape(blocks * slots, nchol)
        part = jnp.dot(left, chol[:, at], preferred_element_type=jnp.float32) * scale
        part = part.astype(jnp.bfloat16).reshape(blocks, chunks, width, tile)
        for q in range(chunks):
            op_send[q, :, :, at] = part[:, q]

    def send_operators(q):
        for group in range(groups):
            def step(k, carry):
                peer = lax.rem(me + k * hop, blocks)
                pltpu.make_async_remote_copy(
                    src_ref=op_send.at[q, place(peer)],
                    dst_ref=op_recv.at[q, me],
                    send_sem=send_sems.at[1, q],
                    recv_sem=op_sems.at[q, group],
                    device_id={"chol": peer},
                    device_id_type=MESH,
                ).start()
                return carry

            lax.fori_loop(max(1, group * share_of), (group + 1) * share_of, step, 0)
        op_recv[q, me] = op_send[q, place(me)]

    def place(d):
        return lax.rem(d, 2) * pairs + d // 2

    def taylor(q):
        def spread(k, carry):
            s = lax.rem(me + (blocks - k) * hop, blocks)
            block = op_recv[q, s].astype(jnp.float32)
            for r in range(rows):
                for h in range(halves):
                    low = r * orbitals + h * 128
                    op_rows[h, pl.ds(s * rows + r, width, stride=orbitals), :] = block[
                        :, low : low + 128
                    ]
            return carry

        for group in range(groups):
            count = share_of - 1 if group == 0 else share_of
            whole = op_recv.at[q, pl.ds(0, count)]
            pltpu.make_async_copy(whole, whole, op_sems.at[q, group]).wait()
            lax.fori_loop(group * share_of, (group + 1) * share_of, spread, 0)
        group = 4

        @pl.loop(0, width // group)
        def _(g):
            ops, terms, sums = [], [], []
            for u in range(group):
                w = g * group + u
                first = pl.ds(pl.multiple_of(w * orbitals, orbitals), orbitals)
                ops.append(
                    jnp.concatenate([op_rows[h, first, :] for h in range(halves)], axis=1).astype(
                        jnp.bfloat16
                    )
                )
                row = slot_row[q * width + w]
                terms.append(br_recv[0, row // cap, row % cap])
                sums.append(terms[u].astype(jnp.float32))
            for degree in range(1, degrees + 1):
                for u in range(group):
                    product = lax.dot_general(
                        terms[u],
                        ops[u],
                        (((1,), (1,)), ((), ())),
                        preferred_element_type=jnp.float32,
                    )
                    terms[u] = (product * (1.0 / degree)).astype(jnp.bfloat16)
                    sums[u] = sums[u] + terms[u].astype(jnp.float32)
            for u in range(group):
                w = g * group + u
                new_walkers[q * width + w] = sums[u].astype(jnp.bfloat16)
                place = pl.ds(pl.multiple_of(w * electrons, electrons), electrons)
                for h in range(halves):
                    totals[h, place, :] = sums[u][:, h * 128 : (h + 1) * 128]

        def turn(d, carry):
            for e in range(elec):
                for h in range(halves):
                    low = e * orbitals + h * 128
                    nw_send[q, d, :, low : low + 128] = totals[
                        h, pl.ds(d * elec + e, width, stride=electrons), :
                    ].astype(jnp.bfloat16)
            return carry

        lax.fori_loop(0, blocks, turn, 0)
        exchange(me, blocks, nw_send, nw_recv, q, send_sems.at[2], recv_sems.at[2], land=place)

    def partial(q, half, target):
        left = nw_recv[q, pl.ds(half * pairs, pairs)].reshape(pairs * width, elec * orbitals)
        step = min(256, nchol)

        @pl.loop(0, nchol // step)
        def _(n):
            at = pl.ds(pl.multiple_of(n * step, step), step)
            target[:, at] = lax.dot_general(
                left, rotated[at, :], (((1,), (1,)), ((), ())), preferred_element_type=jnp.float32
            )

    def bias(q):
        partial(q, 1 - core, pair_send.at[q])
        across = pltpu.make_async_remote_copy(
            src_ref=pair_send.at[q],
            dst_ref=pair_recv.at[q],
            send_sem=send_sems.at[4, q],
            recv_sem=recv_sems.at[4, q],
            device_id={"chol": pair * 2 + 1 - core},
            device_id_type=MESH,
        )
        across.start()
        partial(q, core, pair_own)
        across.wait_recv()
        both = (pair_own[...] + pair_recv[q]).astype(jnp.bfloat16)
        fb_send[q] = both.reshape(pairs, width, nchol)

        def step(k, carry):
            peer = lax.rem(pair + k, pairs)
            pltpu.make_async_remote_copy(
                src_ref=fb_send.at[q, peer],
                dst_ref=fb_recv.at[q, pair],
                send_sem=send_sems.at[3, q],
                recv_sem=recv_sems.at[3, q],
                device_id={"chol": peer * 2 + core},
                device_id_type=MESH,
            ).start()
            return carry

        lax.fori_loop(1, pairs, step, 0)
        fb_recv[q, pair] = fb_send[q, pair]

    def finish(q):
        force_bias[q * width : (q + 1) * width, :] = lax.fori_loop(
            1,
            pairs,
            lambda s, acc: acc + fb_recv[q, s].astype(jnp.float32),
            fb_recv[q, 0].astype(jnp.float32),
        )

    for q in range(min(2, chunks)):
        send_operators(q)
    unfold(rotated_raw, rotated_wide, rotated)
    arrived(blocks, br_recv, 0, recv_sems.at[0])
    for q in range(chunks + 2):
        if q < chunks:
            if q + 2 < chunks:
                send_operators(q + 2)
            taylor(q)
        if 1 <= q <= chunks:
            arrived(blocks, nw_recv, q - 1, recv_sems.at[2])
            bias(q - 1)
        if q >= 2:
            arrived(pairs, fb_recv, q - 2, recv_sems.at[3])
            finish(q - 2)
    arrived(blocks, br_send, 0, send_sems.at[0])
    across.wait_send()
    pltpu.make_async_copy(same_core, same_core, field_sems.at[0]).wait()
    for q in range(chunks):
        arrived(blocks, op_send, q, send_sems.at[1])
        arrived(blocks, nw_send, q, send_sems.at[2])
        arrived(pairs, fb_send, q, send_sems.at[3])
        pltpu.make_async_copy(pair_send.at[q], pair_send.at[q], send_sems.at[4, q]).wait()


def shards(blocks, walkers, fields, chol_vectors, rotated, send_walker, slot_row):
    slots, electrons, orbitals = walkers.shape
    nchol, rows, _ = chol_vectors.shape
    elec = rotated.shape[1]
    cap = send_walker.shape[-1]
    width = min(chunk_slots, slots)
    chunks = slots // width
    dims = (blocks, chunks, width, cap, rows, elec)
    bf16, f32 = jnp.bfloat16, jnp.float32
    vmem, smem = (pl.BlockSpec(memory_space=m) for m in (pltpu.VMEM, pltpu.SMEM))
    return pl.pallas_call(
        functools.partial(kernel, dims),
        out_shape=(
            jax.ShapeDtypeStruct(walkers.shape, bf16),
            jax.ShapeDtypeStruct((slots, nchol), f32),
        ),
        in_specs=[smem, smem, vmem, vmem, pl.BlockSpec(memory_space=pl.ANY), vmem],
        out_specs=(vmem, vmem),
        scratch_shapes=[
            pltpu.VMEM(chol_vectors.shape, bf16),
            pltpu.VMEM((orbitals // 128, rows * unfold_depth, 128), f32),
            pltpu.VMEM((nchol, rows * orbitals), bf16),
            pltpu.VMEM((orbitals // 128, elec * unfold_depth, 128), f32),
            pltpu.VMEM((nchol, elec * orbitals), bf16),
            pltpu.VMEM((2, blocks // 2, slots, nchol), bf16),
            pltpu.VMEM((1, blocks, cap, electrons, orbitals), bf16),
            pltpu.VMEM((1, blocks, cap, electrons, orbitals), bf16),
            pltpu.VMEM((chunks, blocks, width, rows * orbitals), bf16),
            pltpu.VMEM((chunks, blocks, width, rows * orbitals), bf16),
            pltpu.VMEM((orbitals // 128, width * orbitals, 128), f32),
            pltpu.VMEM((orbitals // 128, width * electrons, 128), f32),
            pltpu.VMEM((chunks, blocks, width, elec * orbitals), bf16),
            pltpu.VMEM((chunks, blocks, width, elec * orbitals), bf16),
            pltpu.VMEM((chunks, blocks // 2 * width, nchol), f32),
            pltpu.VMEM((chunks, blocks // 2 * width, nchol), f32),
            pltpu.VMEM((blocks // 2 * width, nchol), f32),
            pltpu.VMEM((chunks, blocks // 2, width, nchol), bf16),
            pltpu.VMEM((chunks, blocks // 2, width, nchol), bf16),
            pltpu.SemaphoreType.DMA((5, chunks)),
            pltpu.SemaphoreType.DMA((5, chunks)),
            pltpu.SemaphoreType.DMA((4,)),
            pltpu.SemaphoreType.DMA,
            pltpu.SemaphoreType.DMA((chunks, math.gcd(4, blocks))),
        ],
        compiler_params=pltpu.CompilerParams(
            collective_id=0, has_side_effects=True, vmem_limit_bytes=60 * 1024 * 1024
        ),
    )(
        send_walker.reshape(-1),
        slot_row,
        walkers,
        fields,
        chol_vectors,
        rotated,
    )


def strided_relay(source, scratch, target, start, count):
    rows, orbitals = source.shape[1:]
    step = min(scratch.shape[1] // rows, count)

    def body(b, carry):
        first = pl.multiple_of(start + b * step, step)
        block = source[pl.ds(first, step)].astype(jnp.float32).reshape(step * rows, orbitals)
        for h in range(orbitals // 128):
            scratch[h, : step * rows] = block[:, h * 128 : (h + 1) * 128]
        for r in range(rows):
            for h in range(orbitals // 128):
                low = r * orbitals + h * 128
                target[pl.ds(first, step), low : low + 128] = scratch[
                    h, pl.ds(r, step, stride=rows), :
                ].astype(jnp.bfloat16)
        return carry

    lax.fori_loop(0, count // step, body, 0)


def parent_kernel(
    dims,
    send_walker,
    slot_row,
    fields,
    walkers_hbm,
    chol_hbm,
    rotated_hbm,
    new_walkers,
    force_bias,
    walkers,
    chol_raw,
    chol_wide,
    chol,
    rotated_raw,
    rotated_wide,
    rotated,
    all_fields,
    left,
    op_wide,
    op_send,
    op_recv,
    totals,
    nw_full,
    nw_send,
    nw_recv,
    part,
    pair_recv,
    row_send,
    row_recv,
    fb_send,
    fb_recv,
    fb_total,
    fw_wide,
    fw_send,
    fw_recv,
    fw_rows,
    branch,
    load_sems,
    field_send,
    field_core,
    field_line,
    field_row,
    op_sent,
    op_got,
    nw_sent,
    nw_got,
    br_sent,
    br_got,
    pair_sent,
    pair_got,
    row_sent,
    row_got,
    fb_sent,
    fb_got,
    fw_sent,
    fw_got,
):
    blocks, cap, rows, elec = dims
    slots, nchol = fields.shape
    electrons, orbitals = walkers.shape[1:]
    halves = orbitals // 128
    me = lax.axis_index("chol")
    pairs, lines, half = blocks // 2, blocks // 4, blocks // 2
    core, pair = lax.rem(me, 2), me // 2
    line, across = pair // 2, lax.rem(pair, 2)
    side, local = me // half, lax.rem(me, half)
    away = 1 - side
    near = electrons // 2
    bf16, f32 = jnp.bfloat16, jnp.float32

    def wait(ref, sem):
        pltpu.make_async_copy(ref, ref, sem).wait()

    def send(src, dst, sent, got, peer):
        pltpu.make_async_remote_copy(
            src_ref=src,
            dst_ref=dst,
            send_sem=sent,
            recv_sem=got,
            device_id={"chol": peer},
            device_id_type=MESH,
        ).start()

    def far_then_near(far, close):
        def first(t, carry):
            far(away * half + lax.rem(local + t, half))
            return carry

        def second(t, carry):
            close(side * half + lax.rem(local + t, half))
            return carry

        lax.fori_loop(0, half, first, 0)
        lax.fori_loop(1, half, second, 0)

    def row_of(d):
        return lax.rem(d, 2) * pairs + d // 2

    pieces = 4
    span = nchol // pieces
    chol_loads = [
        pltpu.make_async_copy(
            chol_hbm.at[pl.ds(p * span, span)], chol_raw.at[pl.ds(p * span, span)], load_sems.at[p]
        )
        for p in range(pieces)
    ]
    for load in chol_loads:
        load.start()
    walker_load = pltpu.make_async_copy(walkers_hbm, walkers, load_sems.at[pieces])
    rotated_load = pltpu.make_async_copy(rotated_hbm, rotated_raw, load_sems.at[pieces + 1])
    walker_load.start()
    rotated_load.start()

    barrier = pltpu.get_barrier_semaphore()

    def greet(k, carry):
        pl.semaphore_signal(
            barrier, inc=1, device_id={"chol": lax.rem(me + k, blocks)}, device_id_type=MESH
        )
        return carry

    lax.fori_loop(1, blocks, greet, 0)

    order = lax.broadcasted_iota(jnp.int32, (slots, slots), 0)
    place = lax.broadcasted_iota(jnp.int32, (slots, slots), 1)
    chosen = jnp.zeros((slots, slots), f32)
    for p in range(slots):
        entry = slot_row[p]
        target = lax.rem(entry, cap) * blocks + entry // cap
        chosen = jnp.where((place == p) & (order == target), 1.0, chosen)
    all_fields[pair, core] = jnp.dot(
        chosen.astype(bf16), fields[...], preferred_element_type=f32
    ).astype(bf16)

    for p in range(pieces):
        chol_loads[p].wait()
        strided_relay(chol_raw, chol_wide, chol, p * span, span)

    scale = field_scale / math.sqrt(nchol)
    cols = rows * orbitals
    tile = min(512, cols)
    deep = tile // orbitals

    def operators(m):
        @pl.loop(0, cols // tile)
        def _(n):
            at = pl.ds(pl.multiple_of(n * tile, tile), tile)
            out = jnp.dot(left[:m], chol[:, at], preferred_element_type=f32) * scale
            for i in range(deep):
                for h in range(halves):
                    low = i * orbitals + h * 128
                    op_wide[h, pl.ds(n * deep + i, m, stride=rows), :] = out[:, low : low + 128]

    def packed(w):
        first = pl.ds(pl.multiple_of(w * rows, rows), rows)
        return jnp.concatenate([op_wide[h, first, :] for h in range(halves)], axis=1).astype(bf16)

    def chip_operators(which):
        left[:slots] = all_fields[pair, which]
        operators(slots)

        def pack(s, carry):
            for c in range(cap):
                op_send[c, s, 0, which] = packed(c * blocks + s)
            return carry

        lax.fori_loop(0, blocks, pack, 0)

    def send_chip_operators(which):
        def to(s):
            send(
                op_send.at[:, s, 0, which],
                op_recv.at[:, me, 0, which],
                op_sent.at[cap],
                op_got.at[cap],
                s,
            )

        far_then_near(to, to)
        for c in range(cap):
            op_recv[c, me, 0, which] = op_send[c, me, 0, which]

    def other_operators(c, first, count):
        for k in range(count):
            chip = lax.rem(pair + first + k, pairs)
            for q in range(2):
                low = (k * 2 + q) * blocks
                at = pl.ds(pl.multiple_of(c * blocks, blocks), blocks)
                left[low : low + blocks] = all_fields[chip, q, at]
        operators(count * 2 * blocks)

        def pack(s, carry):
            for k in range(count):
                for q in range(2):
                    op_send[c, s, first + k, q] = packed((k * 2 + q) * blocks + s)
            return carry

        lax.fori_loop(0, blocks, pack, 0)

        def to(s):
            send(
                op_send.at[c, s, pl.ds(first, count)],
                op_recv.at[c, me, pl.ds(first, count)],
                op_sent.at[c],
                op_got.at[c],
                s,
            )

        far_then_near(to, to)
        for k in range(count):
            for q in range(2):
                op_recv[c, me, first + k, q] = op_send[c, me, first + k, q]

    partner = pair * 2 + 1 - core
    beside = (line * 2 + 1 - across) * 2 + core

    def line_at(j):
        return lax.rem(line + lines - j, lines)

    own, twin = all_fields.at[pair, core], all_fields.at[pair, 1 - core]
    pl.semaphore_wait(barrier, blocks - 1)
    send(own, own, field_send.at[0], field_core.at[0], partner)
    for j in range(1, lines):
        peer = (lax.rem(line + j, lines) * 2 + across) * 2 + core
        send(own, own, field_send.at[2], field_line.at[j], peer)
    send(own, own, field_send.at[1], field_row.at[0], beside)

    @pl.loop(0, 2)
    def _(t):
        @pl.when(t == 1)
        def _():
            for j in range(1, lines):
                held = all_fields.at[line_at(j) * 2 + across, core]
                wait(held, field_line.at[j])
                send(held, held, field_send.at[1], field_row.at[j], beside)
                send(held, held, field_send.at[0], field_core.at[1], partner)
            wait(twin, field_core.at[0])

        which = lax.rem(core + t, 2)
        chip_operators(which)
        send_chip_operators(which)

    for j in range(lines):
        held = all_fields.at[line_at(j) * 2 + 1 - across, core]
        wait(held, field_row.at[j])
        send(held, held, field_send.at[0], field_core.at[1], partner)
    wait(all_fields.at[pl.ds(0, pairs - 1), 0], field_core.at[1])

    split = pairs // 2

    @pl.loop(0, cap)
    def _(c):
        other_operators(c, 1, split)
        other_operators(c, 1 + split, pairs - 1 - split)

    rotated_load.wait()
    strided_relay(rotated_raw, rotated_wide, rotated, 0, nchol)
    walker_load.wait()

    def taylor(c):
        group = 4

        @pl.loop(0, blocks // group)
        def _(g):
            ops, terms, sums = [], [], []
            for u in range(group):
                r = g * group + u
                chip, q = lax.rem(r, pairs), r // pairs
                ops.append(
                    jnp.concatenate(
                        [
                            op_recv[c, o, lax.rem(chip + pairs - o // 2, pairs), q]
                            for o in range(blocks)
                        ],
                        axis=0,
                    )
                )
                entry = jnp.maximum(send_walker[(chip * 2 + q) * cap + c], 0)
                terms.append(walkers[entry])
                sums.append(terms[u].astype(f32))
            for degree in range(1, degrees + 1):
                for u in range(group):
                    product = lax.dot_general(
                        terms[u], ops[u], (((1,), (1,)), ((), ())), preferred_element_type=f32
                    )
                    terms[u] = (product * (1.0 / degree)).astype(bf16)
                    sums[u] = sums[u] + terms[u].astype(f32)
            for u in range(group):
                r = g * group + u
                nw_full[c, r] = sums[u].astype(bf16)
                at = pl.ds(pl.multiple_of(r * electrons, electrons), electrons)
                for h in range(halves):
                    totals[h, at, :] = sums[u][:, h * 128 : (h + 1) * 128]

        def turn(o, carry):
            for e in range(elec):
                for h in range(halves):
                    low = e * orbitals + h * 128
                    nw_send[c, o, :, low : low + 128] = totals[
                        h, pl.ds(o * elec + e, blocks, stride=electrons), :
                    ].astype(bf16)
            return carry

        lax.fori_loop(0, blocks, turn, 0)

        def to_owner(o):
            send(nw_send.at[c, o], nw_recv.at[c, me], nw_sent.at[c], nw_got.at[c], o)

        far_then_near(to_owner, to_owner)
        nw_recv[c, me] = nw_send[c, me]
        mine = pl.ds(pl.multiple_of(side * near, near), near)

        def to_far(d):
            send(
                nw_full.at[c, row_of(d), mine],
                branch.at[c, me, mine],
                br_sent.at[0],
                br_got.at[0],
                d,
            )

        def to_close(d):
            send(nw_full.at[c, row_of(d)], branch.at[c, me], br_sent.at[0], br_got.at[0], d)

        far_then_near(to_far, to_close)
        branch[c, me] = nw_full[c, row_of(me)]

    def bias(c):
        rows_in = nw_recv[c].reshape(blocks * blocks, elec * orbitals)
        step = min(256, nchol)

        @pl.loop(0, nchol // step)
        def _(n):
            at = pl.ds(pl.multiple_of(n * step, step), step)
            out = lax.dot_general(
                rows_in, rotated[at, :], (((1,), (1,)), ((), ())), preferred_element_type=f32
            ).reshape(blocks, 2, pairs, step)
            for q in range(2):
                mine = out[:, q].reshape(blocks * pairs, step)
                for h in range(step // 128):
                    part[c, q, n * (step // 128) + h] = mine[:, h * 128 : (h + 1) * 128]

        send(part.at[c, 1 - core], pair_recv.at[c], pair_sent.at[c], pair_got.at[c], partner)

    def reduced(c, chip, h):
        at = pl.ds(chip, blocks, stride=pairs)
        return part[c, core, h, at, :] + pair_recv[c, h, at, :]

    def reduce(c):
        wait(pair_recv.at[c], pair_got.at[c])

        def pick(z, carry):
            for h in range(nchol // 128):
                both = reduced(c, z * 2 + 1 - across, h)
                row_send[c, z, :, h * 128 : (h + 1) * 128] = both.astype(bf16)
            return carry

        lax.fori_loop(0, lines, pick, 0)
        send(row_send.at[c], row_recv.at[c], row_sent.at[c], row_got.at[c], beside)

    def spread(c):
        wait(row_recv.at[c], row_got.at[c])

        def pick(z, carry):
            for h in range(nchol // 128):
                low = h * 128
                both = reduced(c, z * 2 + across, h)
                both = both + row_recv[c, z, :, low : low + 128].astype(f32)
                fb_send[c, z, :, low : low + 128] = both.astype(bf16)
            return carry

        lax.fori_loop(0, lines, pick, 0)

        def step(k, carry):
            z = lax.rem(line + k, lines)
            send(
                fb_send.at[c, z],
                fb_recv.at[c, line],
                fb_sent.at[c],
                fb_got.at[c],
                (z * 2 + across) * 2 + core,
            )
            return carry

        lax.fori_loop(1, lines, step, 0)
        fb_recv[c, line] = fb_send[c, line]

    def finish(c):
        wait(fb_recv.at[c, pl.ds(0, lines - 1)], fb_got.at[c])
        fb_total[c] = lax.fori_loop(
            1,
            lines,
            lambda s, acc: acc + fb_recv[c, s].astype(f32),
            fb_recv[c, 0].astype(f32),
        )

    def forward():
        count = half * blocks
        for c in range(cap):
            block = nw_recv[c, pl.ds(away * half, half)].astype(f32)
            block = block.reshape(count, elec * orbitals)
            for h in range(elec * orbitals // 128):
                fw_wide[h, c * count : (c + 1) * count] = block[:, h * 128 : (h + 1) * 128]

        def gather(t, carry):
            at = pl.ds(row_of(side * half + t), cap * half, stride=blocks)
            for h in range(elec * orbitals // 128):
                fw_send[t, :, h * 128 : (h + 1) * 128] = fw_wide[h, at, :].astype(bf16)
            return carry

        lax.fori_loop(0, half, gather, 0)

        def step(k, carry):
            t = lax.rem(local + k, half)
            send(fw_send.at[t], fw_recv.at[local], fw_sent.at[0], fw_got.at[0], side * half + t)
            return carry

        lax.fori_loop(1, half, step, 0)
        fw_recv[local] = fw_send[local]

    def collect():
        wait(fw_recv.at[pl.ds(0, half - 1)], fw_got.at[0])

        def fold(o, carry):
            block = fw_recv[o].astype(f32)
            for e in range(elec):
                for h in range(halves):
                    low = e * orbitals + h * 128
                    fw_rows[h, pl.ds(o * elec + e, cap * half, stride=near), :] = block[
                        :, low : low + 128
                    ]
            return carry

        lax.fori_loop(0, half, fold, 0)
        wait(branch.at[:, pl.ds(0, half - 1 + half // 2)], br_got.at[0])

        def put(s, carry):
            for c in range(cap):
                at = pl.ds(pl.multiple_of((c * half + s) * near, near), near)
                value = jnp.concatenate([fw_rows[h, at, :] for h in range(halves)], axis=1)
                mine = pl.ds(pl.multiple_of(side * near, near), near)
                branch[c, away * half + s, mine] = value.astype(bf16)
            return carry

        lax.fori_loop(0, half, put, 0)

        def walker_out(p, carry):
            entry = slot_row[p]
            new_walkers[p] = branch[lax.rem(entry, cap), entry // cap]
            return carry

        lax.fori_loop(0, slots, walker_out, 0)

    wait(op_recv.at[:, pl.ds(0, blocks - 1), 0], op_got.at[cap])
    for c in range(cap):
        wait(op_recv.at[c, pl.ds(0, blocks - 1), pl.ds(1, pairs - 1)], op_got.at[c])
        taylor(c)
    for c in range(cap):
        wait(nw_recv.at[c, pl.ds(0, blocks - 1)], nw_got.at[c])
        bias(c)
        if c == cap - 1:
            forward()
        reduce(c)
        spread(c)
    collect()
    for c in range(cap):
        finish(c)

    def bias_out(p, carry):
        entry = slot_row[p]
        force_bias[pl.ds(p, 1), :] = fb_total[lax.rem(entry, cap), pl.ds(entry // cap, 1), :]
        return carry

    lax.fori_loop(0, slots, bias_out, 0)

    wait(all_fields.at[:, 0], field_send.at[0])
    wait(all_fields.at[pl.ds(0, lines), 0], field_send.at[1])
    wait(all_fields.at[pl.ds(0, lines - 1), 0], field_send.at[2])
    wait(op_recv.at[:, pl.ds(0, blocks - 1), 0], op_sent.at[cap])
    wait(branch.at[:, pl.ds(0, half - 1 + half // 2)], br_sent.at[0])
    wait(fw_send.at[pl.ds(0, half - 1)], fw_sent.at[0])
    for c in range(cap):
        wait(op_recv.at[c, pl.ds(0, blocks - 1), pl.ds(1, pairs - 1)], op_sent.at[c])
        wait(nw_send.at[c, pl.ds(0, blocks - 1)], nw_sent.at[c])
        wait(pair_recv.at[c], pair_sent.at[c])
        wait(row_send.at[c], row_sent.at[c])
        wait(fb_send.at[c, pl.ds(0, lines - 1)], fb_sent.at[c])


def parent_shards(blocks, walkers, fields, chol_vectors, rotated, send_walker, slot_row):
    slots, electrons, orbitals = walkers.shape
    nchol, rows, _ = chol_vectors.shape
    elec = rotated.shape[1]
    cap = send_walker.shape[-1]
    bf16, f32 = jnp.bfloat16, jnp.float32
    pairs, lines, half = blocks // 2, blocks // 4, blocks // 2
    halves, near = orbitals // 128, electrons // 2
    most = max(pairs // 2 * 2 * blocks, slots)
    wide = elec * orbitals
    vmem, smem, anywhere = (
        pl.BlockSpec(memory_space=m) for m in (pltpu.VMEM, pltpu.SMEM, pl.ANY)
    )
    dma = pltpu.SemaphoreType.DMA
    return pl.pallas_call(
        functools.partial(parent_kernel, (blocks, cap, rows, elec)),
        out_shape=(
            jax.ShapeDtypeStruct(walkers.shape, bf16),
            jax.ShapeDtypeStruct((slots, nchol), f32),
        ),
        in_specs=[smem, smem, vmem, anywhere, anywhere, anywhere],
        out_specs=(vmem, vmem),
        scratch_shapes=[
            pltpu.VMEM(walkers.shape, bf16),
            pltpu.VMEM(chol_vectors.shape, bf16),
            pltpu.VMEM((halves, rows * unfold_depth, 128), f32),
            pltpu.VMEM((nchol, rows * orbitals), bf16),
            pltpu.VMEM(rotated.shape, bf16),
            pltpu.VMEM((halves, elec * unfold_depth, 128), f32),
            pltpu.VMEM((nchol, wide), bf16),
            pltpu.VMEM((pairs, 2, slots, nchol), bf16),
            pltpu.VMEM((most, nchol), bf16),
            pltpu.VMEM((halves, most * rows, 128), f32),
            pltpu.VMEM((cap, blocks, pairs, 2, rows, orbitals), bf16),
            pltpu.VMEM((cap, blocks, pairs, 2, rows, orbitals), bf16),
            pltpu.VMEM((halves, blocks * electrons, 128), f32),
            pltpu.VMEM((cap, blocks, electrons, orbitals), bf16),
            pltpu.VMEM((cap, blocks, blocks, wide), bf16),
            pltpu.VMEM((cap, blocks, blocks, wide), bf16),
            pltpu.VMEM((cap, 2, nchol // 128, blocks * pairs, 128), f32),
            pltpu.VMEM((cap, nchol // 128, blocks * pairs, 128), f32),
            pltpu.VMEM((cap, lines, blocks, nchol), bf16),
            pltpu.VMEM((cap, lines, blocks, nchol), bf16),
            pltpu.VMEM((cap, lines, blocks, nchol), bf16),
            pltpu.VMEM((cap, lines, blocks, nchol), bf16),
            pltpu.VMEM((cap, blocks, nchol), f32),
            pltpu.VMEM((wide // 128, cap * half * blocks, 128), f32),
            pltpu.VMEM((half, cap * half, wide), bf16),
            pltpu.VMEM((half, cap * half, wide), bf16),
            pltpu.VMEM((halves, cap * half * near, 128), f32),
            pltpu.VMEM((cap, blocks, electrons, orbitals), bf16),
            dma((6,)),
            dma((3,)),
            dma((2,)),
            dma((lines,)),
            dma((lines,)),
            dma((cap + 1,)),
            dma((cap + 1,)),
            dma((cap,)),
            dma((cap,)),
            dma((1,)),
            dma((1,)),
            dma((cap,)),
            dma((cap,)),
            dma((cap,)),
            dma((cap,)),
            dma((cap,)),
            dma((cap,)),
            dma((1,)),
            dma((1,)),
        ],
        compiler_params=pltpu.CompilerParams(
            collective_id=1, has_side_effects=True, vmem_limit_bytes=60 * 1024 * 1024
        ),
    )(send_walker.reshape(-1), slot_row, fields, walkers, chol_vectors, rotated)


def plan(blocks, walkers, fields, chol_vectors, rotated, send_walker, slot_row):
    every_entry = blocks * send_walker.shape[-1] == walkers.shape[0]
    step = parent_shards if every_entry and blocks % 8 == 0 else shards
    return step(blocks, walkers, fields, chol_vectors, rotated, send_walker, slot_row)


def solution(mesh):
    in_specs = (
        P(("grp", "chol"), None, None),
        P(("grp", "chol"), None),
        P(None, "chol", None),
        P(None, "chol", None),
        P(("grp", "chol"), None, None),
        P(("grp", "chol")),
    )
    out_specs = (P(("grp", "chol"), None, None), P(("grp", "chol"), None))
    return jax.shard_map(
        functools.partial(plan, mesh.shape["chol"]),
        mesh=mesh,
        in_specs=in_specs,
        out_specs=out_specs,
        check_vma=False,
    )
```

```python
import functools
import math

import jax
import jax.numpy as jnp
from jax import lax
from jax.experimental import pallas as pl
from jax.experimental.pallas import tpu as pltpu
from jax.sharding import PartitionSpec as P

field_scale = 1.5
chunk_slots = 16
degrees = 5
unfold_depth = 64
MESH = pl.DeviceIdType.MESH


def stride_of(blocks):
    return next(h for h in (7, 5, 3, 1) if math.gcd(h, blocks) == 1)


def unfold(source, scratch, target):
    depth, rows, orbitals = source.shape
    step = scratch.shape[1] // rows

    def body(b, carry):
        first = pl.multiple_of(b * step, step)
        block = source[pl.ds(first, step)].astype(jnp.float32).reshape(step * rows, orbitals)
        for h in range(orbitals // 128):
            scratch[h] = block[:, h * 128 : (h + 1) * 128]
        for r in range(rows):
            for h in range(orbitals // 128):
                low = r * orbitals + h * 128
                target[pl.ds(first, step), low : low + 128] = scratch[
                    h, pl.ds(r, step, stride=rows), :
                ].astype(jnp.bfloat16)
        return carry

    lax.fori_loop(0, depth // step, body, 0)


def exchange(me, blocks, send, recv, chunk, send_sem, recv_sem, place=lambda d: d, land=lambda d: d):
    hop = stride_of(blocks)

    def step(k, carry):
        peer = lax.rem(me + k * hop, blocks)
        pltpu.make_async_remote_copy(
            src_ref=send.at[chunk, place(peer)],
            dst_ref=recv.at[chunk, land(me)],
            send_sem=send_sem.at[chunk],
            recv_sem=recv_sem.at[chunk],
            device_id={"chol": peer},
            device_id_type=MESH,
        ).start()
        return carry

    lax.fori_loop(1, blocks, step, 0)
    recv[chunk, land(me)] = send[chunk, place(me)]


def arrived(blocks, recv, chunk, sem):
    whole = recv.at[chunk, pl.ds(0, blocks - 1)]
    pltpu.make_async_copy(whole, whole, sem.at[chunk]).wait()


def kernel(
    dims,
    send_walker,
    slot_row,
    walkers,
    fields,
    chol_hbm,
    rotated_raw,
    new_walkers,
    force_bias,
    chol_raw,
    chol_wide,
    chol,
    rotated_wide,
    rotated,
    all_fields,
    br_send,
    br_recv,
    op_send,
    op_recv,
    op_rows,
    totals,
    nw_send,
    nw_recv,
    pair_send,
    pair_recv,
    pair_own,
    fb_send,
    fb_recv,
    send_sems,
    recv_sems,
    field_sems,
    load_sem,
    op_sems,
):
    blocks, chunks, width, cap, rows, elec = dims
    slots, electrons, orbitals = walkers.shape
    nchol = rotated.shape[0]
    halves = orbitals // 128
    me = lax.axis_index("chol")
    pairs = blocks // 2
    core, pair = lax.rem(me, 2), me // 2
    groups = math.gcd(4, blocks)
    share_of = blocks // groups
    hop = stride_of(blocks)
    load = pltpu.make_async_copy(chol_hbm, chol_raw, load_sem)
    load.start()

    barrier = pltpu.get_barrier_semaphore()

    def greet(k, carry):
        pl.semaphore_signal(
            barrier, inc=1, device_id={"chol": lax.rem(me + k, blocks)}, device_id_type=MESH
        )
        return carry

    lax.fori_loop(1, blocks, greet, 0)

    def pick(d, carry):
        for c in range(cap):
            br_send[0, d, c] = walkers[jnp.maximum(send_walker[d * cap + c], 0)]
        return carry

    lax.fori_loop(0, blocks, pick, 0)
    pl.semaphore_wait(barrier, blocks - 1)

    def share(k, carry):
        pltpu.make_async_remote_copy(
            src_ref=fields,
            dst_ref=all_fields.at[core, pair],
            send_sem=field_sems.at[0],
            recv_sem=field_sems.at[1],
            device_id={"chol": lax.rem(pair + k, pairs) * 2 + core},
            device_id_type=MESH,
        ).start()
        return carry

    lax.fori_loop(1, pairs, share, 0)
    all_fields[core, pair] = fields[...]
    load.wait()
    unfold(chol_raw, chol_wide, chol)
    same_core = all_fields.at[core, pl.ds(0, pairs - 1)]
    pltpu.make_async_copy(same_core, same_core, field_sems.at[1]).wait()
    across = pltpu.make_async_remote_copy(
        src_ref=all_fields.at[core],
        dst_ref=all_fields.at[core],
        send_sem=field_sems.at[2],
        recv_sem=field_sems.at[3],
        device_id={"chol": pair * 2 + 1 - core},
        device_id_type=MESH,
    )
    across.start()
    exchange(me, blocks, br_send, br_recv, 0, send_sems.at[0], recv_sems.at[0])

    across.wait_recv()
    scale = field_scale / math.sqrt(nchol)
    cols = rows * orbitals
    tile = min(512, cols)

    @pl.loop(0, cols // tile)
    def _(n):
        at = pl.ds(pl.multiple_of(n * tile, tile), tile)
        left = all_fields[...].reshape(blocks * slots, nchol)
        part = jnp.dot(left, chol[:, at], preferred_element_type=jnp.float32) * scale
        part = part.astype(jnp.bfloat16).reshape(blocks, chunks, width, tile)
        for q in range(chunks):
            op_send[q, :, :, at] = part[:, q]

    def send_operators(q):
        for group in range(groups):
            def step(k, carry):
                peer = lax.rem(me + k * hop, blocks)
                pltpu.make_async_remote_copy(
                    src_ref=op_send.at[q, place(peer)],
                    dst_ref=op_recv.at[q, me],
                    send_sem=send_sems.at[1, q],
                    recv_sem=op_sems.at[q, group],
                    device_id={"chol": peer},
                    device_id_type=MESH,
                ).start()
                return carry

            lax.fori_loop(max(1, group * share_of), (group + 1) * share_of, step, 0)
        op_recv[q, me] = op_send[q, place(me)]

    def place(d):
        return lax.rem(d, 2) * pairs + d // 2

    def taylor(q):
        def spread(k, carry):
            s = lax.rem(me + (blocks - k) * hop, blocks)
            block = op_recv[q, s].astype(jnp.float32)
            for r in range(rows):
                for h in range(halves):
                    low = r * orbitals + h * 128
                    op_rows[h, pl.ds(s * rows + r, width, stride=orbitals), :] = block[
                        :, low : low + 128
                    ]
            return carry

        for group in range(groups):
            count = share_of - 1 if group == 0 else share_of
            whole = op_recv.at[q, pl.ds(0, count)]
            pltpu.make_async_copy(whole, whole, op_sems.at[q, group]).wait()
            lax.fori_loop(group * share_of, (group + 1) * share_of, spread, 0)
        group = 4

        @pl.loop(0, width // group)
        def _(g):
            ops, terms, sums = [], [], []
            for u in range(group):
                w = g * group + u
                first = pl.ds(pl.multiple_of(w * orbitals, orbitals), orbitals)
                ops.append(
                    jnp.concatenate([op_rows[h, first, :] for h in range(halves)], axis=1).astype(
                        jnp.bfloat16
                    )
                )
                row = slot_row[q * width + w]
                terms.append(br_recv[0, row // cap, row % cap])
                sums.append(terms[u].astype(jnp.float32))
            for degree in range(1, degrees + 1):
                for u in range(group):
                    product = lax.dot_general(
                        terms[u],
                        ops[u],
                        (((1,), (1,)), ((), ())),
                        preferred_element_type=jnp.float32,
                    )
                    terms[u] = (product * (1.0 / degree)).astype(jnp.bfloat16)
                    sums[u] = sums[u] + terms[u].astype(jnp.float32)
            for u in range(group):
                w = g * group + u
                new_walkers[q * width + w] = sums[u].astype(jnp.bfloat16)
                place = pl.ds(pl.multiple_of(w * electrons, electrons), electrons)
                for h in range(halves):
                    totals[h, place, :] = sums[u][:, h * 128 : (h + 1) * 128]

        def turn(d, carry):
            for e in range(elec):
                for h in range(halves):
                    low = e * orbitals + h * 128
                    nw_send[q, d, :, low : low + 128] = totals[
                        h, pl.ds(d * elec + e, width, stride=electrons), :
                    ].astype(jnp.bfloat16)
            return carry

        lax.fori_loop(0, blocks, turn, 0)
        exchange(me, blocks, nw_send, nw_recv, q, send_sems.at[2], recv_sems.at[2], land=place)

    def partial(q, half, target):
        left = nw_recv[q, pl.ds(half * pairs, pairs)].reshape(pairs * width, elec * orbitals)
        step = min(256, nchol)

        @pl.loop(0, nchol // step)
        def _(n):
            at = pl.ds(pl.multiple_of(n * step, step), step)
            target[:, at] = lax.dot_general(
                left, rotated[at, :], (((1,), (1,)), ((), ())), preferred_element_type=jnp.float32
            )

    def bias(q):
        partial(q, 1 - core, pair_send.at[q])
        across = pltpu.make_async_remote_copy(
            src_ref=pair_send.at[q],
            dst_ref=pair_recv.at[q],
            send_sem=send_sems.at[4, q],
            recv_sem=recv_sems.at[4, q],
            device_id={"chol": pair * 2 + 1 - core},
            device_id_type=MESH,
        )
        across.start()
        partial(q, core, pair_own)
        across.wait_recv()
        both = (pair_own[...] + pair_recv[q]).astype(jnp.bfloat16)
        fb_send[q] = both.reshape(pairs, width, nchol)

        def step(k, carry):
            peer = lax.rem(pair + k, pairs)
            pltpu.make_async_remote_copy(
                src_ref=fb_send.at[q, peer],
                dst_ref=fb_recv.at[q, pair],
                send_sem=send_sems.at[3, q],
                recv_sem=recv_sems.at[3, q],
                device_id={"chol": peer * 2 + core},
                device_id_type=MESH,
            ).start()
            return carry

        lax.fori_loop(1, pairs, step, 0)
        fb_recv[q, pair] = fb_send[q, pair]

    def finish(q):
        force_bias[q * width : (q + 1) * width, :] = lax.fori_loop(
            1,
            pairs,
            lambda s, acc: acc + fb_recv[q, s].astype(jnp.float32),
            fb_recv[q, 0].astype(jnp.float32),
        )

    for q in range(min(2, chunks)):
        send_operators(q)
    unfold(rotated_raw, rotated_wide, rotated)
    arrived(blocks, br_recv, 0, recv_sems.at[0])
    for q in range(chunks + 2):
        if q < chunks:
            if q + 2 < chunks:
                send_operators(q + 2)
            taylor(q)
        if 1 <= q <= chunks:
            arrived(blocks, nw_recv, q - 1, recv_sems.at[2])
            bias(q - 1)
        if q >= 2:
            arrived(pairs, fb_recv, q - 2, recv_sems.at[3])
            finish(q - 2)
    arrived(blocks, br_send, 0, send_sems.at[0])
    across.wait_send()
    pltpu.make_async_copy(same_core, same_core, field_sems.at[0]).wait()
    for q in range(chunks):
        arrived(blocks, op_send, q, send_sems.at[1])
        arrived(blocks, nw_send, q, send_sems.at[2])
        arrived(pairs, fb_send, q, send_sems.at[3])
        pltpu.make_async_copy(pair_send.at[q], pair_send.at[q], send_sems.at[4, q]).wait()


def shards(blocks, walkers, fields, chol_vectors, rotated, send_walker, slot_row):
    slots, electrons, orbitals = walkers.shape
    nchol, rows, _ = chol_vectors.shape
    elec = rotated.shape[1]
    cap = send_walker.shape[-1]
    width = min(chunk_slots, slots)
    chunks = slots // width
    dims = (blocks, chunks, width, cap, rows, elec)
    bf16, f32 = jnp.bfloat16, jnp.float32
    vmem, smem = (pl.BlockSpec(memory_space=m) for m in (pltpu.VMEM, pltpu.SMEM))
    return pl.pallas_call(
        functools.partial(kernel, dims),
        out_shape=(
            jax.ShapeDtypeStruct(walkers.shape, bf16),
            jax.ShapeDtypeStruct((slots, nchol), f32),
        ),
        in_specs=[smem, smem, vmem, vmem, pl.BlockSpec(memory_space=pl.ANY), vmem],
        out_specs=(vmem, vmem),
        scratch_shapes=[
            pltpu.VMEM(chol_vectors.shape, bf16),
            pltpu.VMEM((orbitals // 128, rows * unfold_depth, 128), f32),
            pltpu.VMEM((nchol, rows * orbitals), bf16),
            pltpu.VMEM((orbitals // 128, elec * unfold_depth, 128), f32),
            pltpu.VMEM((nchol, elec * orbitals), bf16),
            pltpu.VMEM((2, blocks // 2, slots, nchol), bf16),
            pltpu.VMEM((1, blocks, cap, electrons, orbitals), bf16),
            pltpu.VMEM((1, blocks, cap, electrons, orbitals), bf16),
            pltpu.VMEM((chunks, blocks, width, rows * orbitals), bf16),
            pltpu.VMEM((chunks, blocks, width, rows * orbitals), bf16),
            pltpu.VMEM((orbitals // 128, width * orbitals, 128), f32),
            pltpu.VMEM((orbitals // 128, width * electrons, 128), f32),
            pltpu.VMEM((chunks, blocks, width, elec * orbitals), bf16),
            pltpu.VMEM((chunks, blocks, width, elec * orbitals), bf16),
            pltpu.VMEM((chunks, blocks // 2 * width, nchol), f32),
            pltpu.VMEM((chunks, blocks // 2 * width, nchol), f32),
            pltpu.VMEM((blocks // 2 * width, nchol), f32),
            pltpu.VMEM((chunks, blocks // 2, width, nchol), bf16),
            pltpu.VMEM((chunks, blocks // 2, width, nchol), bf16),
            pltpu.SemaphoreType.DMA((5, chunks)),
            pltpu.SemaphoreType.DMA((5, chunks)),
            pltpu.SemaphoreType.DMA((4,)),
            pltpu.SemaphoreType.DMA,
            pltpu.SemaphoreType.DMA((chunks, math.gcd(4, blocks))),
        ],
        compiler_params=pltpu.CompilerParams(
            collective_id=0, has_side_effects=True, vmem_limit_bytes=60 * 1024 * 1024
        ),
    )(
        send_walker.reshape(-1),
        slot_row,
        walkers,
        fields,
        chol_vectors,
        rotated,
    )


def turned(source, target, start, count):
    rows, orbitals = source.shape[1:]
    step = 16

    def body(b, carry):
        first = pl.multiple_of(start + b * step, step)
        block = jnp.swapaxes(source[pl.ds(first, step)], 0, 1)
        for r in range(rows):
            target[pl.ds(first, step), r * orbitals : (r + 1) * orbitals] = block[r]
        return carry

    lax.fori_loop(0, count // step, body, 0)


def parent_kernel(
    dims,
    send_walker,
    slot_row,
    fields,
    walkers_hbm,
    chol_hbm,
    rotated_hbm,
    new_walkers,
    force_bias,
    walkers,
    chol_raw,
    chol,
    rotated_raw,
    rotated,
    all_fields,
    left,
    op_rows,
    op_send,
    op_recv,
    nw_full,
    nw_send,
    nw_recv,
    part,
    pair_recv,
    row_send,
    row_recv,
    fb_send,
    fb_recv,
    fb_total,
    fw_wide,
    fw_send,
    fw_recv,
    fw_rows,
    branch,
    load_sems,
    field_send,
    field_core,
    field_line,
    field_row,
    op_sent,
    op_got,
    nw_sent,
    nw_got,
    br_sent,
    br_got,
    pair_sent,
    pair_got,
    row_sent,
    row_got,
    fb_sent,
    fb_got,
    fw_sent,
    fw_got,
):
    blocks, cap, rows, elec = dims
    slots, nchol = fields.shape
    electrons, orbitals = walkers.shape[1:]
    halves = orbitals // 128
    me = lax.axis_index("chol")
    pairs, lines, half = blocks // 2, blocks // 4, blocks // 2
    hop = stride_of(blocks)
    core, pair = lax.rem(me, 2), me // 2
    line, across = pair // 2, lax.rem(pair, 2)
    side, local = me // half, lax.rem(me, half)
    away = 1 - side
    near = electrons // 2
    bf16, f32 = jnp.bfloat16, jnp.float32

    def wait(ref, sem):
        pltpu.make_async_copy(ref, ref, sem).wait()

    def send(src, dst, sent, got, peer):
        pltpu.make_async_remote_copy(
            src_ref=src,
            dst_ref=dst,
            send_sem=sent,
            recv_sem=got,
            device_id={"chol": peer},
            device_id_type=MESH,
        ).start()

    def everyone(to):
        def step(t, carry):
            to(lax.rem(me + t * hop, blocks))
            return carry

        lax.fori_loop(1, blocks, step, 0)

    def far_then_near(far, close):
        def first(t, carry):
            far(away * half + lax.rem(local + t, half))
            return carry

        def second(t, carry):
            close(side * half + lax.rem(local + t, half))
            return carry

        lax.fori_loop(0, half, first, 0)
        lax.fori_loop(1, half, second, 0)

    def row_of(d):
        return lax.rem(d, 2) * pairs + d // 2

    pieces = 4
    span = nchol // pieces
    chol_loads = [
        pltpu.make_async_copy(
            chol_hbm.at[pl.ds(p * span, span)], chol_raw.at[pl.ds(p * span, span)], load_sems.at[p]
        )
        for p in range(pieces)
    ]
    for load in chol_loads:
        load.start()
    walker_load = pltpu.make_async_copy(walkers_hbm, walkers, load_sems.at[pieces])
    rotated_load = pltpu.make_async_copy(rotated_hbm, rotated_raw, load_sems.at[pieces + 1])
    walker_load.start()
    rotated_load.start()

    barrier = pltpu.get_barrier_semaphore()

    def greet(k, carry):
        pl.semaphore_signal(
            barrier, inc=1, device_id={"chol": lax.rem(me + k, blocks)}, device_id_type=MESH
        )
        return carry

    lax.fori_loop(1, blocks, greet, 0)

    order = lax.broadcasted_iota(jnp.int32, (slots, slots), 0)
    place = lax.broadcasted_iota(jnp.int32, (slots, slots), 1)
    chosen = jnp.zeros((slots, slots), f32)
    for p in range(slots):
        entry = slot_row[p]
        target = lax.rem(entry, cap) * blocks + entry // cap
        chosen = jnp.where((place == p) & (order == target), 1.0, chosen)
    all_fields[pair, core] = jnp.dot(
        chosen.astype(bf16), fields[...], preferred_element_type=f32
    ).astype(bf16)

    for p in range(pieces):
        chol_loads[p].wait()
        turned(chol_raw, chol, p * span, span)

    scale = field_scale / math.sqrt(nchol)
    cols = rows * orbitals
    tile = min(1024, cols)
    deep = tile // orbitals

    def operators(m):
        @pl.loop(0, cols // tile)
        def _(n):
            at = pl.ds(pl.multiple_of(n * tile, tile), tile)
            out = jnp.dot(left[:m], chol[:, at], preferred_element_type=f32) * scale
            for i in range(deep):
                op_rows[n * deep + i, :m] = out[:, i * orbitals : (i + 1) * orbitals].astype(bf16)

    def packed(b):
        return jnp.swapaxes(op_rows[:, b * blocks : (b + 1) * blocks], 0, 1)

    def chip_operators(which):
        left[:slots] = all_fields[pair, which]
        operators(slots)
        for c in range(cap):
            op_send[c, :, 0, which] = packed(c)

    def send_chip_operators(which):
        def to(s):
            send(
                op_send.at[:, s, 0, which],
                op_recv.at[:, me, 0, which],
                op_sent.at[cap],
                op_got.at[cap],
                s,
            )

        everyone(to)
        for c in range(cap):
            op_recv[c, me, 0, which] = op_send[c, me, 0, which]

    def other_operators(c, first, count):
        for k in range(count):
            chip = lax.rem(pair + first + k, pairs)
            for q in range(2):
                low = (k * 2 + q) * blocks
                at = pl.ds(pl.multiple_of(c * blocks, blocks), blocks)
                left[low : low + blocks] = all_fields[chip, q, at]
        operators(count * 2 * blocks)

        for k in range(count):
            for q in range(2):
                op_send[c, :, first + k, q] = packed(k * 2 + q)

        def to(s):
            send(
                op_send.at[c, s, pl.ds(first, count)],
                op_recv.at[c, me, pl.ds(first, count)],
                op_sent.at[c],
                op_got.at[c],
                s,
            )

        everyone(to)
        for k in range(count):
            for q in range(2):
                op_recv[c, me, first + k, q] = op_send[c, me, first + k, q]

    partner = pair * 2 + 1 - core
    beside = (line * 2 + 1 - across) * 2 + core

    def line_at(j):
        return lax.rem(line + lines - j, lines)

    own, twin = all_fields.at[pair, core], all_fields.at[pair, 1 - core]
    pl.semaphore_wait(barrier, blocks - 1)
    send(own, own, field_send.at[0], field_core.at[0], partner)
    for j in range(1, lines):
        peer = (lax.rem(line + j, lines) * 2 + across) * 2 + core
        send(own, own, field_send.at[2], field_line.at[j], peer)
    send(own, own, field_send.at[1], field_row.at[0], beside)

    @pl.loop(0, 2)
    def _(t):
        @pl.when(t == 1)
        def _():
            for j in range(1, lines):
                held = all_fields.at[line_at(j) * 2 + across, core]
                wait(held, field_line.at[j])
                send(held, held, field_send.at[1], field_row.at[j], beside)
                send(held, held, field_send.at[0], field_core.at[1], partner)
            wait(twin, field_core.at[0])

        which = lax.rem(core + t, 2)
        chip_operators(which)
        send_chip_operators(which)

    for j in range(lines):
        held = all_fields.at[line_at(j) * 2 + 1 - across, core]
        wait(held, field_row.at[j])
        send(held, held, field_send.at[0], field_core.at[1], partner)
    wait(all_fields.at[pl.ds(0, pairs - 1), 0], field_core.at[1])

    split = pairs // 2

    @pl.loop(0, cap)
    def _(c):
        other_operators(c, 1, split)
        other_operators(c, 1 + split, pairs - 1 - split)

    rotated_load.wait()
    turned(rotated_raw, rotated, 0, nchol)
    walker_load.wait()

    def taylor(c):
        group = 4

        @pl.loop(0, blocks // group)
        def _(g):
            ops, terms, sums = [], [], []
            for u in range(group):
                r = g * group + u
                chip, q = lax.rem(r, pairs), r // pairs
                ops.append(
                    jnp.concatenate(
                        [
                            op_recv[c, o, lax.rem(chip + pairs - o // 2, pairs), q]
                            for o in range(blocks)
                        ],
                        axis=0,
                    )
                )
                entry = jnp.maximum(send_walker[(chip * 2 + q) * cap + c], 0)
                terms.append(walkers[entry])
                sums.append(terms[u].astype(f32))
            for degree in range(1, degrees + 1):
                for u in range(group):
                    product = lax.dot_general(
                        terms[u], ops[u], (((1,), (1,)), ((), ())), preferred_element_type=f32
                    )
                    terms[u] = (product * (1.0 / degree)).astype(bf16)
                    sums[u] = sums[u] + terms[u].astype(f32)
            for u in range(group):
                r = g * group + u
                nw_full[c, r] = sums[u].astype(bf16)

        for o in range(0, blocks, 16 // elec):
            block = jnp.swapaxes(nw_full[c, :, o * elec : o * elec + 16], 0, 1)
            for e in range(16):
                low = e % elec * orbitals
                nw_send[c, o + e // elec, :, low : low + orbitals] = block[e]

        def to_owner(o):
            send(nw_send.at[c, o], nw_recv.at[c, me], nw_sent.at[c], nw_got.at[c], o)

        everyone(to_owner)
        nw_recv[c, me] = nw_send[c, me]
        mine = pl.ds(pl.multiple_of(side * near, near), near)

        def to_far(d):
            send(
                nw_full.at[c, row_of(d), mine],
                branch.at[c, me, mine],
                br_sent.at[0],
                br_got.at[0],
                d,
            )

        def to_close(d):
            send(nw_full.at[c, row_of(d)], branch.at[c, me], br_sent.at[0], br_got.at[0], d)

        far_then_near(to_far, to_close)
        branch[c, me] = nw_full[c, row_of(me)]

    def bias(c):
        rows_in = nw_recv[c].reshape(blocks * blocks, elec * orbitals)
        step = min(256, nchol)

        @pl.loop(0, nchol // step)
        def _(n):
            at = pl.ds(pl.multiple_of(n * step, step), step)
            out = lax.dot_general(
                rows_in, rotated[at, :], (((1,), (1,)), ((), ())), preferred_element_type=f32
            ).reshape(blocks, 2, pairs, step)
            for q in range(2):
                mine = out[:, q].reshape(blocks * pairs, step)
                for h in range(step // 128):
                    part[c, q, n * (step // 128) + h] = mine[:, h * 128 : (h + 1) * 128]

        send(part.at[c, 1 - core], pair_recv.at[c], pair_sent.at[c], pair_got.at[c], partner)

    def reduced(c, chip, h):
        at = pl.ds(chip, blocks, stride=pairs)
        return part[c, core, h, at, :] + pair_recv[c, h, at, :]

    def reduce(c):
        wait(pair_recv.at[c], pair_got.at[c])

        def pick(z, carry):
            for h in range(nchol // 128):
                both = reduced(c, z * 2 + 1 - across, h)
                row_send[c, z, :, h * 128 : (h + 1) * 128] = both.astype(bf16)
            return carry

        lax.fori_loop(0, lines, pick, 0)
        send(row_send.at[c], row_recv.at[c], row_sent.at[c], row_got.at[c], beside)

    def spread(c):
        wait(row_recv.at[c], row_got.at[c])

        def pick(z, carry):
            for h in range(nchol // 128):
                low = h * 128
                both = reduced(c, z * 2 + across, h)
                both = both + row_recv[c, z, :, low : low + 128].astype(f32)
                fb_send[c, z, :, low : low + 128] = both.astype(bf16)
            return carry

        lax.fori_loop(0, lines, pick, 0)

        def step(k, carry):
            z = lax.rem(line + k, lines)
            send(
                fb_send.at[c, z],
                fb_recv.at[c, line],
                fb_sent.at[c],
                fb_got.at[c],
                (z * 2 + across) * 2 + core,
            )
            return carry

        lax.fori_loop(1, lines, step, 0)
        fb_recv[c, line] = fb_send[c, line]

    def finish(c):
        wait(fb_recv.at[c, pl.ds(0, lines - 1)], fb_got.at[c])
        fb_total[c] = lax.fori_loop(
            1,
            lines,
            lambda s, acc: acc + fb_recv[c, s].astype(f32),
            fb_recv[c, 0].astype(f32),
        )

    def forward():
        count = half * blocks
        for c in range(cap):
            block = nw_recv[c, pl.ds(away * half, half)].astype(f32)
            block = block.reshape(count, elec * orbitals)
            for h in range(elec * orbitals // 128):
                fw_wide[h, c * count : (c + 1) * count] = block[:, h * 128 : (h + 1) * 128]

        def gather(t, carry):
            at = pl.ds(row_of(side * half + t), cap * half, stride=blocks)
            for h in range(elec * orbitals // 128):
                fw_send[t, :, h * 128 : (h + 1) * 128] = fw_wide[h, at, :].astype(bf16)
            return carry

        lax.fori_loop(0, half, gather, 0)

        def step(k, carry):
            t = lax.rem(local + k, half)
            send(fw_send.at[t], fw_recv.at[local], fw_sent.at[0], fw_got.at[0], side * half + t)
            return carry

        lax.fori_loop(1, half, step, 0)
        fw_recv[local] = fw_send[local]

    def collect():
        wait(fw_recv.at[pl.ds(0, half - 1)], fw_got.at[0])

        def fold(o, carry):
            block = fw_recv[o].astype(f32)
            for e in range(elec):
                for h in range(halves):
                    low = e * orbitals + h * 128
                    fw_rows[h, pl.ds(o * elec + e, cap * half, stride=near), :] = block[
                        :, low : low + 128
                    ]
            return carry

        lax.fori_loop(0, half, fold, 0)
        wait(branch.at[:, pl.ds(0, half - 1 + half // 2)], br_got.at[0])

        def put(s, carry):
            for c in range(cap):
                at = pl.ds(pl.multiple_of((c * half + s) * near, near), near)
                value = jnp.concatenate([fw_rows[h, at, :] for h in range(halves)], axis=1)
                mine = pl.ds(pl.multiple_of(side * near, near), near)
                branch[c, away * half + s, mine] = value.astype(bf16)
            return carry

        lax.fori_loop(0, half, put, 0)

        def walker_out(p, carry):
            entry = slot_row[p]
            new_walkers[p] = branch[lax.rem(entry, cap), entry // cap]
            return carry

        lax.fori_loop(0, slots, walker_out, 0)

    wait(op_recv.at[:, pl.ds(0, blocks - 1), 0], op_got.at[cap])
    for c in range(cap):
        wait(op_recv.at[c, pl.ds(0, blocks - 1), pl.ds(1, pairs - 1)], op_got.at[c])
        taylor(c)
    for c in range(cap):
        wait(nw_recv.at[c, pl.ds(0, blocks - 1)], nw_got.at[c])
        bias(c)
        if c == cap - 1:
            forward()
        reduce(c)
        spread(c)
    collect()
    for c in range(cap):
        finish(c)

    def bias_out(p, carry):
        entry = slot_row[p]
        force_bias[pl.ds(p, 1), :] = fb_total[lax.rem(entry, cap), pl.ds(entry // cap, 1), :]
        return carry

    lax.fori_loop(0, slots, bias_out, 0)

    wait(all_fields.at[:, 0], field_send.at[0])
    wait(all_fields.at[pl.ds(0, lines), 0], field_send.at[1])
    wait(all_fields.at[pl.ds(0, lines - 1), 0], field_send.at[2])
    wait(op_recv.at[:, pl.ds(0, blocks - 1), 0], op_sent.at[cap])
    wait(branch.at[:, pl.ds(0, half - 1 + half // 2)], br_sent.at[0])
    wait(fw_send.at[pl.ds(0, half - 1)], fw_sent.at[0])
    for c in range(cap):
        wait(op_recv.at[c, pl.ds(0, blocks - 1), pl.ds(1, pairs - 1)], op_sent.at[c])
        wait(nw_send.at[c, pl.ds(0, blocks - 1)], nw_sent.at[c])
        wait(pair_recv.at[c], pair_sent.at[c])
        wait(row_send.at[c], row_sent.at[c])
        wait(fb_send.at[c, pl.ds(0, lines - 1)], fb_sent.at[c])


def parent_shards(blocks, walkers, fields, chol_vectors, rotated, send_walker, slot_row):
    slots, electrons, orbitals = walkers.shape
    nchol, rows, _ = chol_vectors.shape
    elec = rotated.shape[1]
    cap = send_walker.shape[-1]
    bf16, f32 = jnp.bfloat16, jnp.float32
    pairs, lines, half = blocks // 2, blocks // 4, blocks // 2
    halves, near = orbitals // 128, electrons // 2
    most = max(pairs // 2 * 2 * blocks, slots)
    wide = elec * orbitals
    vmem, smem, anywhere = (
        pl.BlockSpec(memory_space=m) for m in (pltpu.VMEM, pltpu.SMEM, pl.ANY)
    )
    dma = pltpu.SemaphoreType.DMA
    return pl.pallas_call(
        functools.partial(parent_kernel, (blocks, cap, rows, elec)),
        out_shape=(
            jax.ShapeDtypeStruct(walkers.shape, bf16),
            jax.ShapeDtypeStruct((slots, nchol), f32),
        ),
        in_specs=[smem, smem, vmem, anywhere, anywhere, anywhere],
        out_specs=(vmem, vmem),
        scratch_shapes=[
            pltpu.VMEM(walkers.shape, bf16),
            pltpu.VMEM(chol_vectors.shape, bf16),
            pltpu.VMEM((nchol, rows * orbitals), bf16),
            pltpu.VMEM(rotated.shape, bf16),
            pltpu.VMEM((nchol, wide), bf16),
            pltpu.VMEM((pairs, 2, slots, nchol), bf16),
            pltpu.VMEM((most, nchol), bf16),
            pltpu.VMEM((rows, most, orbitals), bf16),
            pltpu.VMEM((cap, blocks, pairs, 2, rows, orbitals), bf16),
            pltpu.VMEM((cap, blocks, pairs, 2, rows, orbitals), bf16),
            pltpu.VMEM((cap, blocks, electrons, orbitals), bf16),
            pltpu.VMEM((cap, blocks, blocks, wide), bf16),
            pltpu.VMEM((cap, blocks, blocks, wide), bf16),
            pltpu.VMEM((cap, 2, nchol // 128, blocks * pairs, 128), f32),
            pltpu.VMEM((cap, nchol // 128, blocks * pairs, 128), f32),
            pltpu.VMEM((cap, lines, blocks, nchol), bf16),
            pltpu.VMEM((cap, lines, blocks, nchol), bf16),
            pltpu.VMEM((cap, lines, blocks, nchol), bf16),
            pltpu.VMEM((cap, lines, blocks, nchol), bf16),
            pltpu.VMEM((cap, blocks, nchol), f32),
            pltpu.VMEM((wide // 128, cap * half * blocks, 128), f32),
            pltpu.VMEM((half, cap * half, wide), bf16),
            pltpu.VMEM((half, cap * half, wide), bf16),
            pltpu.VMEM((halves, cap * half * near, 128), f32),
            pltpu.VMEM((cap, blocks, electrons, orbitals), bf16),
            dma((6,)),
            dma((3,)),
            dma((2,)),
            dma((lines,)),
            dma((lines,)),
            dma((cap + 1,)),
            dma((cap + 1,)),
            dma((cap,)),
            dma((cap,)),
            dma((1,)),
            dma((1,)),
            dma((cap,)),
            dma((cap,)),
            dma((cap,)),
            dma((cap,)),
            dma((cap,)),
            dma((cap,)),
            dma((1,)),
            dma((1,)),
        ],
        compiler_params=pltpu.CompilerParams(
            collective_id=1, has_side_effects=True, vmem_limit_bytes=60 * 1024 * 1024
        ),
    )(send_walker.reshape(-1), slot_row, fields, walkers, chol_vectors, rotated)


def plan(blocks, walkers, fields, chol_vectors, rotated, send_walker, slot_row):
    every_entry = blocks * send_walker.shape[-1] == walkers.shape[0]
    step = parent_shards if every_entry and blocks % 8 == 0 else shards
    return step(blocks, walkers, fields, chol_vectors, rotated, send_walker, slot_row)


def solution(mesh):
    in_specs = (
        P(("grp", "chol"), None, None),
        P(("grp", "chol"), None),
        P(None, "chol", None),
        P(None, "chol", None),
        P(("grp", "chol"), None, None),
        P(("grp", "chol")),
    )
    out_specs = (P(("grp", "chol"), None, None), P(("grp", "chol"), None))
    return jax.shard_map(
        functools.partial(plan, mesh.shape["chol"]),
        mesh=mesh,
        in_specs=in_specs,
        out_specs=out_specs,
        check_vma=False,
    )
```

```python
import functools
import math

import jax
import jax.numpy as jnp
from jax import lax
from jax.experimental import pallas as pl
from jax.experimental.pallas import tpu as pltpu
from jax.sharding import PartitionSpec as P

field_scale = 1.5
chunk_slots = 16
degrees = 5
unfold_depth = 64
MESH = pl.DeviceIdType.MESH


def stride_of(blocks):
    return next(h for h in (7, 5, 3, 1) if math.gcd(h, blocks) == 1)


def unfold(source, scratch, target):
    depth, rows, orbitals = source.shape
    step = scratch.shape[1] // rows

    def body(b, carry):
        first = pl.multiple_of(b * step, step)
        block = source[pl.ds(first, step)].astype(jnp.float32).reshape(step * rows, orbitals)
        for h in range(orbitals // 128):
            scratch[h] = block[:, h * 128 : (h + 1) * 128]
        for r in range(rows):
            for h in range(orbitals // 128):
                low = r * orbitals + h * 128
                target[pl.ds(first, step), low : low + 128] = scratch[
                    h, pl.ds(r, step, stride=rows), :
                ].astype(jnp.bfloat16)
        return carry

    lax.fori_loop(0, depth // step, body, 0)


def exchange(me, blocks, send, recv, chunk, send_sem, recv_sem, place=lambda d: d, land=lambda d: d):
    hop = stride_of(blocks)

    def step(k, carry):
        peer = lax.rem(me + k * hop, blocks)
        pltpu.make_async_remote_copy(
            src_ref=send.at[chunk, place(peer)],
            dst_ref=recv.at[chunk, land(me)],
            send_sem=send_sem.at[chunk],
            recv_sem=recv_sem.at[chunk],
            device_id={"chol": peer},
            device_id_type=MESH,
        ).start()
        return carry

    lax.fori_loop(1, blocks, step, 0)
    recv[chunk, land(me)] = send[chunk, place(me)]


def arrived(blocks, recv, chunk, sem):
    whole = recv.at[chunk, pl.ds(0, blocks - 1)]
    pltpu.make_async_copy(whole, whole, sem.at[chunk]).wait()


def kernel(
    dims,
    send_walker,
    slot_row,
    walkers,
    fields,
    chol_hbm,
    rotated_raw,
    new_walkers,
    force_bias,
    chol_raw,
    chol_wide,
    chol,
    rotated_wide,
    rotated,
    all_fields,
    br_send,
    br_recv,
    op_send,
    op_recv,
    op_rows,
    totals,
    nw_send,
    nw_recv,
    pair_send,
    pair_recv,
    pair_own,
    fb_send,
    fb_recv,
    send_sems,
    recv_sems,
    field_sems,
    load_sem,
    op_sems,
):
    blocks, chunks, width, cap, rows, elec = dims
    slots, electrons, orbitals = walkers.shape
    nchol = rotated.shape[0]
    halves = orbitals // 128
    me = lax.axis_index("chol")
    pairs = blocks // 2
    core, pair = lax.rem(me, 2), me // 2
    groups = math.gcd(4, blocks)
    share_of = blocks // groups
    hop = stride_of(blocks)
    load = pltpu.make_async_copy(chol_hbm, chol_raw, load_sem)
    load.start()

    barrier = pltpu.get_barrier_semaphore()

    def greet(k, carry):
        pl.semaphore_signal(
            barrier, inc=1, device_id={"chol": lax.rem(me + k, blocks)}, device_id_type=MESH
        )
        return carry

    lax.fori_loop(1, blocks, greet, 0)

    def pick(d, carry):
        for c in range(cap):
            br_send[0, d, c] = walkers[jnp.maximum(send_walker[d * cap + c], 0)]
        return carry

    lax.fori_loop(0, blocks, pick, 0)
    pl.semaphore_wait(barrier, blocks - 1)

    def share(k, carry):
        pltpu.make_async_remote_copy(
            src_ref=fields,
            dst_ref=all_fields.at[core, pair],
            send_sem=field_sems.at[0],
            recv_sem=field_sems.at[1],
            device_id={"chol": lax.rem(pair + k, pairs) * 2 + core},
            device_id_type=MESH,
        ).start()
        return carry

    lax.fori_loop(1, pairs, share, 0)
    all_fields[core, pair] = fields[...]
    load.wait()
    unfold(chol_raw, chol_wide, chol)
    same_core = all_fields.at[core, pl.ds(0, pairs - 1)]
    pltpu.make_async_copy(same_core, same_core, field_sems.at[1]).wait()
    across = pltpu.make_async_remote_copy(
        src_ref=all_fields.at[core],
        dst_ref=all_fields.at[core],
        send_sem=field_sems.at[2],
        recv_sem=field_sems.at[3],
        device_id={"chol": pair * 2 + 1 - core},
        device_id_type=MESH,
    )
    across.start()
    exchange(me, blocks, br_send, br_recv, 0, send_sems.at[0], recv_sems.at[0])

    across.wait_recv()
    scale = field_scale / math.sqrt(nchol)
    cols = rows * orbitals
    tile = min(512, cols)

    @pl.loop(0, cols // tile)
    def _(n):
        at = pl.ds(pl.multiple_of(n * tile, tile), tile)
        left = all_fields[...].reshape(blocks * slots, nchol)
        part = jnp.dot(left, chol[:, at], preferred_element_type=jnp.float32) * scale
        part = part.astype(jnp.bfloat16).reshape(blocks, chunks, width, tile)
        for q in range(chunks):
            op_send[q, :, :, at] = part[:, q]

    def send_operators(q):
        for group in range(groups):
            def step(k, carry):
                peer = lax.rem(me + k * hop, blocks)
                pltpu.make_async_remote_copy(
                    src_ref=op_send.at[q, place(peer)],
                    dst_ref=op_recv.at[q, me],
                    send_sem=send_sems.at[1, q],
                    recv_sem=op_sems.at[q, group],
                    device_id={"chol": peer},
                    device_id_type=MESH,
                ).start()
                return carry

            lax.fori_loop(max(1, group * share_of), (group + 1) * share_of, step, 0)
        op_recv[q, me] = op_send[q, place(me)]

    def place(d):
        return lax.rem(d, 2) * pairs + d // 2

    def taylor(q):
        def spread(k, carry):
            s = lax.rem(me + (blocks - k) * hop, blocks)
            block = op_recv[q, s].astype(jnp.float32)
            for r in range(rows):
                for h in range(halves):
                    low = r * orbitals + h * 128
                    op_rows[h, pl.ds(s * rows + r, width, stride=orbitals), :] = block[
                        :, low : low + 128
                    ]
            return carry

        for group in range(groups):
            count = share_of - 1 if group == 0 else share_of
            whole = op_recv.at[q, pl.ds(0, count)]
            pltpu.make_async_copy(whole, whole, op_sems.at[q, group]).wait()
            lax.fori_loop(group * share_of, (group + 1) * share_of, spread, 0)
        group = 4

        @pl.loop(0, width // group)
        def _(g):
            ops, terms, sums = [], [], []
            for u in range(group):
                w = g * group + u
                first = pl.ds(pl.multiple_of(w * orbitals, orbitals), orbitals)
                ops.append(
                    jnp.concatenate([op_rows[h, first, :] for h in range(halves)], axis=1).astype(
                        jnp.bfloat16
                    )
                )
                row = slot_row[q * width + w]
                terms.append(br_recv[0, row // cap, row % cap])
                sums.append(terms[u].astype(jnp.float32))
            for degree in range(1, degrees + 1):
                for u in range(group):
                    product = lax.dot_general(
                        terms[u],
                        ops[u],
                        (((1,), (1,)), ((), ())),
                        preferred_element_type=jnp.float32,
                    )
                    terms[u] = (product * (1.0 / degree)).astype(jnp.bfloat16)
                    sums[u] = sums[u] + terms[u].astype(jnp.float32)
            for u in range(group):
                w = g * group + u
                new_walkers[q * width + w] = sums[u].astype(jnp.bfloat16)
                place = pl.ds(pl.multiple_of(w * electrons, electrons), electrons)
                for h in range(halves):
                    totals[h, place, :] = sums[u][:, h * 128 : (h + 1) * 128]

        def turn(d, carry):
            for e in range(elec):
                for h in range(halves):
                    low = e * orbitals + h * 128
                    nw_send[q, d, :, low : low + 128] = totals[
                        h, pl.ds(d * elec + e, width, stride=electrons), :
                    ].astype(jnp.bfloat16)
            return carry

        lax.fori_loop(0, blocks, turn, 0)
        exchange(me, blocks, nw_send, nw_recv, q, send_sems.at[2], recv_sems.at[2], land=place)

    def partial(q, half, target):
        left = nw_recv[q, pl.ds(half * pairs, pairs)].reshape(pairs * width, elec * orbitals)
        step = min(256, nchol)

        @pl.loop(0, nchol // step)
        def _(n):
            at = pl.ds(pl.multiple_of(n * step, step), step)
            target[:, at] = lax.dot_general(
                left, rotated[at, :], (((1,), (1,)), ((), ())), preferred_element_type=jnp.float32
            )

    def bias(q):
        partial(q, 1 - core, pair_send.at[q])
        across = pltpu.make_async_remote_copy(
            src_ref=pair_send.at[q],
            dst_ref=pair_recv.at[q],
            send_sem=send_sems.at[4, q],
            recv_sem=recv_sems.at[4, q],
            device_id={"chol": pair * 2 + 1 - core},
            device_id_type=MESH,
        )
        across.start()
        partial(q, core, pair_own)
        across.wait_recv()
        both = (pair_own[...] + pair_recv[q]).astype(jnp.bfloat16)
        fb_send[q] = both.reshape(pairs, width, nchol)

        def step(k, carry):
            peer = lax.rem(pair + k, pairs)
            pltpu.make_async_remote_copy(
                src_ref=fb_send.at[q, peer],
                dst_ref=fb_recv.at[q, pair],
                send_sem=send_sems.at[3, q],
                recv_sem=recv_sems.at[3, q],
                device_id={"chol": peer * 2 + core},
                device_id_type=MESH,
            ).start()
            return carry

        lax.fori_loop(1, pairs, step, 0)
        fb_recv[q, pair] = fb_send[q, pair]

    def finish(q):
        force_bias[q * width : (q + 1) * width, :] = lax.fori_loop(
            1,
            pairs,
            lambda s, acc: acc + fb_recv[q, s].astype(jnp.float32),
            fb_recv[q, 0].astype(jnp.float32),
        )

    for q in range(min(2, chunks)):
        send_operators(q)
    unfold(rotated_raw, rotated_wide, rotated)
    arrived(blocks, br_recv, 0, recv_sems.at[0])
    for q in range(chunks + 2):
        if q < chunks:
            if q + 2 < chunks:
                send_operators(q + 2)
            taylor(q)
        if 1 <= q <= chunks:
            arrived(blocks, nw_recv, q - 1, recv_sems.at[2])
            bias(q - 1)
        if q >= 2:
            arrived(pairs, fb_recv, q - 2, recv_sems.at[3])
            finish(q - 2)
    arrived(blocks, br_send, 0, send_sems.at[0])
    across.wait_send()
    pltpu.make_async_copy(same_core, same_core, field_sems.at[0]).wait()
    for q in range(chunks):
        arrived(blocks, op_send, q, send_sems.at[1])
        arrived(blocks, nw_send, q, send_sems.at[2])
        arrived(pairs, fb_send, q, send_sems.at[3])
        pltpu.make_async_copy(pair_send.at[q], pair_send.at[q], send_sems.at[4, q]).wait()


def shards(blocks, walkers, fields, chol_vectors, rotated, send_walker, slot_row):
    slots, electrons, orbitals = walkers.shape
    nchol, rows, _ = chol_vectors.shape
    elec = rotated.shape[1]
    cap = send_walker.shape[-1]
    width = min(chunk_slots, slots)
    chunks = slots // width
    dims = (blocks, chunks, width, cap, rows, elec)
    bf16, f32 = jnp.bfloat16, jnp.float32
    vmem, smem = (pl.BlockSpec(memory_space=m) for m in (pltpu.VMEM, pltpu.SMEM))
    return pl.pallas_call(
        functools.partial(kernel, dims),
        out_shape=(
            jax.ShapeDtypeStruct(walkers.shape, bf16),
            jax.ShapeDtypeStruct((slots, nchol), f32),
        ),
        in_specs=[smem, smem, vmem, vmem, pl.BlockSpec(memory_space=pl.ANY), vmem],
        out_specs=(vmem, vmem),
        scratch_shapes=[
            pltpu.VMEM(chol_vectors.shape, bf16),
            pltpu.VMEM((orbitals // 128, rows * unfold_depth, 128), f32),
            pltpu.VMEM((nchol, rows * orbitals), bf16),
            pltpu.VMEM((orbitals // 128, elec * unfold_depth, 128), f32),
            pltpu.VMEM((nchol, elec * orbitals), bf16),
            pltpu.VMEM((2, blocks // 2, slots, nchol), bf16),
            pltpu.VMEM((1, blocks, cap, electrons, orbitals), bf16),
            pltpu.VMEM((1, blocks, cap, electrons, orbitals), bf16),
            pltpu.VMEM((chunks, blocks, width, rows * orbitals), bf16),
            pltpu.VMEM((chunks, blocks, width, rows * orbitals), bf16),
            pltpu.VMEM((orbitals // 128, width * orbitals, 128), f32),
            pltpu.VMEM((orbitals // 128, width * electrons, 128), f32),
            pltpu.VMEM((chunks, blocks, width, elec * orbitals), bf16),
            pltpu.VMEM((chunks, blocks, width, elec * orbitals), bf16),
            pltpu.VMEM((chunks, blocks // 2 * width, nchol), f32),
            pltpu.VMEM((chunks, blocks // 2 * width, nchol), f32),
            pltpu.VMEM((blocks // 2 * width, nchol), f32),
            pltpu.VMEM((chunks, blocks // 2, width, nchol), bf16),
            pltpu.VMEM((chunks, blocks // 2, width, nchol), bf16),
            pltpu.SemaphoreType.DMA((5, chunks)),
            pltpu.SemaphoreType.DMA((5, chunks)),
            pltpu.SemaphoreType.DMA((4,)),
            pltpu.SemaphoreType.DMA,
            pltpu.SemaphoreType.DMA((chunks, math.gcd(4, blocks))),
        ],
        compiler_params=pltpu.CompilerParams(
            collective_id=0, has_side_effects=True, vmem_limit_bytes=60 * 1024 * 1024
        ),
    )(
        send_walker.reshape(-1),
        slot_row,
        walkers,
        fields,
        chol_vectors,
        rotated,
    )


def turned(source, target, start, count):
    rows, orbitals = source.shape[1:]
    step = 16

    def body(b, carry):
        first = pl.multiple_of(start + b * step, step)
        block = jnp.swapaxes(source[pl.ds(first, step)], 0, 1)
        for r in range(rows):
            target[pl.ds(first, step), r * orbitals : (r + 1) * orbitals] = block[r]
        return carry

    lax.fori_loop(0, count // step, body, 0)


def parent_kernel(
    dims,
    send_walker,
    slot_row,
    fields,
    walkers_hbm,
    chol_hbm,
    rotated_hbm,
    branch,
    fb_total,
    walkers,
    chol_raw,
    chol,
    rotated_raw,
    rotated,
    all_fields,
    left,
    op_rows,
    op_send,
    op_recv,
    nw_full,
    nw_send,
    nw_recv,
    part,
    pair_recv,
    row_send,
    row_recv,
    fb_send,
    fb_recv,
    fw_wide,
    fw_send,
    fw_recv,
    fw_rows,
    load_sems,
    field_send,
    field_core,
    field_line,
    field_row,
    op_sent,
    op_got,
    nw_sent,
    nw_got,
    br_sent,
    br_got,
    pair_sent,
    pair_got,
    row_sent,
    row_got,
    fb_sent,
    fb_got,
    fw_sent,
    fw_got,
):
    blocks, cap, rows, elec = dims
    slots, nchol = fields.shape
    electrons, orbitals = walkers.shape[1:]
    halves = orbitals // 128
    me = lax.axis_index("chol")
    pairs, lines, half = blocks // 2, blocks // 4, blocks // 2
    hop = stride_of(blocks)
    core, pair = lax.rem(me, 2), me // 2
    line, across = pair // 2, lax.rem(pair, 2)
    side, local = me // half, lax.rem(me, half)
    away = 1 - side
    near = electrons // 2
    bf16, f32 = jnp.bfloat16, jnp.float32

    def wait(ref, sem):
        pltpu.make_async_copy(ref, ref, sem).wait()

    def send(src, dst, sent, got, peer):
        pltpu.make_async_remote_copy(
            src_ref=src,
            dst_ref=dst,
            send_sem=sent,
            recv_sem=got,
            device_id={"chol": peer},
            device_id_type=MESH,
        ).start()

    def everyone(to):
        def step(t, carry):
            to(lax.rem(me + t * hop, blocks))
            return carry

        lax.fori_loop(1, blocks, step, 0)

    def row_of(d):
        return lax.rem(d, 2) * pairs + d // 2

    pieces = 4
    span = nchol // pieces
    chol_loads = [
        pltpu.make_async_copy(
            chol_hbm.at[pl.ds(p * span, span)], chol_raw.at[pl.ds(p * span, span)], load_sems.at[p]
        )
        for p in range(pieces)
    ]
    for load in chol_loads:
        load.start()
    walker_load = pltpu.make_async_copy(walkers_hbm, walkers, load_sems.at[pieces])
    rotated_load = pltpu.make_async_copy(rotated_hbm, rotated_raw, load_sems.at[pieces + 1])
    walker_load.start()
    rotated_load.start()

    barrier = pltpu.get_barrier_semaphore()

    def greet(k, carry):
        pl.semaphore_signal(
            barrier, inc=1, device_id={"chol": lax.rem(me + k, blocks)}, device_id_type=MESH
        )
        return carry

    lax.fori_loop(1, blocks, greet, 0)

    order = lax.broadcasted_iota(jnp.int32, (slots, slots), 0)
    place = lax.broadcasted_iota(jnp.int32, (slots, slots), 1)
    chosen = jnp.zeros((slots, slots), f32)
    for p in range(slots):
        entry = slot_row[p]
        target = lax.rem(entry, cap) * blocks + entry // cap
        chosen = jnp.where((place == p) & (order == target), 1.0, chosen)
    all_fields[pair, core] = jnp.dot(
        chosen.astype(bf16), fields[...], preferred_element_type=f32
    ).astype(bf16)

    for p in range(pieces):
        chol_loads[p].wait()
        turned(chol_raw, chol, p * span, span)

    scale = field_scale / math.sqrt(nchol)
    cols = rows * orbitals
    tile = min(1024, cols)
    deep = tile // orbitals

    def operators(m):
        @pl.loop(0, cols // tile)
        def _(n):
            at = pl.ds(pl.multiple_of(n * tile, tile), tile)
            out = jnp.dot(left[:m], chol[:, at], preferred_element_type=f32) * scale
            for i in range(deep):
                op_rows[n * deep + i, :m] = out[:, i * orbitals : (i + 1) * orbitals].astype(bf16)

    def packed(b):
        return jnp.swapaxes(op_rows[:, b * blocks : (b + 1) * blocks], 0, 1)

    def chip_operators(which):
        left[:slots] = all_fields[pair, which]
        operators(slots)
        for c in range(cap):
            op_send[c, :, 0, which] = packed(c)

    def send_chip_operators(which):
        def to(s):
            send(
                op_send.at[:, s, 0, which],
                op_recv.at[:, me, 0, which],
                op_sent.at[cap],
                op_got.at[cap],
                s,
            )

        everyone(to)
        for c in range(cap):
            op_recv[c, me, 0, which] = op_send[c, me, 0, which]

    def other_operators(c, first, count):
        for k in range(count):
            chip = lax.rem(pair + first + k, pairs)
            for q in range(2):
                low = (k * 2 + q) * blocks
                at = pl.ds(pl.multiple_of(c * blocks, blocks), blocks)
                left[low : low + blocks] = all_fields[chip, q, at]
        operators(count * 2 * blocks)

        for k in range(count):
            for q in range(2):
                op_send[c, :, first + k, q] = packed(k * 2 + q)

        def to(s):
            send(
                op_send.at[c, s, pl.ds(first, count)],
                op_recv.at[c, me, pl.ds(first, count)],
                op_sent.at[c],
                op_got.at[c],
                s,
            )

        everyone(to)
        for k in range(count):
            for q in range(2):
                op_recv[c, me, first + k, q] = op_send[c, me, first + k, q]

    partner = pair * 2 + 1 - core
    beside = (line * 2 + 1 - across) * 2 + core

    def line_at(j):
        return lax.rem(line + lines - j, lines)

    own, twin = all_fields.at[pair, core], all_fields.at[pair, 1 - core]
    pl.semaphore_wait(barrier, blocks - 1)
    send(own, own, field_send.at[0], field_core.at[0], partner)
    for j in range(1, lines):
        peer = (lax.rem(line + j, lines) * 2 + across) * 2 + core
        send(own, own, field_send.at[2], field_line.at[j], peer)
    send(own, own, field_send.at[1], field_row.at[0], beside)

    @pl.loop(0, 2)
    def _(t):
        @pl.when(t == 1)
        def _():
            for j in range(1, lines):
                held = all_fields.at[line_at(j) * 2 + across, core]
                wait(held, field_line.at[j])
                send(held, held, field_send.at[1], field_row.at[j], beside)
                send(held, held, field_send.at[0], field_core.at[1], partner)
            wait(twin, field_core.at[0])

        which = lax.rem(core + t, 2)
        chip_operators(which)
        send_chip_operators(which)

    for j in range(lines):
        held = all_fields.at[line_at(j) * 2 + 1 - across, core]
        wait(held, field_row.at[j])
        send(held, held, field_send.at[0], field_core.at[1], partner)
    wait(all_fields.at[pl.ds(0, pairs - 1), 0], field_core.at[1])

    split = pairs // 2

    @pl.loop(0, cap)
    def _(c):
        other_operators(c, 1, split)
        other_operators(c, 1 + split, pairs - 1 - split)

    rotated_load.wait()
    turned(rotated_raw, rotated, 0, nchol)
    walker_load.wait()

    def taylor(c):
        group = 4

        @pl.loop(0, blocks // group)
        def _(g):
            ops, terms, sums = [], [], []
            for u in range(group):
                r = g * group + u
                chip, q = lax.rem(r, pairs), r // pairs
                ops.append(
                    jnp.concatenate(
                        [
                            op_recv[c, o, lax.rem(chip + pairs - o // 2, pairs), q]
                            for o in range(blocks)
                        ],
                        axis=0,
                    )
                )
                entry = jnp.maximum(send_walker[c, chip * 2 + q], 0)
                terms.append(walkers[entry])
                sums.append(terms[u].astype(f32))
            for degree in range(1, degrees + 1):
                for u in range(group):
                    product = lax.dot_general(
                        terms[u], ops[u], (((1,), (1,)), ((), ())), preferred_element_type=f32
                    )
                    terms[u] = (product * (1.0 / degree)).astype(bf16)
                    sums[u] = sums[u] + terms[u].astype(f32)
            for u in range(group):
                r = g * group + u
                nw_full[c, r] = sums[u].astype(bf16)

        for o in range(0, blocks, 16 // elec):
            block = jnp.swapaxes(nw_full[c, :, o * elec : o * elec + 16], 0, 1)
            for e in range(16):
                low = e % elec * orbitals
                nw_send[c, o + e // elec, :, low : low + orbitals] = block[e]

        def to_owner(o):
            send(nw_send.at[c, o], nw_recv.at[c, me], nw_sent.at[c], nw_got.at[c], o)

        everyone(to_owner)
        nw_recv[c, me] = nw_send[c, me]
        mine = pl.ds(pl.multiple_of(side * near, near), near)

        def to_slot(d):
            @pl.when(d // half != side)
            def _():
                send(
                    nw_full.at[c, row_of(d), mine],
                    branch.at[c, me, mine],
                    br_sent.at[0],
                    br_got.at[0],
                    d,
                )

            @pl.when(d // half == side)
            def _():
                send(nw_full.at[c, row_of(d)], branch.at[c, me], br_sent.at[0], br_got.at[0], d)

        everyone(to_slot)
        branch[c, me] = nw_full[c, row_of(me)]

    def bias(c):
        rows_in = nw_recv[c].reshape(blocks * blocks, elec * orbitals)
        step = min(256, nchol)

        @pl.loop(0, nchol // step)
        def _(n):
            at = pl.ds(pl.multiple_of(n * step, step), step)
            out = lax.dot_general(
                rows_in, rotated[at, :], (((1,), (1,)), ((), ())), preferred_element_type=f32
            ).reshape(blocks, 2, pairs, step)
            for q in range(2):
                mine = out[:, q].reshape(blocks * pairs, step)
                for h in range(step // 128):
                    part[c, q, n * (step // 128) + h] = mine[:, h * 128 : (h + 1) * 128]

        send(part.at[c, 1 - core], pair_recv.at[c], pair_sent.at[c], pair_got.at[c], partner)

    def reduced(c, chip, h):
        at = pl.ds(chip, blocks, stride=pairs)
        return part[c, core, h, at, :] + pair_recv[c, h, at, :]

    def reduce(c):
        wait(pair_recv.at[c], pair_got.at[c])

        def pick(z, carry):
            for h in range(nchol // 128):
                both = reduced(c, z * 2 + 1 - across, h)
                row_send[c, z, :, h * 128 : (h + 1) * 128] = both.astype(bf16)
            return carry

        lax.fori_loop(0, lines, pick, 0)
        send(row_send.at[c], row_recv.at[c], row_sent.at[c], row_got.at[c], beside)

    def spread(c):
        wait(row_recv.at[c], row_got.at[c])

        def pick(z, carry):
            for h in range(nchol // 128):
                low = h * 128
                both = reduced(c, z * 2 + across, h)
                both = both + row_recv[c, z, :, low : low + 128].astype(f32)
                fb_send[c, z, :, low : low + 128] = both.astype(bf16)
            return carry

        lax.fori_loop(0, lines, pick, 0)

        def step(k, carry):
            z = lax.rem(line + k, lines)
            send(
                fb_send.at[c, z],
                fb_recv.at[c, line],
                fb_sent.at[c],
                fb_got.at[c],
                (z * 2 + across) * 2 + core,
            )
            return carry

        lax.fori_loop(1, lines, step, 0)
        fb_recv[c, line] = fb_send[c, line]

    def finish(c):
        wait(fb_recv.at[c, pl.ds(0, lines - 1)], fb_got.at[c])
        fb_total[c] = lax.fori_loop(
            1,
            lines,
            lambda s, acc: acc + fb_recv[c, s].astype(f32),
            fb_recv[c, 0].astype(f32),
        )

    def forward():
        count = half * blocks
        for c in range(cap):
            block = nw_recv[c, pl.ds(away * half, half)].astype(f32)
            block = block.reshape(count, elec * orbitals)
            for h in range(elec * orbitals // 128):
                fw_wide[h, c * count : (c + 1) * count] = block[:, h * 128 : (h + 1) * 128]

        def gather(t, carry):
            at = pl.ds(row_of(side * half + t), cap * half, stride=blocks)
            for h in range(elec * orbitals // 128):
                fw_send[t, :, h * 128 : (h + 1) * 128] = fw_wide[h, at, :].astype(bf16)
            return carry

        lax.fori_loop(0, half, gather, 0)

        def step(k, carry):
            t = lax.rem(local + k, half)
            send(fw_send.at[t], fw_recv.at[local], fw_sent.at[0], fw_got.at[0], side * half + t)
            return carry

        lax.fori_loop(1, half, step, 0)
        fw_recv[local] = fw_send[local]

    def collect():
        wait(fw_recv.at[pl.ds(0, half - 1)], fw_got.at[0])

        def fold(o, carry):
            block = fw_recv[o].astype(f32)
            for e in range(elec):
                for h in range(halves):
                    low = e * orbitals + h * 128
                    fw_rows[h, pl.ds(o * elec + e, cap * half, stride=near), :] = block[
                        :, low : low + 128
                    ]
            return carry

        lax.fori_loop(0, half, fold, 0)
        wait(branch.at[:, pl.ds(0, half - 1 + half // 2)], br_got.at[0])

        def put(s, carry):
            for c in range(cap):
                at = pl.ds(pl.multiple_of((c * half + s) * near, near), near)
                value = jnp.concatenate([fw_rows[h, at, :] for h in range(halves)], axis=1)
                mine = pl.ds(pl.multiple_of(side * near, near), near)
                branch[c, away * half + s, mine] = value.astype(bf16)
            return carry

        lax.fori_loop(0, half, put, 0)

    wait(op_recv.at[:, pl.ds(0, blocks - 1), 0], op_got.at[cap])
    for c in range(cap):
        wait(op_recv.at[c, pl.ds(0, blocks - 1), pl.ds(1, pairs - 1)], op_got.at[c])
        taylor(c)
    for c in range(cap):
        wait(nw_recv.at[c, pl.ds(0, blocks - 1)], nw_got.at[c])
        bias(c)
        if c == cap - 1:
            forward()
        reduce(c)
        spread(c)
    collect()
    for c in range(cap):
        finish(c)

    wait(all_fields.at[:, 0], field_send.at[0])
    wait(all_fields.at[pl.ds(0, lines), 0], field_send.at[1])
    wait(all_fields.at[pl.ds(0, lines - 1), 0], field_send.at[2])
    wait(op_recv.at[:, pl.ds(0, blocks - 1), 0], op_sent.at[cap])
    wait(branch.at[:, pl.ds(0, half - 1 + half // 2)], br_sent.at[0])
    wait(fw_send.at[pl.ds(0, half - 1)], fw_sent.at[0])
    for c in range(cap):
        wait(op_recv.at[c, pl.ds(0, blocks - 1), pl.ds(1, pairs - 1)], op_sent.at[c])
        wait(nw_send.at[c, pl.ds(0, blocks - 1)], nw_sent.at[c])
        wait(pair_recv.at[c], pair_sent.at[c])
        wait(row_send.at[c], row_sent.at[c])
        wait(fb_send.at[c, pl.ds(0, lines - 1)], fb_sent.at[c])


def place_kernel(slot_row, branch, fb_total, new_walkers, force_bias):
    cap = branch.shape[0]

    @pl.loop(0, slot_row.shape[0])
    def _(p):
        entry = slot_row[p]
        c, s = lax.rem(entry, cap), entry // cap
        new_walkers[p] = branch[c, s]
        force_bias[pl.ds(p, 1), :] = fb_total[c, pl.ds(s, 1), :]


def parent_shards(blocks, walkers, fields, chol_vectors, rotated, send_walker, slot_row):
    slots, electrons, orbitals = walkers.shape
    nchol, rows, _ = chol_vectors.shape
    elec = rotated.shape[1]
    cap = send_walker.shape[-1]
    bf16, f32 = jnp.bfloat16, jnp.float32
    pairs, lines, half = blocks // 2, blocks // 4, blocks // 2
    halves, near = orbitals // 128, electrons // 2
    most = max(pairs // 2 * 2 * blocks, slots)
    wide = elec * orbitals
    vmem, smem, anywhere = (
        pl.BlockSpec(memory_space=m) for m in (pltpu.VMEM, pltpu.SMEM, pl.ANY)
    )
    dma = pltpu.SemaphoreType.DMA
    branch, fb_total = pl.pallas_call(
        functools.partial(parent_kernel, (blocks, cap, rows, elec)),
        out_shape=(
            jax.ShapeDtypeStruct((cap, blocks, electrons, orbitals), bf16),
            jax.ShapeDtypeStruct((cap, blocks, nchol), f32),
        ),
        in_specs=[smem, smem, vmem, anywhere, anywhere, anywhere],
        out_specs=(vmem, vmem),
        scratch_shapes=[
            pltpu.VMEM(walkers.shape, bf16),
            pltpu.VMEM(chol_vectors.shape, bf16),
            pltpu.VMEM((nchol, rows * orbitals), bf16),
            pltpu.VMEM(rotated.shape, bf16),
            pltpu.VMEM((nchol, wide), bf16),
            pltpu.VMEM((pairs, 2, slots, nchol), bf16),
            pltpu.VMEM((most, nchol), bf16),
            pltpu.VMEM((rows, most, orbitals), bf16),
            pltpu.VMEM((cap, blocks, pairs, 2, rows, orbitals), bf16),
            pltpu.VMEM((cap, blocks, pairs, 2, rows, orbitals), bf16),
            pltpu.VMEM((cap, blocks, electrons, orbitals), bf16),
            pltpu.VMEM((cap, blocks, blocks, wide), bf16),
            pltpu.VMEM((cap, blocks, blocks, wide), bf16),
            pltpu.VMEM((cap, 2, nchol // 128, blocks * pairs, 128), f32),
            pltpu.VMEM((cap, nchol // 128, blocks * pairs, 128), f32),
            pltpu.VMEM((cap, lines, blocks, nchol), bf16),
            pltpu.VMEM((cap, lines, blocks, nchol), bf16),
            pltpu.VMEM((cap, lines, blocks, nchol), bf16),
            pltpu.VMEM((cap, lines, blocks, nchol), bf16),
            pltpu.VMEM((wide // 128, cap * half * blocks, 128), f32),
            pltpu.VMEM((half, cap * half, wide), bf16),
            pltpu.VMEM((half, cap * half, wide), bf16),
            pltpu.VMEM((halves, cap * half * near, 128), f32),
            dma((6,)),
            dma((3,)),
            dma((2,)),
            dma((lines,)),
            dma((lines,)),
            dma((cap + 1,)),
            dma((cap + 1,)),
            dma((cap,)),
            dma((cap,)),
            dma((1,)),
            dma((1,)),
            dma((cap,)),
            dma((cap,)),
            dma((cap,)),
            dma((cap,)),
            dma((cap,)),
            dma((cap,)),
            dma((1,)),
            dma((1,)),
        ],
        compiler_params=pltpu.CompilerParams(
            collective_id=1, has_side_effects=True, vmem_limit_bytes=60 * 1024 * 1024
        ),
    )(
        jnp.transpose(send_walker, (0, 2, 1)).reshape(cap, blocks),
        slot_row,
        fields,
        walkers,
        chol_vectors,
        rotated,
    )
    return pl.pallas_call(
        place_kernel,
        out_shape=(
            jax.ShapeDtypeStruct(walkers.shape, bf16),
            jax.ShapeDtypeStruct((slots, nchol), f32),
        ),
        in_specs=[smem, vmem, vmem],
        out_specs=(vmem, vmem),
    )(slot_row, branch, fb_total)


def plan(blocks, walkers, fields, chol_vectors, rotated, send_walker, slot_row):
    every_entry = blocks * send_walker.shape[-1] == walkers.shape[0]
    step = parent_shards if every_entry and blocks % 8 == 0 else shards
    return step(blocks, walkers, fields, chol_vectors, rotated, send_walker, slot_row)


def solution(mesh):
    in_specs = (
        P(("grp", "chol"), None, None),
        P(("grp", "chol"), None),
        P(None, "chol", None),
        P(None, "chol", None),
        P(("grp", "chol"), None, None),
        P(("grp", "chol")),
    )
    out_specs = (P(("grp", "chol"), None, None), P(("grp", "chol"), None))
    return jax.shard_map(
        functools.partial(plan, mesh.shape["chol"]),
        mesh=mesh,
        in_specs=in_specs,
        out_specs=out_specs,
        check_vma=False,
    )
```

```python
import functools
import math

import jax
import jax.numpy as jnp
from jax import lax
from jax.experimental import pallas as pl
from jax.experimental.pallas import tpu as pltpu
from jax.sharding import PartitionSpec as P

field_scale = 1.5
chunk_slots = 16
degrees = 5
unfold_depth = 64
MESH = pl.DeviceIdType.MESH


def stride_of(blocks):
    return next(h for h in (7, 5, 3, 1) if math.gcd(h, blocks) == 1)


def unfold(source, scratch, target):
    depth, rows, orbitals = source.shape
    step = scratch.shape[1] // rows

    def body(b, carry):
        first = pl.multiple_of(b * step, step)
        block = source[pl.ds(first, step)].astype(jnp.float32).reshape(step * rows, orbitals)
        for h in range(orbitals // 128):
            scratch[h] = block[:, h * 128 : (h + 1) * 128]
        for r in range(rows):
            for h in range(orbitals // 128):
                low = r * orbitals + h * 128
                target[pl.ds(first, step), low : low + 128] = scratch[
                    h, pl.ds(r, step, stride=rows), :
                ].astype(jnp.bfloat16)
        return carry

    lax.fori_loop(0, depth // step, body, 0)


def exchange(me, blocks, send, recv, chunk, send_sem, recv_sem, place=lambda d: d, land=lambda d: d):
    hop = stride_of(blocks)

    def step(k, carry):
        peer = lax.rem(me + k * hop, blocks)
        pltpu.make_async_remote_copy(
            src_ref=send.at[chunk, place(peer)],
            dst_ref=recv.at[chunk, land(me)],
            send_sem=send_sem.at[chunk],
            recv_sem=recv_sem.at[chunk],
            device_id={"chol": peer},
            device_id_type=MESH,
        ).start()
        return carry

    lax.fori_loop(1, blocks, step, 0)
    recv[chunk, land(me)] = send[chunk, place(me)]


def arrived(blocks, recv, chunk, sem):
    whole = recv.at[chunk, pl.ds(0, blocks - 1)]
    pltpu.make_async_copy(whole, whole, sem.at[chunk]).wait()


def kernel(
    dims,
    send_walker,
    slot_row,
    walkers,
    fields,
    chol_hbm,
    rotated_raw,
    new_walkers,
    force_bias,
    chol_raw,
    chol_wide,
    chol,
    rotated_wide,
    rotated,
    all_fields,
    br_send,
    br_recv,
    op_send,
    op_recv,
    op_rows,
    totals,
    nw_send,
    nw_recv,
    pair_send,
    pair_recv,
    pair_own,
    fb_send,
    fb_recv,
    send_sems,
    recv_sems,
    field_sems,
    load_sem,
    op_sems,
):
    blocks, chunks, width, cap, rows, elec = dims
    slots, electrons, orbitals = walkers.shape
    nchol = rotated.shape[0]
    halves = orbitals // 128
    me = lax.axis_index("chol")
    pairs = blocks // 2
    core, pair = lax.rem(me, 2), me // 2
    groups = math.gcd(4, blocks)
    share_of = blocks // groups
    hop = stride_of(blocks)
    load = pltpu.make_async_copy(chol_hbm, chol_raw, load_sem)
    load.start()

    barrier = pltpu.get_barrier_semaphore()

    def greet(k, carry):
        pl.semaphore_signal(
            barrier, inc=1, device_id={"chol": lax.rem(me + k, blocks)}, device_id_type=MESH
        )
        return carry

    lax.fori_loop(1, blocks, greet, 0)

    def pick(d, carry):
        for c in range(cap):
            br_send[0, d, c] = walkers[jnp.maximum(send_walker[d * cap + c], 0)]
        return carry

    lax.fori_loop(0, blocks, pick, 0)
    pl.semaphore_wait(barrier, blocks - 1)

    def share(k, carry):
        pltpu.make_async_remote_copy(
            src_ref=fields,
            dst_ref=all_fields.at[core, pair],
            send_sem=field_sems.at[0],
            recv_sem=field_sems.at[1],
            device_id={"chol": lax.rem(pair + k, pairs) * 2 + core},
            device_id_type=MESH,
        ).start()
        return carry

    lax.fori_loop(1, pairs, share, 0)
    all_fields[core, pair] = fields[...]
    load.wait()
    unfold(chol_raw, chol_wide, chol)
    same_core = all_fields.at[core, pl.ds(0, pairs - 1)]
    pltpu.make_async_copy(same_core, same_core, field_sems.at[1]).wait()
    across = pltpu.make_async_remote_copy(
        src_ref=all_fields.at[core],
        dst_ref=all_fields.at[core],
        send_sem=field_sems.at[2],
        recv_sem=field_sems.at[3],
        device_id={"chol": pair * 2 + 1 - core},
        device_id_type=MESH,
    )
    across.start()
    exchange(me, blocks, br_send, br_recv, 0, send_sems.at[0], recv_sems.at[0])

    across.wait_recv()
    scale = field_scale / math.sqrt(nchol)
    cols = rows * orbitals
    tile = min(512, cols)

    @pl.loop(0, cols // tile)
    def _(n):
        at = pl.ds(pl.multiple_of(n * tile, tile), tile)
        left = all_fields[...].reshape(blocks * slots, nchol)
        part = jnp.dot(left, chol[:, at], preferred_element_type=jnp.float32) * scale
        part = part.astype(jnp.bfloat16).reshape(blocks, chunks, width, tile)
        for q in range(chunks):
            op_send[q, :, :, at] = part[:, q]

    def send_operators(q):
        for group in range(groups):
            def step(k, carry):
                peer = lax.rem(me + k * hop, blocks)
                pltpu.make_async_remote_copy(
                    src_ref=op_send.at[q, place(peer)],
                    dst_ref=op_recv.at[q, me],
                    send_sem=send_sems.at[1, q],
                    recv_sem=op_sems.at[q, group],
                    device_id={"chol": peer},
                    device_id_type=MESH,
                ).start()
                return carry

            lax.fori_loop(max(1, group * share_of), (group + 1) * share_of, step, 0)
        op_recv[q, me] = op_send[q, place(me)]

    def place(d):
        return lax.rem(d, 2) * pairs + d // 2

    def taylor(q):
        def spread(k, carry):
            s = lax.rem(me + (blocks - k) * hop, blocks)
            block = op_recv[q, s].astype(jnp.float32)
            for r in range(rows):
                for h in range(halves):
                    low = r * orbitals + h * 128
                    op_rows[h, pl.ds(s * rows + r, width, stride=orbitals), :] = block[
                        :, low : low + 128
                    ]
            return carry

        for group in range(groups):
            count = share_of - 1 if group == 0 else share_of
            whole = op_recv.at[q, pl.ds(0, count)]
            pltpu.make_async_copy(whole, whole, op_sems.at[q, group]).wait()
            lax.fori_loop(group * share_of, (group + 1) * share_of, spread, 0)
        group = 4

        @pl.loop(0, width // group)
        def _(g):
            ops, terms, sums = [], [], []
            for u in range(group):
                w = g * group + u
                first = pl.ds(pl.multiple_of(w * orbitals, orbitals), orbitals)
                ops.append(
                    jnp.concatenate([op_rows[h, first, :] for h in range(halves)], axis=1).astype(
                        jnp.bfloat16
                    )
                )
                row = slot_row[q * width + w]
                terms.append(br_recv[0, row // cap, row % cap])
                sums.append(terms[u].astype(jnp.float32))
            for degree in range(1, degrees + 1):
                for u in range(group):
                    product = lax.dot_general(
                        terms[u],
                        ops[u],
                        (((1,), (1,)), ((), ())),
                        preferred_element_type=jnp.float32,
                    )
                    terms[u] = (product * (1.0 / degree)).astype(jnp.bfloat16)
                    sums[u] = sums[u] + terms[u].astype(jnp.float32)
            for u in range(group):
                w = g * group + u
                new_walkers[q * width + w] = sums[u].astype(jnp.bfloat16)
                place = pl.ds(pl.multiple_of(w * electrons, electrons), electrons)
                for h in range(halves):
                    totals[h, place, :] = sums[u][:, h * 128 : (h + 1) * 128]

        def turn(d, carry):
            for e in range(elec):
                for h in range(halves):
                    low = e * orbitals + h * 128
                    nw_send[q, d, :, low : low + 128] = totals[
                        h, pl.ds(d * elec + e, width, stride=electrons), :
                    ].astype(jnp.bfloat16)
            return carry

        lax.fori_loop(0, blocks, turn, 0)
        exchange(me, blocks, nw_send, nw_recv, q, send_sems.at[2], recv_sems.at[2], land=place)

    def partial(q, half, target):
        left = nw_recv[q, pl.ds(half * pairs, pairs)].reshape(pairs * width, elec * orbitals)
        step = min(256, nchol)

        @pl.loop(0, nchol // step)
        def _(n):
            at = pl.ds(pl.multiple_of(n * step, step), step)
            target[:, at] = lax.dot_general(
                left, rotated[at, :], (((1,), (1,)), ((), ())), preferred_element_type=jnp.float32
            )

    def bias(q):
        partial(q, 1 - core, pair_send.at[q])
        across = pltpu.make_async_remote_copy(
            src_ref=pair_send.at[q],
            dst_ref=pair_recv.at[q],
            send_sem=send_sems.at[4, q],
            recv_sem=recv_sems.at[4, q],
            device_id={"chol": pair * 2 + 1 - core},
            device_id_type=MESH,
        )
        across.start()
        partial(q, core, pair_own)
        across.wait_recv()
        both = (pair_own[...] + pair_recv[q]).astype(jnp.bfloat16)
        fb_send[q] = both.reshape(pairs, width, nchol)

        def step(k, carry):
            peer = lax.rem(pair + k, pairs)
            pltpu.make_async_remote_copy(
                src_ref=fb_send.at[q, peer],
                dst_ref=fb_recv.at[q, pair],
                send_sem=send_sems.at[3, q],
                recv_sem=recv_sems.at[3, q],
                device_id={"chol": peer * 2 + core},
                device_id_type=MESH,
            ).start()
            return carry

        lax.fori_loop(1, pairs, step, 0)
        fb_recv[q, pair] = fb_send[q, pair]

    def finish(q):
        force_bias[q * width : (q + 1) * width, :] = lax.fori_loop(
            1,
            pairs,
            lambda s, acc: acc + fb_recv[q, s].astype(jnp.float32),
            fb_recv[q, 0].astype(jnp.float32),
        )

    for q in range(min(2, chunks)):
        send_operators(q)
    unfold(rotated_raw, rotated_wide, rotated)
    arrived(blocks, br_recv, 0, recv_sems.at[0])
    for q in range(chunks + 2):
        if q < chunks:
            if q + 2 < chunks:
                send_operators(q + 2)
            taylor(q)
        if 1 <= q <= chunks:
            arrived(blocks, nw_recv, q - 1, recv_sems.at[2])
            bias(q - 1)
        if q >= 2:
            arrived(pairs, fb_recv, q - 2, recv_sems.at[3])
            finish(q - 2)
    arrived(blocks, br_send, 0, send_sems.at[0])
    across.wait_send()
    pltpu.make_async_copy(same_core, same_core, field_sems.at[0]).wait()
    for q in range(chunks):
        arrived(blocks, op_send, q, send_sems.at[1])
        arrived(blocks, nw_send, q, send_sems.at[2])
        arrived(pairs, fb_send, q, send_sems.at[3])
        pltpu.make_async_copy(pair_send.at[q], pair_send.at[q], send_sems.at[4, q]).wait()


def shards(blocks, walkers, fields, chol_vectors, rotated, send_walker, slot_row):
    slots, electrons, orbitals = walkers.shape
    nchol, rows, _ = chol_vectors.shape
    elec = rotated.shape[1]
    cap = send_walker.shape[-1]
    width = min(chunk_slots, slots)
    chunks = slots // width
    dims = (blocks, chunks, width, cap, rows, elec)
    bf16, f32 = jnp.bfloat16, jnp.float32
    vmem, smem = (pl.BlockSpec(memory_space=m) for m in (pltpu.VMEM, pltpu.SMEM))
    return pl.pallas_call(
        functools.partial(kernel, dims),
        out_shape=(
            jax.ShapeDtypeStruct(walkers.shape, bf16),
            jax.ShapeDtypeStruct((slots, nchol), f32),
        ),
        in_specs=[smem, smem, vmem, vmem, pl.BlockSpec(memory_space=pl.ANY), vmem],
        out_specs=(vmem, vmem),
        scratch_shapes=[
            pltpu.VMEM(chol_vectors.shape, bf16),
            pltpu.VMEM((orbitals // 128, rows * unfold_depth, 128), f32),
            pltpu.VMEM((nchol, rows * orbitals), bf16),
            pltpu.VMEM((orbitals // 128, elec * unfold_depth, 128), f32),
            pltpu.VMEM((nchol, elec * orbitals), bf16),
            pltpu.VMEM((2, blocks // 2, slots, nchol), bf16),
            pltpu.VMEM((1, blocks, cap, electrons, orbitals), bf16),
            pltpu.VMEM((1, blocks, cap, electrons, orbitals), bf16),
            pltpu.VMEM((chunks, blocks, width, rows * orbitals), bf16),
            pltpu.VMEM((chunks, blocks, width, rows * orbitals), bf16),
            pltpu.VMEM((orbitals // 128, width * orbitals, 128), f32),
            pltpu.VMEM((orbitals // 128, width * electrons, 128), f32),
            pltpu.VMEM((chunks, blocks, width, elec * orbitals), bf16),
            pltpu.VMEM((chunks, blocks, width, elec * orbitals), bf16),
            pltpu.VMEM((chunks, blocks // 2 * width, nchol), f32),
            pltpu.VMEM((chunks, blocks // 2 * width, nchol), f32),
            pltpu.VMEM((blocks // 2 * width, nchol), f32),
            pltpu.VMEM((chunks, blocks // 2, width, nchol), bf16),
            pltpu.VMEM((chunks, blocks // 2, width, nchol), bf16),
            pltpu.SemaphoreType.DMA((5, chunks)),
            pltpu.SemaphoreType.DMA((5, chunks)),
            pltpu.SemaphoreType.DMA((4,)),
            pltpu.SemaphoreType.DMA,
            pltpu.SemaphoreType.DMA((chunks, math.gcd(4, blocks))),
        ],
        compiler_params=pltpu.CompilerParams(
            collective_id=0, has_side_effects=True, vmem_limit_bytes=60 * 1024 * 1024
        ),
    )(
        send_walker.reshape(-1),
        slot_row,
        walkers,
        fields,
        chol_vectors,
        rotated,
    )


def turned(source, target, start, count):
    rows, orbitals = source.shape[1:]
    step = 16

    def body(b, carry):
        first = pl.multiple_of(start + b * step, step)
        block = jnp.swapaxes(source[pl.ds(first, step)], 0, 1)
        for r in range(rows):
            target[pl.ds(first, step), r * orbitals : (r + 1) * orbitals] = block[r]
        return carry

    lax.fori_loop(0, count // step, body, 0)


def parent_kernel(
    dims,
    send_walker,
    slot_row,
    fields,
    walkers_hbm,
    chol_hbm,
    rotated_hbm,
    branch,
    fb_total,
    walkers,
    chol_raw,
    chol,
    rotated_raw,
    rotated,
    all_fields,
    left,
    op_rows,
    op_send,
    op_recv,
    nw_full,
    nw_send,
    nw_recv,
    part,
    pair_recv,
    row_send,
    row_recv,
    fb_send,
    fb_recv,
    fw_wide,
    fw_send,
    fw_recv,
    fw_rows,
    load_sems,
    field_send,
    field_core,
    field_line,
    field_row,
    op_sent,
    op_got,
    nw_sent,
    nw_got,
    br_sent,
    br_got,
    pair_sent,
    pair_got,
    row_sent,
    row_got,
    fb_sent,
    fb_got,
    fw_sent,
    fw_got,
):
    blocks, cap, rows, elec = dims
    slots, nchol = fields.shape
    electrons, orbitals = walkers.shape[1:]
    halves = orbitals // 128
    me = lax.axis_index("chol")
    pairs, lines, half = blocks // 2, blocks // 4, blocks // 2
    hop = stride_of(blocks)
    core, pair = lax.rem(me, 2), me // 2
    line, across = pair // 2, lax.rem(pair, 2)
    side, local = me // half, lax.rem(me, half)
    away = 1 - side
    near = electrons // 2
    bf16, f32 = jnp.bfloat16, jnp.float32

    def wait(ref, sem):
        pltpu.make_async_copy(ref, ref, sem).wait()

    def send(src, dst, sent, got, peer):
        pltpu.make_async_remote_copy(
            src_ref=src,
            dst_ref=dst,
            send_sem=sent,
            recv_sem=got,
            device_id={"chol": peer},
            device_id_type=MESH,
        ).start()

    def everyone(to):
        def step(t, carry):
            to(lax.rem(me + t * hop, blocks))
            return carry

        lax.fori_loop(1, blocks, step, 0)

    def row_of(d):
        return lax.rem(d, 2) * pairs + d // 2

    pieces = 4
    span = nchol // pieces
    chol_loads = [
        pltpu.make_async_copy(
            chol_hbm.at[pl.ds(p * span, span)], chol_raw.at[pl.ds(p * span, span)], load_sems.at[p]
        )
        for p in range(pieces)
    ]
    for load in chol_loads:
        load.start()
    walker_load = pltpu.make_async_copy(walkers_hbm, walkers, load_sems.at[pieces])
    rotated_load = pltpu.make_async_copy(rotated_hbm, rotated_raw, load_sems.at[pieces + 1])
    walker_load.start()
    rotated_load.start()

    barrier = pltpu.get_barrier_semaphore()

    def greet(k, carry):
        pl.semaphore_signal(
            barrier, inc=1, device_id={"chol": lax.rem(me + k, blocks)}, device_id_type=MESH
        )
        return carry

    lax.fori_loop(1, blocks, greet, 0)

    order = lax.broadcasted_iota(jnp.int32, (slots, slots), 0)
    place = lax.broadcasted_iota(jnp.int32, (slots, slots), 1)
    chosen = jnp.zeros((slots, slots), f32)
    for p in range(slots):
        entry = slot_row[p]
        target = lax.rem(entry, cap) * blocks + entry // cap
        chosen = jnp.where((place == p) & (order == target), 1.0, chosen)
    all_fields[pair, core] = jnp.dot(
        chosen.astype(bf16), fields[...], preferred_element_type=f32
    ).astype(bf16)

    for p in range(pieces):
        chol_loads[p].wait()
        turned(chol_raw, chol, p * span, span)

    scale = field_scale / math.sqrt(nchol)
    cols = rows * orbitals
    tile = min(1024, cols)
    deep = tile // orbitals

    def operators(m):
        @pl.loop(0, cols // tile)
        def _(n):
            at = pl.ds(pl.multiple_of(n * tile, tile), tile)
            out = jnp.dot(left[:m], chol[:, at], preferred_element_type=f32) * scale
            for i in range(deep):
                op_rows[n * deep + i, :m] = out[:, i * orbitals : (i + 1) * orbitals].astype(bf16)

    def packed(b):
        return jnp.swapaxes(op_rows[:, b * blocks : (b + 1) * blocks], 0, 1)

    def chip_operators(which):
        left[:slots] = all_fields[pair, which]
        operators(slots)
        for c in range(cap):
            op_send[c, :, 0, which] = packed(c)

    def send_chip_operators(which):
        def to(s):
            send(
                op_send.at[:, s, 0, which],
                op_recv.at[:, me, 0, which],
                op_sent.at[cap],
                op_got.at[cap],
                s,
            )

        everyone(to)
        for c in range(cap):
            op_recv[c, me, 0, which] = op_send[c, me, 0, which]

    def other_operators(c, first, count):
        for k in range(count):
            chip = lax.rem(pair + first + k, pairs)
            for q in range(2):
                low = (k * 2 + q) * blocks
                at = pl.ds(pl.multiple_of(c * blocks, blocks), blocks)
                left[low : low + blocks] = all_fields[chip, q, at]
        operators(count * 2 * blocks)

        for k in range(count):
            for q in range(2):
                op_send[c, :, first + k, q] = packed(k * 2 + q)

        def to(s):
            send(
                op_send.at[c, s, pl.ds(first, count)],
                op_recv.at[c, me, pl.ds(first, count)],
                op_sent.at[c],
                op_got.at[c],
                s,
            )

        everyone(to)
        for k in range(count):
            for q in range(2):
                op_recv[c, me, first + k, q] = op_send[c, me, first + k, q]

    partner = pair * 2 + 1 - core
    beside = (line * 2 + 1 - across) * 2 + core

    def line_at(j):
        return lax.rem(line + lines - j, lines)

    own, twin = all_fields.at[pair, core], all_fields.at[pair, 1 - core]
    pl.semaphore_wait(barrier, blocks - 1)
    send(own, own, field_send.at[0], field_core.at[0], partner)
    for j in range(1, lines):
        peer = (lax.rem(line + j, lines) * 2 + across) * 2 + core
        send(own, own, field_send.at[2], field_line.at[j], peer)
    send(own, own, field_send.at[1], field_row.at[0], beside)

    @pl.loop(0, 2)
    def _(t):
        @pl.when(t == 1)
        def _():
            for j in range(1, lines):
                held = all_fields.at[line_at(j) * 2 + across, core]
                wait(held, field_line.at[j])
                send(held, held, field_send.at[1], field_row.at[j], beside)
                send(held, held, field_send.at[0], field_core.at[1], partner)
            wait(twin, field_core.at[0])

        which = lax.rem(core + t, 2)
        chip_operators(which)
        send_chip_operators(which)

    for j in range(lines):
        held = all_fields.at[line_at(j) * 2 + 1 - across, core]
        wait(held, field_row.at[j])
        send(held, held, field_send.at[0], field_core.at[1], partner)
    wait(all_fields.at[pl.ds(0, pairs - 1), 0], field_core.at[1])

    split = pairs // 2

    @pl.loop(0, cap)
    def _(c):
        other_operators(c, 1, split)
        other_operators(c, 1 + split, pairs - 1 - split)

    rotated_load.wait()
    turned(rotated_raw, rotated, 0, nchol)
    walker_load.wait()

    def taylor(c):
        group = 4

        @pl.loop(0, blocks // group)
        def _(g):
            ops, terms, sums = [], [], []
            for u in range(group):
                r = g * group + u
                chip, q = lax.rem(r, pairs), r // pairs
                ops.append(
                    jnp.concatenate(
                        [
                            op_recv[c, o, lax.rem(chip + pairs - o // 2, pairs), q]
                            for o in range(blocks)
                        ],
                        axis=0,
                    )
                )
                entry = jnp.maximum(send_walker[c, chip * 2 + q], 0)
                terms.append(walkers[entry])
                sums.append(terms[u].astype(f32))
            for degree in range(1, degrees + 1):
                for u in range(group):
                    product = lax.dot_general(
                        terms[u], ops[u], (((1,), (1,)), ((), ())), preferred_element_type=f32
                    )
                    terms[u] = (product * (1.0 / degree)).astype(bf16)
                    sums[u] = sums[u] + terms[u].astype(f32)
            for u in range(group):
                r = g * group + u
                nw_full[c, r] = sums[u].astype(bf16)

        for o in range(0, blocks, 16 // elec):
            block = jnp.swapaxes(nw_full[c, :, o * elec : o * elec + 16], 0, 1)
            for e in range(16):
                low = e % elec * orbitals
                nw_send[c, o + e // elec, :, low : low + orbitals] = block[e]

        def to_owner(o):
            send(nw_send.at[c, o], nw_recv.at[c, me], nw_sent.at[c], nw_got.at[c], o)

        everyone(to_owner)
        nw_recv[c, me] = nw_send[c, me]

    def send_walkers(c):
        mine = pl.ds(pl.multiple_of(side * near, near), near)

        def to_slot(d):
            @pl.when(d // half != side)
            def _():
                send(
                    nw_full.at[c, row_of(d), mine],
                    branch.at[c, me, mine],
                    br_sent.at[0],
                    br_got.at[0],
                    d,
                )

            @pl.when(d // half == side)
            def _():
                send(nw_full.at[c, row_of(d)], branch.at[c, me], br_sent.at[0], br_got.at[0], d)

        everyone(to_slot)
        branch[c, me] = nw_full[c, row_of(me)]

    def bias(c):
        rows_in = nw_recv[c].reshape(blocks * blocks, elec * orbitals)
        step = min(256, nchol)

        @pl.loop(0, nchol // step)
        def _(n):
            at = pl.ds(pl.multiple_of(n * step, step), step)
            out = lax.dot_general(
                rows_in, rotated[at, :], (((1,), (1,)), ((), ())), preferred_element_type=f32
            ).reshape(blocks, 2, pairs, step)
            for q in range(2):
                mine = out[:, q].reshape(blocks * pairs, step)
                for h in range(step // 128):
                    part[c, q, n * (step // 128) + h] = mine[:, h * 128 : (h + 1) * 128]

        send(part.at[c, 1 - core], pair_recv.at[c], pair_sent.at[c], pair_got.at[c], partner)

    def reduced(c, chip, h):
        at = pl.ds(chip, blocks, stride=pairs)
        return part[c, core, h, at, :] + pair_recv[c, h, at, :]

    def reduce(c):
        wait(pair_recv.at[c], pair_got.at[c])

        def pick(z, carry):
            for h in range(nchol // 128):
                both = reduced(c, z * 2 + 1 - across, h)
                row_send[c, z, :, h * 128 : (h + 1) * 128] = both.astype(bf16)
            return carry

        lax.fori_loop(0, lines, pick, 0)
        send(row_send.at[c], row_recv.at[c], row_sent.at[c], row_got.at[c], beside)

    def spread(c):
        wait(row_recv.at[c], row_got.at[c])

        def pick(z, carry):
            for h in range(nchol // 128):
                low = h * 128
                both = reduced(c, z * 2 + across, h)
                both = both + row_recv[c, z, :, low : low + 128].astype(f32)
                fb_send[c, z, :, low : low + 128] = both.astype(bf16)
            return carry

        lax.fori_loop(0, lines, pick, 0)

        def step(k, carry):
            z = lax.rem(line + k, lines)
            send(
                fb_send.at[c, z],
                fb_recv.at[c, line],
                fb_sent.at[c],
                fb_got.at[c],
                (z * 2 + across) * 2 + core,
            )
            return carry

        lax.fori_loop(1, lines, step, 0)
        fb_recv[c, line] = fb_send[c, line]

    def finish(c):
        wait(fb_recv.at[c, pl.ds(0, lines - 1)], fb_got.at[c])
        fb_total[c] = lax.fori_loop(
            1,
            lines,
            lambda s, acc: acc + fb_recv[c, s].astype(f32),
            fb_recv[c, 0].astype(f32),
        )

    def forward():
        count = half * blocks
        for c in range(cap):
            block = nw_recv[c, pl.ds(away * half, half)].astype(f32)
            block = block.reshape(count, elec * orbitals)
            for h in range(elec * orbitals // 128):
                fw_wide[h, c * count : (c + 1) * count] = block[:, h * 128 : (h + 1) * 128]

        def gather(t, carry):
            at = pl.ds(row_of(side * half + t), cap * half, stride=blocks)
            for h in range(elec * orbitals // 128):
                fw_send[t, :, h * 128 : (h + 1) * 128] = fw_wide[h, at, :].astype(bf16)
            return carry

        lax.fori_loop(0, half, gather, 0)

        def step(k, carry):
            t = lax.rem(local + k, half)
            send(fw_send.at[t], fw_recv.at[local], fw_sent.at[0], fw_got.at[0], side * half + t)
            return carry

        lax.fori_loop(1, half, step, 0)
        fw_recv[local] = fw_send[local]

    def collect():
        wait(fw_recv.at[pl.ds(0, half - 1)], fw_got.at[0])

        def fold(o, carry):
            block = fw_recv[o].astype(f32)
            for e in range(elec):
                for h in range(halves):
                    low = e * orbitals + h * 128
                    fw_rows[h, pl.ds(o * elec + e, cap * half, stride=near), :] = block[
                        :, low : low + 128
                    ]
            return carry

        lax.fori_loop(0, half, fold, 0)
        wait(branch.at[:, pl.ds(0, half - 1 + half // 2)], br_got.at[0])

        def put(s, carry):
            for c in range(cap):
                at = pl.ds(pl.multiple_of((c * half + s) * near, near), near)
                value = jnp.concatenate([fw_rows[h, at, :] for h in range(halves)], axis=1)
                mine = pl.ds(pl.multiple_of(side * near, near), near)
                branch[c, away * half + s, mine] = value.astype(bf16)
            return carry

        lax.fori_loop(0, half, put, 0)

    wait(op_recv.at[:, pl.ds(0, blocks - 1), 0], op_got.at[cap])
    for c in range(cap):
        wait(op_recv.at[c, pl.ds(0, blocks - 1), pl.ds(1, pairs - 1)], op_got.at[c])
        taylor(c)
    for c in range(cap):
        send_walkers(c)
    for c in range(cap):
        wait(nw_recv.at[c, pl.ds(0, blocks - 1)], nw_got.at[c])
        bias(c)
        if c == cap - 1:
            forward()
        reduce(c)
        spread(c)
    collect()
    for c in range(cap):
        finish(c)

    wait(all_fields.at[:, 0], field_send.at[0])
    wait(all_fields.at[pl.ds(0, lines), 0], field_send.at[1])
    wait(all_fields.at[pl.ds(0, lines - 1), 0], field_send.at[2])
    wait(op_recv.at[:, pl.ds(0, blocks - 1), 0], op_sent.at[cap])
    wait(branch.at[:, pl.ds(0, half - 1 + half // 2)], br_sent.at[0])
    wait(fw_send.at[pl.ds(0, half - 1)], fw_sent.at[0])
    for c in range(cap):
        wait(op_recv.at[c, pl.ds(0, blocks - 1), pl.ds(1, pairs - 1)], op_sent.at[c])
        wait(nw_send.at[c, pl.ds(0, blocks - 1)], nw_sent.at[c])
        wait(pair_recv.at[c], pair_sent.at[c])
        wait(row_send.at[c], row_sent.at[c])
        wait(fb_send.at[c, pl.ds(0, lines - 1)], fb_sent.at[c])


def place_kernel(slot_row, branch, fb_total, new_walkers, force_bias):
    cap = branch.shape[0]

    @pl.loop(0, slot_row.shape[0])
    def _(p):
        entry = slot_row[p]
        c, s = lax.rem(entry, cap), entry // cap
        new_walkers[p] = branch[c, s]
        force_bias[pl.ds(p, 1), :] = fb_total[c, pl.ds(s, 1), :]


def parent_shards(blocks, walkers, fields, chol_vectors, rotated, send_walker, slot_row):
    slots, electrons, orbitals = walkers.shape
    nchol, rows, _ = chol_vectors.shape
    elec = rotated.shape[1]
    cap = send_walker.shape[-1]
    bf16, f32 = jnp.bfloat16, jnp.float32
    pairs, lines, half = blocks // 2, blocks // 4, blocks // 2
    halves, near = orbitals // 128, electrons // 2
    most = max(pairs // 2 * 2 * blocks, slots)
    wide = elec * orbitals
    vmem, smem, anywhere = (
        pl.BlockSpec(memory_space=m) for m in (pltpu.VMEM, pltpu.SMEM, pl.ANY)
    )
    dma = pltpu.SemaphoreType.DMA
    branch, fb_total = pl.pallas_call(
        functools.partial(parent_kernel, (blocks, cap, rows, elec)),
        out_shape=(
            jax.ShapeDtypeStruct((cap, blocks, electrons, orbitals), bf16),
            jax.ShapeDtypeStruct((cap, blocks, nchol), f32),
        ),
        in_specs=[smem, smem, vmem, anywhere, anywhere, anywhere],
        out_specs=(vmem, vmem),
        scratch_shapes=[
            pltpu.VMEM(walkers.shape, bf16),
            pltpu.VMEM(chol_vectors.shape, bf16),
            pltpu.VMEM((nchol, rows * orbitals), bf16),
            pltpu.VMEM(rotated.shape, bf16),
            pltpu.VMEM((nchol, wide), bf16),
            pltpu.VMEM((pairs, 2, slots, nchol), bf16),
            pltpu.VMEM((most, nchol), bf16),
            pltpu.VMEM((rows, most, orbitals), bf16),
            pltpu.VMEM((cap, blocks, pairs, 2, rows, orbitals), bf16),
            pltpu.VMEM((cap, blocks, pairs, 2, rows, orbitals), bf16),
            pltpu.VMEM((cap, blocks, electrons, orbitals), bf16),
            pltpu.VMEM((cap, blocks, blocks, wide), bf16),
            pltpu.VMEM((cap, blocks, blocks, wide), bf16),
            pltpu.VMEM((cap, 2, nchol // 128, blocks * pairs, 128), f32),
            pltpu.VMEM((cap, nchol // 128, blocks * pairs, 128), f32),
            pltpu.VMEM((cap, lines, blocks, nchol), bf16),
            pltpu.VMEM((cap, lines, blocks, nchol), bf16),
            pltpu.VMEM((cap, lines, blocks, nchol), bf16),
            pltpu.VMEM((cap, lines, blocks, nchol), bf16),
            pltpu.VMEM((wide // 128, cap * half * blocks, 128), f32),
            pltpu.VMEM((half, cap * half, wide), bf16),
            pltpu.VMEM((half, cap * half, wide), bf16),
            pltpu.VMEM((halves, cap * half * near, 128), f32),
            dma((6,)),
            dma((3,)),
            dma((2,)),
            dma((lines,)),
            dma((lines,)),
            dma((cap + 1,)),
            dma((cap + 1,)),
            dma((cap,)),
            dma((cap,)),
            dma((1,)),
            dma((1,)),
            dma((cap,)),
            dma((cap,)),
            dma((cap,)),
            dma((cap,)),
            dma((cap,)),
            dma((cap,)),
            dma((1,)),
            dma((1,)),
        ],
        compiler_params=pltpu.CompilerParams(
            collective_id=1, has_side_effects=True, vmem_limit_bytes=60 * 1024 * 1024
        ),
    )(
        jnp.transpose(send_walker, (0, 2, 1)).reshape(cap, blocks),
        slot_row,
        fields,
        walkers,
        chol_vectors,
        rotated,
    )
    return pl.pallas_call(
        place_kernel,
        out_shape=(
            jax.ShapeDtypeStruct(walkers.shape, bf16),
            jax.ShapeDtypeStruct((slots, nchol), f32),
        ),
        in_specs=[smem, vmem, vmem],
        out_specs=(vmem, vmem),
    )(slot_row, branch, fb_total)


def plan(blocks, walkers, fields, chol_vectors, rotated, send_walker, slot_row):
    every_entry = blocks * send_walker.shape[-1] == walkers.shape[0]
    step = parent_shards if every_entry and blocks % 8 == 0 else shards
    return step(blocks, walkers, fields, chol_vectors, rotated, send_walker, slot_row)


def solution(mesh):
    in_specs = (
        P(("grp", "chol"), None, None),
        P(("grp", "chol"), None),
        P(None, "chol", None),
        P(None, "chol", None),
        P(("grp", "chol"), None, None),
        P(("grp", "chol")),
    )
    out_specs = (P(("grp", "chol"), None, None), P(("grp", "chol"), None))
    return jax.shard_map(
        functools.partial(plan, mesh.shape["chol"]),
        mesh=mesh,
        in_specs=in_specs,
        out_specs=out_specs,
        check_vma=False,
    )
```

```python
import functools
import math

import jax
import jax.numpy as jnp
from jax import lax
from jax.experimental import pallas as pl
from jax.experimental.pallas import tpu as pltpu
from jax.sharding import PartitionSpec as P

field_scale = 1.5
chunk_slots = 16
degrees = 5
unfold_depth = 64
MESH = pl.DeviceIdType.MESH


def stride_of(blocks):
    return next(h for h in (7, 5, 3, 1) if math.gcd(h, blocks) == 1)


def unfold(source, scratch, target):
    depth, rows, orbitals = source.shape
    step = scratch.shape[1] // rows

    def body(b, carry):
        first = pl.multiple_of(b * step, step)
        block = source[pl.ds(first, step)].astype(jnp.float32).reshape(step * rows, orbitals)
        for h in range(orbitals // 128):
            scratch[h] = block[:, h * 128 : (h + 1) * 128]
        for r in range(rows):
            for h in range(orbitals // 128):
                low = r * orbitals + h * 128
                target[pl.ds(first, step), low : low + 128] = scratch[
                    h, pl.ds(r, step, stride=rows), :
                ].astype(jnp.bfloat16)
        return carry

    lax.fori_loop(0, depth // step, body, 0)


def exchange(me, blocks, send, recv, chunk, send_sem, recv_sem, place=lambda d: d, land=lambda d: d):
    hop = stride_of(blocks)

    def step(k, carry):
        peer = lax.rem(me + k * hop, blocks)
        pltpu.make_async_remote_copy(
            src_ref=send.at[chunk, place(peer)],
            dst_ref=recv.at[chunk, land(me)],
            send_sem=send_sem.at[chunk],
            recv_sem=recv_sem.at[chunk],
            device_id={"chol": peer},
            device_id_type=MESH,
        ).start()
        return carry

    lax.fori_loop(1, blocks, step, 0)
    recv[chunk, land(me)] = send[chunk, place(me)]


def arrived(blocks, recv, chunk, sem):
    whole = recv.at[chunk, pl.ds(0, blocks - 1)]
    pltpu.make_async_copy(whole, whole, sem.at[chunk]).wait()


def kernel(
    dims,
    send_walker,
    slot_row,
    walkers,
    fields,
    chol_hbm,
    rotated_raw,
    new_walkers,
    force_bias,
    chol_raw,
    chol_wide,
    chol,
    rotated_wide,
    rotated,
    all_fields,
    br_send,
    br_recv,
    op_send,
    op_recv,
    op_rows,
    totals,
    nw_send,
    nw_recv,
    pair_send,
    pair_recv,
    pair_own,
    fb_send,
    fb_recv,
    send_sems,
    recv_sems,
    field_sems,
    load_sem,
    op_sems,
):
    blocks, chunks, width, cap, rows, elec = dims
    slots, electrons, orbitals = walkers.shape
    nchol = rotated.shape[0]
    halves = orbitals // 128
    me = lax.axis_index("chol")
    pairs = blocks // 2
    core, pair = lax.rem(me, 2), me // 2
    groups = math.gcd(4, blocks)
    share_of = blocks // groups
    hop = stride_of(blocks)
    load = pltpu.make_async_copy(chol_hbm, chol_raw, load_sem)
    load.start()

    barrier = pltpu.get_barrier_semaphore()

    def greet(k, carry):
        pl.semaphore_signal(
            barrier, inc=1, device_id={"chol": lax.rem(me + k, blocks)}, device_id_type=MESH
        )
        return carry

    lax.fori_loop(1, blocks, greet, 0)

    def pick(d, carry):
        for c in range(cap):
            br_send[0, d, c] = walkers[jnp.maximum(send_walker[d * cap + c], 0)]
        return carry

    lax.fori_loop(0, blocks, pick, 0)
    pl.semaphore_wait(barrier, blocks - 1)

    def share(k, carry):
        pltpu.make_async_remote_copy(
            src_ref=fields,
            dst_ref=all_fields.at[core, pair],
            send_sem=field_sems.at[0],
            recv_sem=field_sems.at[1],
            device_id={"chol": lax.rem(pair + k, pairs) * 2 + core},
            device_id_type=MESH,
        ).start()
        return carry

    lax.fori_loop(1, pairs, share, 0)
    all_fields[core, pair] = fields[...]
    load.wait()
    unfold(chol_raw, chol_wide, chol)
    same_core = all_fields.at[core, pl.ds(0, pairs - 1)]
    pltpu.make_async_copy(same_core, same_core, field_sems.at[1]).wait()
    across = pltpu.make_async_remote_copy(
        src_ref=all_fields.at[core],
        dst_ref=all_fields.at[core],
        send_sem=field_sems.at[2],
        recv_sem=field_sems.at[3],
        device_id={"chol": pair * 2 + 1 - core},
        device_id_type=MESH,
    )
    across.start()
    exchange(me, blocks, br_send, br_recv, 0, send_sems.at[0], recv_sems.at[0])

    across.wait_recv()
    scale = field_scale / math.sqrt(nchol)
    cols = rows * orbitals
    tile = min(512, cols)

    @pl.loop(0, cols // tile)
    def _(n):
        at = pl.ds(pl.multiple_of(n * tile, tile), tile)
        left = all_fields[...].reshape(blocks * slots, nchol)
        part = jnp.dot(left, chol[:, at], preferred_element_type=jnp.float32) * scale
        part = part.astype(jnp.bfloat16).reshape(blocks, chunks, width, tile)
        for q in range(chunks):
            op_send[q, :, :, at] = part[:, q]

    def send_operators(q):
        for group in range(groups):
            def step(k, carry):
                peer = lax.rem(me + k * hop, blocks)
                pltpu.make_async_remote_copy(
                    src_ref=op_send.at[q, place(peer)],
                    dst_ref=op_recv.at[q, me],
                    send_sem=send_sems.at[1, q],
                    recv_sem=op_sems.at[q, group],
                    device_id={"chol": peer},
                    device_id_type=MESH,
                ).start()
                return carry

            lax.fori_loop(max(1, group * share_of), (group + 1) * share_of, step, 0)
        op_recv[q, me] = op_send[q, place(me)]

    def place(d):
        return lax.rem(d, 2) * pairs + d // 2

    def taylor(q):
        def spread(k, carry):
            s = lax.rem(me + (blocks - k) * hop, blocks)
            block = op_recv[q, s].astype(jnp.float32)
            for r in range(rows):
                for h in range(halves):
                    low = r * orbitals + h * 128
                    op_rows[h, pl.ds(s * rows + r, width, stride=orbitals), :] = block[
                        :, low : low + 128
                    ]
            return carry

        for group in range(groups):
            count = share_of - 1 if group == 0 else share_of
            whole = op_recv.at[q, pl.ds(0, count)]
            pltpu.make_async_copy(whole, whole, op_sems.at[q, group]).wait()
            lax.fori_loop(group * share_of, (group + 1) * share_of, spread, 0)
        group = 4

        @pl.loop(0, width // group)
        def _(g):
            ops, terms, sums = [], [], []
            for u in range(group):
                w = g * group + u
                first = pl.ds(pl.multiple_of(w * orbitals, orbitals), orbitals)
                ops.append(
                    jnp.concatenate([op_rows[h, first, :] for h in range(halves)], axis=1).astype(
                        jnp.bfloat16
                    )
                )
                row = slot_row[q * width + w]
                terms.append(br_recv[0, row // cap, row % cap])
                sums.append(terms[u].astype(jnp.float32))
            for degree in range(1, degrees + 1):
                for u in range(group):
                    product = lax.dot_general(
                        terms[u],
                        ops[u],
                        (((1,), (1,)), ((), ())),
                        preferred_element_type=jnp.float32,
                    )
                    terms[u] = (product * (1.0 / degree)).astype(jnp.bfloat16)
                    sums[u] = sums[u] + terms[u].astype(jnp.float32)
            for u in range(group):
                w = g * group + u
                new_walkers[q * width + w] = sums[u].astype(jnp.bfloat16)
                place = pl.ds(pl.multiple_of(w * electrons, electrons), electrons)
                for h in range(halves):
                    totals[h, place, :] = sums[u][:, h * 128 : (h + 1) * 128]

        def turn(d, carry):
            for e in range(elec):
                for h in range(halves):
                    low = e * orbitals + h * 128
                    nw_send[q, d, :, low : low + 128] = totals[
                        h, pl.ds(d * elec + e, width, stride=electrons), :
                    ].astype(jnp.bfloat16)
            return carry

        lax.fori_loop(0, blocks, turn, 0)
        exchange(me, blocks, nw_send, nw_recv, q, send_sems.at[2], recv_sems.at[2], land=place)

    def partial(q, half, target):
        left = nw_recv[q, pl.ds(half * pairs, pairs)].reshape(pairs * width, elec * orbitals)
        step = min(256, nchol)

        @pl.loop(0, nchol // step)
        def _(n):
            at = pl.ds(pl.multiple_of(n * step, step), step)
            target[:, at] = lax.dot_general(
                left, rotated[at, :], (((1,), (1,)), ((), ())), preferred_element_type=jnp.float32
            )

    def bias(q):
        partial(q, 1 - core, pair_send.at[q])
        across = pltpu.make_async_remote_copy(
            src_ref=pair_send.at[q],
            dst_ref=pair_recv.at[q],
            send_sem=send_sems.at[4, q],
            recv_sem=recv_sems.at[4, q],
            device_id={"chol": pair * 2 + 1 - core},
            device_id_type=MESH,
        )
        across.start()
        partial(q, core, pair_own)
        across.wait_recv()
        both = (pair_own[...] + pair_recv[q]).astype(jnp.bfloat16)
        fb_send[q] = both.reshape(pairs, width, nchol)

        def step(k, carry):
            peer = lax.rem(pair + k, pairs)
            pltpu.make_async_remote_copy(
                src_ref=fb_send.at[q, peer],
                dst_ref=fb_recv.at[q, pair],
                send_sem=send_sems.at[3, q],
                recv_sem=recv_sems.at[3, q],
                device_id={"chol": peer * 2 + core},
                device_id_type=MESH,
            ).start()
            return carry

        lax.fori_loop(1, pairs, step, 0)
        fb_recv[q, pair] = fb_send[q, pair]

    def finish(q):
        force_bias[q * width : (q + 1) * width, :] = lax.fori_loop(
            1,
            pairs,
            lambda s, acc: acc + fb_recv[q, s].astype(jnp.float32),
            fb_recv[q, 0].astype(jnp.float32),
        )

    for q in range(min(2, chunks)):
        send_operators(q)
    unfold(rotated_raw, rotated_wide, rotated)
    arrived(blocks, br_recv, 0, recv_sems.at[0])
    for q in range(chunks + 2):
        if q < chunks:
            if q + 2 < chunks:
                send_operators(q + 2)
            taylor(q)
        if 1 <= q <= chunks:
            arrived(blocks, nw_recv, q - 1, recv_sems.at[2])
            bias(q - 1)
        if q >= 2:
            arrived(pairs, fb_recv, q - 2, recv_sems.at[3])
            finish(q - 2)
    arrived(blocks, br_send, 0, send_sems.at[0])
    across.wait_send()
    pltpu.make_async_copy(same_core, same_core, field_sems.at[0]).wait()
    for q in range(chunks):
        arrived(blocks, op_send, q, send_sems.at[1])
        arrived(blocks, nw_send, q, send_sems.at[2])
        arrived(pairs, fb_send, q, send_sems.at[3])
        pltpu.make_async_copy(pair_send.at[q], pair_send.at[q], send_sems.at[4, q]).wait()


def shards(blocks, walkers, fields, chol_vectors, rotated, send_walker, slot_row):
    slots, electrons, orbitals = walkers.shape
    nchol, rows, _ = chol_vectors.shape
    elec = rotated.shape[1]
    cap = send_walker.shape[-1]
    width = min(chunk_slots, slots)
    chunks = slots // width
    dims = (blocks, chunks, width, cap, rows, elec)
    bf16, f32 = jnp.bfloat16, jnp.float32
    vmem, smem = (pl.BlockSpec(memory_space=m) for m in (pltpu.VMEM, pltpu.SMEM))
    return pl.pallas_call(
        functools.partial(kernel, dims),
        out_shape=(
            jax.ShapeDtypeStruct(walkers.shape, bf16),
            jax.ShapeDtypeStruct((slots, nchol), f32),
        ),
        in_specs=[smem, smem, vmem, vmem, pl.BlockSpec(memory_space=pl.ANY), vmem],
        out_specs=(vmem, vmem),
        scratch_shapes=[
            pltpu.VMEM(chol_vectors.shape, bf16),
            pltpu.VMEM((orbitals // 128, rows * unfold_depth, 128), f32),
            pltpu.VMEM((nchol, rows * orbitals), bf16),
            pltpu.VMEM((orbitals // 128, elec * unfold_depth, 128), f32),
            pltpu.VMEM((nchol, elec * orbitals), bf16),
            pltpu.VMEM((2, blocks // 2, slots, nchol), bf16),
            pltpu.VMEM((1, blocks, cap, electrons, orbitals), bf16),
            pltpu.VMEM((1, blocks, cap, electrons, orbitals), bf16),
            pltpu.VMEM((chunks, blocks, width, rows * orbitals), bf16),
            pltpu.VMEM((chunks, blocks, width, rows * orbitals), bf16),
            pltpu.VMEM((orbitals // 128, width * orbitals, 128), f32),
            pltpu.VMEM((orbitals // 128, width * electrons, 128), f32),
            pltpu.VMEM((chunks, blocks, width, elec * orbitals), bf16),
            pltpu.VMEM((chunks, blocks, width, elec * orbitals), bf16),
            pltpu.VMEM((chunks, blocks // 2 * width, nchol), f32),
            pltpu.VMEM((chunks, blocks // 2 * width, nchol), f32),
            pltpu.VMEM((blocks // 2 * width, nchol), f32),
            pltpu.VMEM((chunks, blocks // 2, width, nchol), bf16),
            pltpu.VMEM((chunks, blocks // 2, width, nchol), bf16),
            pltpu.SemaphoreType.DMA((5, chunks)),
            pltpu.SemaphoreType.DMA((5, chunks)),
            pltpu.SemaphoreType.DMA((4,)),
            pltpu.SemaphoreType.DMA,
            pltpu.SemaphoreType.DMA((chunks, math.gcd(4, blocks))),
        ],
        compiler_params=pltpu.CompilerParams(
            collective_id=0, has_side_effects=True, vmem_limit_bytes=60 * 1024 * 1024
        ),
    )(
        send_walker.reshape(-1),
        slot_row,
        walkers,
        fields,
        chol_vectors,
        rotated,
    )


def turned(source, target, start, count):
    rows, orbitals = source.shape[1:]
    step = 16

    def body(b, carry):
        first = pl.multiple_of(start + b * step, step)
        block = jnp.swapaxes(source[pl.ds(first, step)], 0, 1)
        for r in range(rows):
            target[pl.ds(first, step), r * orbitals : (r + 1) * orbitals] = block[r]
        return carry

    lax.fori_loop(0, count // step, body, 0)


def parent_kernel(
    dims,
    send_walker,
    slot_row,
    fields,
    walkers_hbm,
    chol_hbm,
    rotated_hbm,
    branch,
    fb_total,
    walkers,
    chol_raw,
    chol,
    rotated_raw,
    rotated,
    all_fields,
    left,
    op_rows,
    op_send,
    op_recv,
    nw_full,
    nw_send,
    nw_recv,
    part,
    pair_recv,
    row_send,
    row_recv,
    fb_send,
    fb_recv,
    fw_wide,
    fw_send,
    fw_recv,
    fw_rows,
    load_sems,
    field_send,
    field_core,
    field_line,
    field_row,
    op_sent,
    op_got,
    nw_sent,
    nw_got,
    br_sent,
    br_got,
    pair_sent,
    pair_got,
    row_sent,
    row_got,
    fb_sent,
    fb_got,
    fw_sent,
    fw_got,
):
    blocks, cap, rows, elec = dims
    slots, nchol = fields.shape
    electrons, orbitals = walkers.shape[1:]
    halves = orbitals // 128
    me = lax.axis_index("chol")
    pairs, lines, half = blocks // 2, blocks // 4, blocks // 2
    hop = stride_of(blocks)
    core, pair = lax.rem(me, 2), me // 2
    line, across = pair // 2, lax.rem(pair, 2)
    side, local = me // half, lax.rem(me, half)
    away = 1 - side
    near = electrons // 2
    bf16, f32 = jnp.bfloat16, jnp.float32

    def wait(ref, sem):
        pltpu.make_async_copy(ref, ref, sem).wait()

    def send(src, dst, sent, got, peer):
        pltpu.make_async_remote_copy(
            src_ref=src,
            dst_ref=dst,
            send_sem=sent,
            recv_sem=got,
            device_id={"chol": peer},
            device_id_type=MESH,
        ).start()

    def everyone(to):
        def step(t, carry):
            to(lax.rem(me + t * hop, blocks))
            return carry

        lax.fori_loop(1, blocks, step, 0)

    def chip_at(k):
        beyond = across if k < lines else 1 - across
        return lax.rem(line + k % lines, lines) * 2 + beyond

    def steps_from(o, chip):
        z, y = chip // 2, lax.rem(chip, 2)
        apart = y if o // 2 % 2 == 0 else 1 - y
        return lax.rem(z + lines - o // 4, lines) + apart * lines

    def row_of(d):
        return lax.rem(d, 2) * pairs + d // 2

    pieces = 4
    span = nchol // pieces
    chol_loads = [
        pltpu.make_async_copy(
            chol_hbm.at[pl.ds(p * span, span)], chol_raw.at[pl.ds(p * span, span)], load_sems.at[p]
        )
        for p in range(pieces)
    ]
    for load in chol_loads:
        load.start()
    walker_load = pltpu.make_async_copy(walkers_hbm, walkers, load_sems.at[pieces])
    rotated_load = pltpu.make_async_copy(rotated_hbm, rotated_raw, load_sems.at[pieces + 1])
    walker_load.start()
    rotated_load.start()

    barrier = pltpu.get_barrier_semaphore()

    def greet(k, carry):
        pl.semaphore_signal(
            barrier, inc=1, device_id={"chol": lax.rem(me + k, blocks)}, device_id_type=MESH
        )
        return carry

    lax.fori_loop(1, blocks, greet, 0)

    order = lax.broadcasted_iota(jnp.int32, (slots, slots), 0)
    place = lax.broadcasted_iota(jnp.int32, (slots, slots), 1)
    chosen = jnp.zeros((slots, slots), f32)
    for p in range(slots):
        entry = slot_row[p]
        target = lax.rem(entry, cap) * blocks + entry // cap
        chosen = jnp.where((place == p) & (order == target), 1.0, chosen)
    all_fields[pair, core] = jnp.dot(
        chosen.astype(bf16), fields[...], preferred_element_type=f32
    ).astype(bf16)

    for p in range(pieces):
        chol_loads[p].wait()
        turned(chol_raw, chol, p * span, span)

    scale = field_scale / math.sqrt(nchol)
    cols = rows * orbitals
    tile = min(1024, cols)
    deep = tile // orbitals

    def operators(m):
        @pl.loop(0, cols // tile)
        def _(n):
            at = pl.ds(pl.multiple_of(n * tile, tile), tile)
            out = jnp.dot(left[:m], chol[:, at], preferred_element_type=f32) * scale
            for i in range(deep):
                op_rows[n * deep + i, :m] = out[:, i * orbitals : (i + 1) * orbitals].astype(bf16)

    def packed(b):
        return jnp.swapaxes(op_rows[:, b * blocks : (b + 1) * blocks], 0, 1)

    def chip_operators(which):
        left[:slots] = all_fields[pair, which]
        operators(slots)
        for c in range(cap):
            op_send[c, :, 0, which] = packed(c)

    def send_chip_operators(which):
        def to(s):
            send(
                op_send.at[:, s, 0, which],
                op_recv.at[:, me, 0, which],
                op_sent.at[cap],
                op_got.at[cap],
                s,
            )

        everyone(to)
        for c in range(cap):
            op_recv[c, me, 0, which] = op_send[c, me, 0, which]

    def other_operators(c, first, count):
        for k in range(count):
            chip = chip_at(first + k)
            for q in range(2):
                low = (k * 2 + q) * blocks
                at = pl.ds(pl.multiple_of(c * blocks, blocks), blocks)
                left[low : low + blocks] = all_fields[chip, q, at]
        operators(count * 2 * blocks)

        for k in range(count):
            for q in range(2):
                op_send[c, :, first + k, q] = packed(k * 2 + q)

        def to(s):
            send(
                op_send.at[c, s, pl.ds(first, count)],
                op_recv.at[c, me, pl.ds(first, count)],
                op_sent.at[c],
                op_got.at[c],
                s,
            )

        everyone(to)
        for k in range(count):
            for q in range(2):
                op_recv[c, me, first + k, q] = op_send[c, me, first + k, q]

    partner = pair * 2 + 1 - core
    beside = (line * 2 + 1 - across) * 2 + core

    bank = lines // 2
    low_bank = line < bank
    outer = jnp.where(low_bank, line < bank - 1, line > bank)
    rank = jnp.where(outer, 1, 0)
    other_line = jnp.where(low_bank, bank - 1 - line, lines + bank - 1 - line)
    far_inner = jnp.where(low_bank, bank, bank - 1)
    far_outer = jnp.where(low_bank, lines - 1, 0)
    held_lines = (line, other_line, far_inner, far_outer)

    def line_at(j):
        return held_lines[j]

    def along(z):
        return (z * 2 + across) * 2 + core

    own, twin = all_fields.at[pair, core], all_fields.at[pair, 1 - core]
    pl.semaphore_wait(barrier, blocks - 1)
    send(own, own, field_send.at[0], field_core.at[0], partner)
    send(own, own, field_send.at[2], field_line.at[2 + rank], along(far_inner))
    send(own, own, field_send.at[2], field_line.at[1], along(other_line))
    send(own, own, field_send.at[1], field_row.at[0], beside)

    def hand_on(held, j):
        @pl.when(rank == 0)
        def _():
            send(held, held, field_send.at[2], field_line.at[j], along(other_line))

    @pl.loop(0, 2)
    def _(t):
        @pl.when(t == 1)
        def _():
            for j in range(1, lines):
                held = all_fields.at[line_at(j) * 2 + across, core]
                wait(held, field_line.at[j])
                if j > 1:
                    hand_on(held, j)
                send(held, held, field_send.at[1], field_row.at[j], beside)
                send(held, held, field_send.at[0], field_core.at[1], partner)
            wait(twin, field_core.at[0])

        which = lax.rem(core + t, 2)
        chip_operators(which)
        send_chip_operators(which)

    wait(all_fields.at[pl.ds(0, lines - 1), 0], field_core.at[1])

    @pl.loop(0, cap)
    def _(c):
        other_operators(c, 1, lines - 1)

        @pl.when(c == 0)
        def _():
            for j in range(lines):
                held = all_fields.at[line_at(j) * 2 + 1 - across, core]
                wait(held, field_row.at[j])
                send(held, held, field_send.at[0], field_core.at[2], partner)
            wait(all_fields.at[pl.ds(0, lines), 0], field_core.at[2])

        other_operators(c, lines, lines)

    rotated_load.wait()
    turned(rotated_raw, rotated, 0, nchol)
    walker_load.wait()

    def taylor(c):
        group = 4

        @pl.loop(0, blocks // group)
        def _(g):
            ops, terms, sums = [], [], []
            for u in range(group):
                r = g * group + u
                chip, q = lax.rem(r, pairs), r // pairs
                ops.append(
                    jnp.concatenate(
                        [
                            op_recv[c, o, steps_from(o, chip), q]
                            for o in range(blocks)
                        ],
                        axis=0,
                    )
                )
                entry = jnp.maximum(send_walker[c, chip * 2 + q], 0)
                terms.append(walkers[entry])
                sums.append(terms[u].astype(f32))
            for degree in range(1, degrees + 1):
                for u in range(group):
                    product = lax.dot_general(
                        terms[u], ops[u], (((1,), (1,)), ((), ())), preferred_element_type=f32
                    )
                    terms[u] = (product * (1.0 / degree)).astype(bf16)
                    sums[u] = sums[u] + terms[u].astype(f32)
            for u in range(group):
                r = g * group + u
                nw_full[c, r] = sums[u].astype(bf16)

        for o in range(0, blocks, 16 // elec):
            block = jnp.swapaxes(nw_full[c, :, o * elec : o * elec + 16], 0, 1)
            for e in range(16):
                low = e % elec * orbitals
                nw_send[c, o + e // elec, :, low : low + orbitals] = block[e]

        def to_owner(o):
            send(nw_send.at[c, o], nw_recv.at[c, me], nw_sent.at[c], nw_got.at[c], o)

        everyone(to_owner)
        nw_recv[c, me] = nw_send[c, me]

    def send_walkers(c):
        mine = pl.ds(pl.multiple_of(side * near, near), near)

        def to_slot(d):
            @pl.when(d // half != side)
            def _():
                send(
                    nw_full.at[c, row_of(d), mine],
                    branch.at[c, me, mine],
                    br_sent.at[0],
                    br_got.at[0],
                    d,
                )

            @pl.when(d // half == side)
            def _():
                send(nw_full.at[c, row_of(d)], branch.at[c, me], br_sent.at[0], br_got.at[0], d)

        everyone(to_slot)
        branch[c, me] = nw_full[c, row_of(me)]

    def bias(c):
        rows_in = nw_recv[c].reshape(blocks * blocks, elec * orbitals)
        step = min(256, nchol)

        @pl.loop(0, nchol // step)
        def _(n):
            at = pl.ds(pl.multiple_of(n * step, step), step)
            out = lax.dot_general(
                rows_in, rotated[at, :], (((1,), (1,)), ((), ())), preferred_element_type=f32
            ).reshape(blocks, 2, pairs, step)
            for q in range(2):
                mine = out[:, q].reshape(blocks * pairs, step)
                for h in range(step // 128):
                    part[c, q, n * (step // 128) + h] = mine[:, h * 128 : (h + 1) * 128]

        send(part.at[c, 1 - core], pair_recv.at[c], pair_sent.at[c], pair_got.at[c], partner)

    def reduced(c, chip, h):
        at = pl.ds(chip, blocks, stride=pairs)
        return part[c, core, h, at, :] + pair_recv[c, h, at, :]

    def reduce(c):
        wait(pair_recv.at[c], pair_got.at[c])

        def pick(z, carry):
            for h in range(nchol // 128):
                both = reduced(c, z * 2 + 1 - across, h)
                row_send[c, z, :, h * 128 : (h + 1) * 128] = both.astype(bf16)
            return carry

        lax.fori_loop(0, lines, pick, 0)
        send(row_send.at[c], row_recv.at[c], row_sent.at[c], row_got.at[c], beside)

    def spread(c):
        wait(row_recv.at[c], row_got.at[c])

        def pick(z, carry):
            for h in range(nchol // 128):
                low = h * 128
                both = reduced(c, z * 2 + across, h)
                both = both + row_recv[c, z, :, low : low + 128].astype(f32)
                fb_send[c, z, :, low : low + 128] = both.astype(bf16)
            return carry

        lax.fori_loop(0, lines, pick, 0)

        def step(k, carry):
            z = lax.rem(line + k, lines)
            send(
                fb_send.at[c, z],
                fb_recv.at[c, line],
                fb_sent.at[c],
                fb_got.at[c],
                (z * 2 + across) * 2 + core,
            )
            return carry

        lax.fori_loop(1, lines, step, 0)
        fb_recv[c, line] = fb_send[c, line]

    def finish(c):
        wait(fb_recv.at[c, pl.ds(0, lines - 1)], fb_got.at[c])
        fb_total[c] = lax.fori_loop(
            1,
            lines,
            lambda s, acc: acc + fb_recv[c, s].astype(f32),
            fb_recv[c, 0].astype(f32),
        )

    def forward():
        count = half * blocks
        for c in range(cap):
            block = nw_recv[c, pl.ds(away * half, half)].astype(f32)
            block = block.reshape(count, elec * orbitals)
            for h in range(elec * orbitals // 128):
                fw_wide[h, c * count : (c + 1) * count] = block[:, h * 128 : (h + 1) * 128]

        def gather(t, carry):
            at = pl.ds(row_of(side * half + t), cap * half, stride=blocks)
            for h in range(elec * orbitals // 128):
                fw_send[t, :, h * 128 : (h + 1) * 128] = fw_wide[h, at, :].astype(bf16)
            return carry

        lax.fori_loop(0, half, gather, 0)

        def step(k, carry):
            t = lax.rem(local + k, half)
            send(fw_send.at[t], fw_recv.at[local], fw_sent.at[0], fw_got.at[0], side * half + t)
            return carry

        lax.fori_loop(1, half, step, 0)
        fw_recv[local] = fw_send[local]

    def collect():
        wait(fw_recv.at[pl.ds(0, half - 1)], fw_got.at[0])

        def fold(o, carry):
            block = fw_recv[o].astype(f32)
            for e in range(elec):
                for h in range(halves):
                    low = e * orbitals + h * 128
                    fw_rows[h, pl.ds(o * elec + e, cap * half, stride=near), :] = block[
                        :, low : low + 128
                    ]
            return carry

        lax.fori_loop(0, half, fold, 0)
        wait(branch.at[:, pl.ds(0, half - 1 + half // 2)], br_got.at[0])

        def put(s, carry):
            for c in range(cap):
                at = pl.ds(pl.multiple_of((c * half + s) * near, near), near)
                value = jnp.concatenate([fw_rows[h, at, :] for h in range(halves)], axis=1)
                mine = pl.ds(pl.multiple_of(side * near, near), near)
                branch[c, away * half + s, mine] = value.astype(bf16)
            return carry

        lax.fori_loop(0, half, put, 0)

    wait(op_recv.at[:, pl.ds(0, blocks - 1), 0], op_got.at[cap])
    for c in range(cap):
        wait(op_recv.at[c, pl.ds(0, blocks - 1), pl.ds(1, pairs - 1)], op_got.at[c])
        taylor(c)
    for c in range(cap):
        send_walkers(c)
    for c in range(cap):
        wait(nw_recv.at[c, pl.ds(0, blocks - 1)], nw_got.at[c])
        bias(c)
        if c == cap - 1:
            forward()
        reduce(c)
        spread(c)
    collect()
    for c in range(cap):
        finish(c)

    wait(all_fields.at[:, 0], field_send.at[0])
    wait(all_fields.at[pl.ds(0, lines), 0], field_send.at[1])

    @pl.when(rank == 0)
    def _():
        wait(all_fields.at[pl.ds(0, 4), 0], field_send.at[2])

    @pl.when(rank == 1)
    def _():
        wait(all_fields.at[pl.ds(0, 2), 0], field_send.at[2])

    wait(op_recv.at[:, pl.ds(0, blocks - 1), 0], op_sent.at[cap])
    wait(branch.at[:, pl.ds(0, half - 1 + half // 2)], br_sent.at[0])
    wait(fw_send.at[pl.ds(0, half - 1)], fw_sent.at[0])
    for c in range(cap):
        wait(op_recv.at[c, pl.ds(0, blocks - 1), pl.ds(1, pairs - 1)], op_sent.at[c])
        wait(nw_send.at[c, pl.ds(0, blocks - 1)], nw_sent.at[c])
        wait(pair_recv.at[c], pair_sent.at[c])
        wait(row_send.at[c], row_sent.at[c])
        wait(fb_send.at[c, pl.ds(0, lines - 1)], fb_sent.at[c])


def place_kernel(slot_row, branch, fb_total, new_walkers, force_bias):
    cap = branch.shape[0]

    @pl.loop(0, slot_row.shape[0])
    def _(p):
        entry = slot_row[p]
        c, s = lax.rem(entry, cap), entry // cap
        new_walkers[p] = branch[c, s]
        force_bias[pl.ds(p, 1), :] = fb_total[c, pl.ds(s, 1), :]


def parent_shards(blocks, walkers, fields, chol_vectors, rotated, send_walker, slot_row):
    slots, electrons, orbitals = walkers.shape
    nchol, rows, _ = chol_vectors.shape
    elec = rotated.shape[1]
    cap = send_walker.shape[-1]
    bf16, f32 = jnp.bfloat16, jnp.float32
    pairs, lines, half = blocks // 2, blocks // 4, blocks // 2
    halves, near = orbitals // 128, electrons // 2
    most = max(pairs // 2 * 2 * blocks, slots)
    wide = elec * orbitals
    vmem, smem, anywhere = (
        pl.BlockSpec(memory_space=m) for m in (pltpu.VMEM, pltpu.SMEM, pl.ANY)
    )
    dma = pltpu.SemaphoreType.DMA
    branch, fb_total = pl.pallas_call(
        functools.partial(parent_kernel, (blocks, cap, rows, elec)),
        out_shape=(
            jax.ShapeDtypeStruct((cap, blocks, electrons, orbitals), bf16),
            jax.ShapeDtypeStruct((cap, blocks, nchol), f32),
        ),
        in_specs=[smem, smem, vmem, anywhere, anywhere, anywhere],
        out_specs=(vmem, vmem),
        scratch_shapes=[
            pltpu.VMEM(walkers.shape, bf16),
            pltpu.VMEM(chol_vectors.shape, bf16),
            pltpu.VMEM((nchol, rows * orbitals), bf16),
            pltpu.VMEM(rotated.shape, bf16),
            pltpu.VMEM((nchol, wide), bf16),
            pltpu.VMEM((pairs, 2, slots, nchol), bf16),
            pltpu.VMEM((most, nchol), bf16),
            pltpu.VMEM((rows, most, orbitals), bf16),
            pltpu.VMEM((cap, blocks, pairs, 2, rows, orbitals), bf16),
            pltpu.VMEM((cap, blocks, pairs, 2, rows, orbitals), bf16),
            pltpu.VMEM((cap, blocks, electrons, orbitals), bf16),
            pltpu.VMEM((cap, blocks, blocks, wide), bf16),
            pltpu.VMEM((cap, blocks, blocks, wide), bf16),
            pltpu.VMEM((cap, 2, nchol // 128, blocks * pairs, 128), f32),
            pltpu.VMEM((cap, nchol // 128, blocks * pairs, 128), f32),
            pltpu.VMEM((cap, lines, blocks, nchol), bf16),
            pltpu.VMEM((cap, lines, blocks, nchol), bf16),
            pltpu.VMEM((cap, lines, blocks, nchol), bf16),
            pltpu.VMEM((cap, lines, blocks, nchol), bf16),
            pltpu.VMEM((wide // 128, cap * half * blocks, 128), f32),
            pltpu.VMEM((half, cap * half, wide), bf16),
            pltpu.VMEM((half, cap * half, wide), bf16),
            pltpu.VMEM((halves, cap * half * near, 128), f32),
            dma((6,)),
            dma((3,)),
            dma((3,)),
            dma((lines,)),
            dma((lines,)),
            dma((cap + 1,)),
            dma((cap + 1,)),
            dma((cap,)),
            dma((cap,)),
            dma((1,)),
            dma((1,)),
            dma((cap,)),
            dma((cap,)),
            dma((cap,)),
            dma((cap,)),
            dma((cap,)),
            dma((cap,)),
            dma((1,)),
            dma((1,)),
        ],
        compiler_params=pltpu.CompilerParams(
            collective_id=1, has_side_effects=True, vmem_limit_bytes=60 * 1024 * 1024
        ),
    )(
        jnp.transpose(send_walker, (0, 2, 1)).reshape(cap, blocks),
        slot_row,
        fields,
        walkers,
        chol_vectors,
        rotated,
    )
    return pl.pallas_call(
        place_kernel,
        out_shape=(
            jax.ShapeDtypeStruct(walkers.shape, bf16),
            jax.ShapeDtypeStruct((slots, nchol), f32),
        ),
        in_specs=[smem, vmem, vmem],
        out_specs=(vmem, vmem),
    )(slot_row, branch, fb_total)


def plan(blocks, walkers, fields, chol_vectors, rotated, send_walker, slot_row):
    every_entry = blocks * send_walker.shape[-1] == walkers.shape[0]
    step = parent_shards if every_entry and blocks == 4 * 2 * 2 else shards
    return step(blocks, walkers, fields, chol_vectors, rotated, send_walker, slot_row)


def solution(mesh):
    in_specs = (
        P(("grp", "chol"), None, None),
        P(("grp", "chol"), None),
        P(None, "chol", None),
        P(None, "chol", None),
        P(("grp", "chol"), None, None),
        P(("grp", "chol")),
    )
    out_specs = (P(("grp", "chol"), None, None), P(("grp", "chol"), None))
    return jax.shard_map(
        functools.partial(plan, mesh.shape["chol"]),
        mesh=mesh,
        in_specs=in_specs,
        out_specs=out_specs,
        check_vma=False,
    )
```

```python
import functools
import math

import jax
import jax.numpy as jnp
from jax import lax
from jax.experimental import pallas as pl
from jax.experimental.pallas import tpu as pltpu
from jax.sharding import PartitionSpec as P

field_scale = 1.5
chunk_slots = 16
degrees = 5
unfold_depth = 64
MESH = pl.DeviceIdType.MESH


def stride_of(blocks):
    return next(h for h in (7, 5, 3, 1) if math.gcd(h, blocks) == 1)


def unfold(source, scratch, target):
    depth, rows, orbitals = source.shape
    step = scratch.shape[1] // rows

    def body(b, carry):
        first = pl.multiple_of(b * step, step)
        block = source[pl.ds(first, step)].astype(jnp.float32).reshape(step * rows, orbitals)
        for h in range(orbitals // 128):
            scratch[h] = block[:, h * 128 : (h + 1) * 128]
        for r in range(rows):
            for h in range(orbitals // 128):
                low = r * orbitals + h * 128
                target[pl.ds(first, step), low : low + 128] = scratch[
                    h, pl.ds(r, step, stride=rows), :
                ].astype(jnp.bfloat16)
        return carry

    lax.fori_loop(0, depth // step, body, 0)


def exchange(me, blocks, send, recv, chunk, send_sem, recv_sem, place=lambda d: d, land=lambda d: d):
    hop = stride_of(blocks)

    def step(k, carry):
        peer = lax.rem(me + k * hop, blocks)
        pltpu.make_async_remote_copy(
            src_ref=send.at[chunk, place(peer)],
            dst_ref=recv.at[chunk, land(me)],
            send_sem=send_sem.at[chunk],
            recv_sem=recv_sem.at[chunk],
            device_id={"chol": peer},
            device_id_type=MESH,
        ).start()
        return carry

    lax.fori_loop(1, blocks, step, 0)
    recv[chunk, land(me)] = send[chunk, place(me)]


def arrived(blocks, recv, chunk, sem):
    whole = recv.at[chunk, pl.ds(0, blocks - 1)]
    pltpu.make_async_copy(whole, whole, sem.at[chunk]).wait()


def kernel(
    dims,
    send_walker,
    slot_row,
    walkers,
    fields,
    chol_hbm,
    rotated_raw,
    new_walkers,
    force_bias,
    chol_raw,
    chol_wide,
    chol,
    rotated_wide,
    rotated,
    all_fields,
    br_send,
    br_recv,
    op_send,
    op_recv,
    op_rows,
    totals,
    nw_send,
    nw_recv,
    pair_send,
    pair_recv,
    pair_own,
    fb_send,
    fb_recv,
    send_sems,
    recv_sems,
    field_sems,
    load_sem,
    op_sems,
):
    blocks, chunks, width, cap, rows, elec = dims
    slots, electrons, orbitals = walkers.shape
    nchol = rotated.shape[0]
    halves = orbitals // 128
    me = lax.axis_index("chol")
    pairs = blocks // 2
    core, pair = lax.rem(me, 2), me // 2
    groups = math.gcd(4, blocks)
    share_of = blocks // groups
    hop = stride_of(blocks)
    load = pltpu.make_async_copy(chol_hbm, chol_raw, load_sem)
    load.start()

    barrier = pltpu.get_barrier_semaphore()

    def greet(k, carry):
        pl.semaphore_signal(
            barrier, inc=1, device_id={"chol": lax.rem(me + k, blocks)}, device_id_type=MESH
        )
        return carry

    lax.fori_loop(1, blocks, greet, 0)

    def pick(d, carry):
        for c in range(cap):
            br_send[0, d, c] = walkers[jnp.maximum(send_walker[d * cap + c], 0)]
        return carry

    lax.fori_loop(0, blocks, pick, 0)
    pl.semaphore_wait(barrier, blocks - 1)

    def share(k, carry):
        pltpu.make_async_remote_copy(
            src_ref=fields,
            dst_ref=all_fields.at[core, pair],
            send_sem=field_sems.at[0],
            recv_sem=field_sems.at[1],
            device_id={"chol": lax.rem(pair + k, pairs) * 2 + core},
            device_id_type=MESH,
        ).start()
        return carry

    lax.fori_loop(1, pairs, share, 0)
    all_fields[core, pair] = fields[...]
    load.wait()
    unfold(chol_raw, chol_wide, chol)
    same_core = all_fields.at[core, pl.ds(0, pairs - 1)]
    pltpu.make_async_copy(same_core, same_core, field_sems.at[1]).wait()
    across = pltpu.make_async_remote_copy(
        src_ref=all_fields.at[core],
        dst_ref=all_fields.at[core],
        send_sem=field_sems.at[2],
        recv_sem=field_sems.at[3],
        device_id={"chol": pair * 2 + 1 - core},
        device_id_type=MESH,
    )
    across.start()
    exchange(me, blocks, br_send, br_recv, 0, send_sems.at[0], recv_sems.at[0])

    across.wait_recv()
    scale = field_scale / math.sqrt(nchol)
    cols = rows * orbitals
    tile = min(512, cols)

    @pl.loop(0, cols // tile)
    def _(n):
        at = pl.ds(pl.multiple_of(n * tile, tile), tile)
        left = all_fields[...].reshape(blocks * slots, nchol)
        part = jnp.dot(left, chol[:, at], preferred_element_type=jnp.float32) * scale
        part = part.astype(jnp.bfloat16).reshape(blocks, chunks, width, tile)
        for q in range(chunks):
            op_send[q, :, :, at] = part[:, q]

    def send_operators(q):
        for group in range(groups):
            def step(k, carry):
                peer = lax.rem(me + k * hop, blocks)
                pltpu.make_async_remote_copy(
                    src_ref=op_send.at[q, place(peer)],
                    dst_ref=op_recv.at[q, me],
                    send_sem=send_sems.at[1, q],
                    recv_sem=op_sems.at[q, group],
                    device_id={"chol": peer},
                    device_id_type=MESH,
                ).start()
                return carry

            lax.fori_loop(max(1, group * share_of), (group + 1) * share_of, step, 0)
        op_recv[q, me] = op_send[q, place(me)]

    def place(d):
        return lax.rem(d, 2) * pairs + d // 2

    def taylor(q):
        def spread(k, carry):
            s = lax.rem(me + (blocks - k) * hop, blocks)
            block = op_recv[q, s].astype(jnp.float32)
            for r in range(rows):
                for h in range(halves):
                    low = r * orbitals + h * 128
                    op_rows[h, pl.ds(s * rows + r, width, stride=orbitals), :] = block[
                        :, low : low + 128
                    ]
            return carry

        for group in range(groups):
            count = share_of - 1 if group == 0 else share_of
            whole = op_recv.at[q, pl.ds(0, count)]
            pltpu.make_async_copy(whole, whole, op_sems.at[q, group]).wait()
            lax.fori_loop(group * share_of, (group + 1) * share_of, spread, 0)
        group = 4

        @pl.loop(0, width // group)
        def _(g):
            ops, terms, sums = [], [], []
            for u in range(group):
                w = g * group + u
                first = pl.ds(pl.multiple_of(w * orbitals, orbitals), orbitals)
                ops.append(
                    jnp.concatenate([op_rows[h, first, :] for h in range(halves)], axis=1).astype(
                        jnp.bfloat16
                    )
                )
                row = slot_row[q * width + w]
                terms.append(br_recv[0, row // cap, row % cap])
                sums.append(terms[u].astype(jnp.float32))
            for degree in range(1, degrees + 1):
                for u in range(group):
                    product = lax.dot_general(
                        terms[u],
                        ops[u],
                        (((1,), (1,)), ((), ())),
                        preferred_element_type=jnp.float32,
                    )
                    terms[u] = (product * (1.0 / degree)).astype(jnp.bfloat16)
                    sums[u] = sums[u] + terms[u].astype(jnp.float32)
            for u in range(group):
                w = g * group + u
                new_walkers[q * width + w] = sums[u].astype(jnp.bfloat16)
                place = pl.ds(pl.multiple_of(w * electrons, electrons), electrons)
                for h in range(halves):
                    totals[h, place, :] = sums[u][:, h * 128 : (h + 1) * 128]

        def turn(d, carry):
            for e in range(elec):
                for h in range(halves):
                    low = e * orbitals + h * 128
                    nw_send[q, d, :, low : low + 128] = totals[
                        h, pl.ds(d * elec + e, width, stride=electrons), :
                    ].astype(jnp.bfloat16)
            return carry

        lax.fori_loop(0, blocks, turn, 0)
        exchange(me, blocks, nw_send, nw_recv, q, send_sems.at[2], recv_sems.at[2], land=place)

    def partial(q, half, target):
        left = nw_recv[q, pl.ds(half * pairs, pairs)].reshape(pairs * width, elec * orbitals)
        step = min(256, nchol)

        @pl.loop(0, nchol // step)
        def _(n):
            at = pl.ds(pl.multiple_of(n * step, step), step)
            target[:, at] = lax.dot_general(
                left, rotated[at, :], (((1,), (1,)), ((), ())), preferred_element_type=jnp.float32
            )

    def bias(q):
        partial(q, 1 - core, pair_send.at[q])
        across = pltpu.make_async_remote_copy(
            src_ref=pair_send.at[q],
            dst_ref=pair_recv.at[q],
            send_sem=send_sems.at[4, q],
            recv_sem=recv_sems.at[4, q],
            device_id={"chol": pair * 2 + 1 - core},
            device_id_type=MESH,
        )
        across.start()
        partial(q, core, pair_own)
        across.wait_recv()
        both = (pair_own[...] + pair_recv[q]).astype(jnp.bfloat16)
        fb_send[q] = both.reshape(pairs, width, nchol)

        def step(k, carry):
            peer = lax.rem(pair + k, pairs)
            pltpu.make_async_remote_copy(
                src_ref=fb_send.at[q, peer],
                dst_ref=fb_recv.at[q, pair],
                send_sem=send_sems.at[3, q],
                recv_sem=recv_sems.at[3, q],
                device_id={"chol": peer * 2 + core},
                device_id_type=MESH,
            ).start()
            return carry

        lax.fori_loop(1, pairs, step, 0)
        fb_recv[q, pair] = fb_send[q, pair]

    def finish(q):
        force_bias[q * width : (q + 1) * width, :] = lax.fori_loop(
            1,
            pairs,
            lambda s, acc: acc + fb_recv[q, s].astype(jnp.float32),
            fb_recv[q, 0].astype(jnp.float32),
        )

    for q in range(min(2, chunks)):
        send_operators(q)
    unfold(rotated_raw, rotated_wide, rotated)
    arrived(blocks, br_recv, 0, recv_sems.at[0])
    for q in range(chunks + 2):
        if q < chunks:
            if q + 2 < chunks:
                send_operators(q + 2)
            taylor(q)
        if 1 <= q <= chunks:
            arrived(blocks, nw_recv, q - 1, recv_sems.at[2])
            bias(q - 1)
        if q >= 2:
            arrived(pairs, fb_recv, q - 2, recv_sems.at[3])
            finish(q - 2)
    arrived(blocks, br_send, 0, send_sems.at[0])
    across.wait_send()
    pltpu.make_async_copy(same_core, same_core, field_sems.at[0]).wait()
    for q in range(chunks):
        arrived(blocks, op_send, q, send_sems.at[1])
        arrived(blocks, nw_send, q, send_sems.at[2])
        arrived(pairs, fb_send, q, send_sems.at[3])
        pltpu.make_async_copy(pair_send.at[q], pair_send.at[q], send_sems.at[4, q]).wait()


def shards(blocks, walkers, fields, chol_vectors, rotated, send_walker, slot_row):
    slots, electrons, orbitals = walkers.shape
    nchol, rows, _ = chol_vectors.shape
    elec = rotated.shape[1]
    cap = send_walker.shape[-1]
    width = min(chunk_slots, slots)
    chunks = slots // width
    dims = (blocks, chunks, width, cap, rows, elec)
    bf16, f32 = jnp.bfloat16, jnp.float32
    vmem, smem = (pl.BlockSpec(memory_space=m) for m in (pltpu.VMEM, pltpu.SMEM))
    return pl.pallas_call(
        functools.partial(kernel, dims),
        out_shape=(
            jax.ShapeDtypeStruct(walkers.shape, bf16),
            jax.ShapeDtypeStruct((slots, nchol), f32),
        ),
        in_specs=[smem, smem, vmem, vmem, pl.BlockSpec(memory_space=pl.ANY), vmem],
        out_specs=(vmem, vmem),
        scratch_shapes=[
            pltpu.VMEM(chol_vectors.shape, bf16),
            pltpu.VMEM((orbitals // 128, rows * unfold_depth, 128), f32),
            pltpu.VMEM((nchol, rows * orbitals), bf16),
            pltpu.VMEM((orbitals // 128, elec * unfold_depth, 128), f32),
            pltpu.VMEM((nchol, elec * orbitals), bf16),
            pltpu.VMEM((2, blocks // 2, slots, nchol), bf16),
            pltpu.VMEM((1, blocks, cap, electrons, orbitals), bf16),
            pltpu.VMEM((1, blocks, cap, electrons, orbitals), bf16),
            pltpu.VMEM((chunks, blocks, width, rows * orbitals), bf16),
            pltpu.VMEM((chunks, blocks, width, rows * orbitals), bf16),
            pltpu.VMEM((orbitals // 128, width * orbitals, 128), f32),
            pltpu.VMEM((orbitals // 128, width * electrons, 128), f32),
            pltpu.VMEM((chunks, blocks, width, elec * orbitals), bf16),
            pltpu.VMEM((chunks, blocks, width, elec * orbitals), bf16),
            pltpu.VMEM((chunks, blocks // 2 * width, nchol), f32),
            pltpu.VMEM((chunks, blocks // 2 * width, nchol), f32),
            pltpu.VMEM((blocks // 2 * width, nchol), f32),
            pltpu.VMEM((chunks, blocks // 2, width, nchol), bf16),
            pltpu.VMEM((chunks, blocks // 2, width, nchol), bf16),
            pltpu.SemaphoreType.DMA((5, chunks)),
            pltpu.SemaphoreType.DMA((5, chunks)),
            pltpu.SemaphoreType.DMA((4,)),
            pltpu.SemaphoreType.DMA,
            pltpu.SemaphoreType.DMA((chunks, math.gcd(4, blocks))),
        ],
        compiler_params=pltpu.CompilerParams(
            collective_id=0, has_side_effects=True, vmem_limit_bytes=60 * 1024 * 1024
        ),
    )(
        send_walker.reshape(-1),
        slot_row,
        walkers,
        fields,
        chol_vectors,
        rotated,
    )


def turned(source, target, start, count):
    rows, orbitals = source.shape[1:]
    step = 16

    def body(b, carry):
        first = pl.multiple_of(start + b * step, step)
        block = jnp.swapaxes(source[pl.ds(first, step)], 0, 1)
        for r in range(rows):
            target[pl.ds(first, step), r * orbitals : (r + 1) * orbitals] = block[r]
        return carry

    lax.fori_loop(0, count // step, body, 0)


def parent_kernel(
    dims,
    send_walker,
    slot_row,
    fields,
    walkers_hbm,
    chol_hbm,
    rotated_hbm,
    branch,
    fb_total,
    walkers,
    chol_raw,
    chol,
    rotated_raw,
    rotated,
    all_fields,
    left,
    op_rows,
    op_send,
    op_recv,
    nw_full,
    nw_send,
    nw_recv,
    part,
    pair_recv,
    row_send,
    row_recv,
    fb_send,
    fb_recv,
    fw_wide,
    fw_send,
    fw_recv,
    fw_rows,
    load_sems,
    field_send,
    field_core,
    field_line,
    field_row,
    op_sent,
    op_got,
    nw_sent,
    nw_got,
    br_sent,
    br_got,
    pair_sent,
    pair_got,
    row_sent,
    row_got,
    fb_sent,
    fb_got,
    fw_sent,
    fw_got,
):
    blocks, cap, rows, elec = dims
    slots, nchol = fields.shape
    electrons, orbitals = walkers.shape[1:]
    halves = orbitals // 128
    me = lax.axis_index("chol")
    pairs, lines, half = blocks // 2, blocks // 4, blocks // 2
    hop = stride_of(blocks)
    core, pair = lax.rem(me, 2), me // 2
    line, across = pair // 2, lax.rem(pair, 2)
    side, local = me // half, lax.rem(me, half)
    away = 1 - side
    near = electrons // 2
    bf16, f32 = jnp.bfloat16, jnp.float32

    def wait(ref, sem):
        pltpu.make_async_copy(ref, ref, sem).wait()

    def send(src, dst, sent, got, peer):
        pltpu.make_async_remote_copy(
            src_ref=src,
            dst_ref=dst,
            send_sem=sent,
            recv_sem=got,
            device_id={"chol": peer},
            device_id_type=MESH,
        ).start()

    def everyone(to):
        def step(t, carry):
            to(lax.rem(me + t * hop, blocks))
            return carry

        lax.fori_loop(1, blocks, step, 0)

    def chip_at(k):
        beyond = across if k < lines else 1 - across
        return lax.rem(line + k % lines, lines) * 2 + beyond

    def steps_from(o, chip):
        z, y = chip // 2, lax.rem(chip, 2)
        apart = y if o // 2 % 2 == 0 else 1 - y
        return lax.rem(z + lines - o // 4, lines) + apart * lines

    def row_of(d):
        return lax.rem(d, 2) * pairs + d // 2

    pieces = 4
    span = nchol // pieces
    chol_loads = [
        pltpu.make_async_copy(
            chol_hbm.at[pl.ds(p * span, span)], chol_raw.at[pl.ds(p * span, span)], load_sems.at[p]
        )
        for p in range(pieces)
    ]
    for load in chol_loads:
        load.start()
    walker_load = pltpu.make_async_copy(walkers_hbm, walkers, load_sems.at[pieces])
    rotated_load = pltpu.make_async_copy(rotated_hbm, rotated_raw, load_sems.at[pieces + 1])
    walker_load.start()
    rotated_load.start()

    barrier = pltpu.get_barrier_semaphore()

    def greet(k, carry):
        pl.semaphore_signal(
            barrier, inc=1, device_id={"chol": lax.rem(me + k, blocks)}, device_id_type=MESH
        )
        return carry

    lax.fori_loop(1, blocks, greet, 0)

    order = lax.broadcasted_iota(jnp.int32, (slots, slots), 0)
    place = lax.broadcasted_iota(jnp.int32, (slots, slots), 1)
    chosen = jnp.zeros((slots, slots), f32)
    for p in range(slots):
        entry = slot_row[p]
        target = lax.rem(entry, cap) * blocks + entry // cap
        chosen = jnp.where((place == p) & (order == target), 1.0, chosen)
    all_fields[pair, core] = jnp.dot(
        chosen.astype(bf16), fields[...], preferred_element_type=f32
    ).astype(bf16)

    for p in range(pieces):
        chol_loads[p].wait()
        turned(chol_raw, chol, p * span, span)

    scale = field_scale / math.sqrt(nchol)
    cols = rows * orbitals
    tile = min(2048, cols)
    deep = tile // orbitals

    def operators(m):
        @pl.loop(0, cols // tile)
        def _(n):
            at = pl.ds(pl.multiple_of(n * tile, tile), tile)
            out = jnp.dot(left[:m], chol[:, at], preferred_element_type=f32) * scale
            for i in range(deep):
                op_rows[n * deep + i, :m] = out[:, i * orbitals : (i + 1) * orbitals].astype(bf16)

    def packed(b):
        return jnp.swapaxes(op_rows[:, b * blocks : (b + 1) * blocks], 0, 1)

    def chip_operators(which):
        left[:slots] = all_fields[pair, which]
        operators(slots)
        for c in range(cap):
            op_send[c, :, 0, which] = packed(c)

    def send_chip_operators(which):
        def to(s):
            send(
                op_send.at[:, s, 0, which],
                op_recv.at[:, me, 0, which],
                op_sent.at[cap],
                op_got.at[cap],
                s,
            )

        everyone(to)
        for c in range(cap):
            op_recv[c, me, 0, which] = op_send[c, me, 0, which]

    def other_operators(c, first, count):
        for k in range(count):
            chip = chip_at(first + k)
            for q in range(2):
                low = (k * 2 + q) * blocks
                at = pl.ds(pl.multiple_of(c * blocks, blocks), blocks)
                left[low : low + blocks] = all_fields[chip, q, at]
        operators(count * 2 * blocks)

        for k in range(count):
            for q in range(2):
                op_send[c, :, first + k, q] = packed(k * 2 + q)

        def to(s):
            send(
                op_send.at[c, s, pl.ds(first, count)],
                op_recv.at[c, me, pl.ds(first, count)],
                op_sent.at[c],
                op_got.at[c],
                s,
            )

        everyone(to)
        for k in range(count):
            for q in range(2):
                op_recv[c, me, first + k, q] = op_send[c, me, first + k, q]

    partner = pair * 2 + 1 - core
    beside = (line * 2 + 1 - across) * 2 + core

    bank = lines // 2
    low_bank = line < bank
    outer = jnp.where(low_bank, line < bank - 1, line > bank)
    rank = jnp.where(outer, 1, 0)
    other_line = jnp.where(low_bank, bank - 1 - line, lines + bank - 1 - line)
    far_inner = jnp.where(low_bank, bank, bank - 1)
    far_outer = jnp.where(low_bank, lines - 1, 0)
    held_lines = (line, other_line, far_inner, far_outer)

    def line_at(j):
        return held_lines[j]

    def along(z):
        return (z * 2 + across) * 2 + core

    own, twin = all_fields.at[pair, core], all_fields.at[pair, 1 - core]
    pl.semaphore_wait(barrier, blocks - 1)
    send(own, own, field_send.at[0], field_core.at[0], partner)
    send(own, own, field_send.at[2], field_line.at[2 + rank], along(far_inner))
    send(own, own, field_send.at[2], field_line.at[1], along(other_line))
    send(own, own, field_send.at[1], field_row.at[0], beside)

    def hand_on(held, j):
        @pl.when(rank == 0)
        def _():
            send(held, held, field_send.at[2], field_line.at[j], along(other_line))

    @pl.loop(0, 2)
    def _(t):
        @pl.when(t == 1)
        def _():
            for j in range(1, lines):
                held = all_fields.at[line_at(j) * 2 + across, core]
                wait(held, field_line.at[j])
                if j > 1:
                    hand_on(held, j)
                send(held, held, field_send.at[1], field_row.at[j], beside)
                send(held, held, field_send.at[0], field_core.at[1], partner)
            wait(twin, field_core.at[0])

        which = lax.rem(core + t, 2)
        chip_operators(which)
        send_chip_operators(which)

    wait(all_fields.at[pl.ds(0, lines - 1), 0], field_core.at[1])

    @pl.loop(0, cap)
    def _(c):
        other_operators(c, 1, lines - 1)

        @pl.when(c == 0)
        def _():
            for j in range(lines):
                held = all_fields.at[line_at(j) * 2 + 1 - across, core]
                wait(held, field_row.at[j])
                send(held, held, field_send.at[0], field_core.at[2], partner)
            wait(all_fields.at[pl.ds(0, lines), 0], field_core.at[2])

        other_operators(c, lines, lines)

    rotated_load.wait()
    turned(rotated_raw, rotated, 0, nchol)
    walker_load.wait()

    def taylor(c):
        group = 4

        @pl.loop(0, blocks // group)
        def _(g):
            ops, terms, sums = [], [], []
            for u in range(group):
                r = g * group + u
                chip, q = lax.rem(r, pairs), r // pairs
                ops.append(
                    jnp.concatenate(
                        [
                            op_recv[c, o, steps_from(o, chip), q]
                            for o in range(blocks)
                        ],
                        axis=0,
                    )
                )
                entry = jnp.maximum(send_walker[c, chip * 2 + q], 0)
                terms.append(walkers[entry])
                sums.append(terms[u].astype(f32))
            for degree in range(1, degrees + 1):
                for u in range(group):
                    product = lax.dot_general(
                        terms[u], ops[u], (((1,), (1,)), ((), ())), preferred_element_type=f32
                    )
                    terms[u] = (product * (1.0 / degree)).astype(bf16)
                    sums[u] = sums[u] + terms[u].astype(f32)
            for u in range(group):
                r = g * group + u
                nw_full[c, r] = sums[u].astype(bf16)

        for o in range(0, blocks, 16 // elec):
            block = jnp.swapaxes(nw_full[c, :, o * elec : o * elec + 16], 0, 1)
            for e in range(16):
                low = e % elec * orbitals
                nw_send[c, o + e // elec, :, low : low + orbitals] = block[e]

        def to_owner(o):
            send(nw_send.at[c, o], nw_recv.at[c, me], nw_sent.at[c], nw_got.at[c], o)

        everyone(to_owner)
        nw_recv[c, me] = nw_send[c, me]

    def send_walkers(c):
        mine = pl.ds(pl.multiple_of(side * near, near), near)

        def to_slot(d):
            @pl.when(d // half != side)
            def _():
                send(
                    nw_full.at[c, row_of(d), mine],
                    branch.at[c, me, mine],
                    br_sent.at[0],
                    br_got.at[0],
                    d,
                )

            @pl.when(d // half == side)
            def _():
                send(nw_full.at[c, row_of(d)], branch.at[c, me], br_sent.at[0], br_got.at[0], d)

        everyone(to_slot)
        branch[c, me] = nw_full[c, row_of(me)]

    def bias(c):
        rows_in = nw_recv[c].reshape(blocks * blocks, elec * orbitals)
        step = min(256, nchol)

        @pl.loop(0, nchol // step)
        def _(n):
            at = pl.ds(pl.multiple_of(n * step, step), step)
            out = lax.dot_general(
                rows_in, rotated[at, :], (((1,), (1,)), ((), ())), preferred_element_type=f32
            ).reshape(blocks, 2, pairs, step)
            for q in range(2):
                mine = out[:, q].reshape(blocks * pairs, step)
                for h in range(step // 128):
                    part[c, q, n * (step // 128) + h] = mine[:, h * 128 : (h + 1) * 128]

        send(part.at[c, 1 - core], pair_recv.at[c], pair_sent.at[c], pair_got.at[c], partner)

    def reduced(c, chip, h):
        at = pl.ds(chip, blocks, stride=pairs)
        return part[c, core, h, at, :] + pair_recv[c, h, at, :]

    def reduce(c):
        wait(pair_recv.at[c], pair_got.at[c])

        def pick(z, carry):
            for h in range(nchol // 128):
                both = reduced(c, z * 2 + 1 - across, h)
                row_send[c, z, :, h * 128 : (h + 1) * 128] = both.astype(bf16)
            return carry

        lax.fori_loop(0, lines, pick, 0)
        send(row_send.at[c], row_recv.at[c], row_sent.at[c], row_got.at[c], beside)

    def spread(c):
        wait(row_recv.at[c], row_got.at[c])

        def pick(z, carry):
            for h in range(nchol // 128):
                low = h * 128
                both = reduced(c, z * 2 + across, h)
                both = both + row_recv[c, z, :, low : low + 128].astype(f32)
                fb_send[c, z, :, low : low + 128] = both.astype(bf16)
            return carry

        lax.fori_loop(0, lines, pick, 0)

        def step(k, carry):
            z = lax.rem(line + k, lines)
            send(
                fb_send.at[c, z],
                fb_recv.at[c, line],
                fb_sent.at[c],
                fb_got.at[c],
                (z * 2 + across) * 2 + core,
            )
            return carry

        lax.fori_loop(1, lines, step, 0)
        fb_recv[c, line] = fb_send[c, line]

    def finish(c):
        wait(fb_recv.at[c, pl.ds(0, lines - 1)], fb_got.at[c])
        fb_total[c] = lax.fori_loop(
            1,
            lines,
            lambda s, acc: acc + fb_recv[c, s].astype(f32),
            fb_recv[c, 0].astype(f32),
        )

    def forward():
        count = half * blocks
        for c in range(cap):
            block = nw_recv[c, pl.ds(away * half, half)].astype(f32)
            block = block.reshape(count, elec * orbitals)
            for h in range(elec * orbitals // 128):
                fw_wide[h, c * count : (c + 1) * count] = block[:, h * 128 : (h + 1) * 128]

        def gather(t, carry):
            at = pl.ds(row_of(side * half + t), cap * half, stride=blocks)
            for h in range(elec * orbitals // 128):
                fw_send[t, :, h * 128 : (h + 1) * 128] = fw_wide[h, at, :].astype(bf16)
            return carry

        lax.fori_loop(0, half, gather, 0)

        def step(k, carry):
            t = lax.rem(local + k, half)
            send(fw_send.at[t], fw_recv.at[local], fw_sent.at[0], fw_got.at[0], side * half + t)
            return carry

        lax.fori_loop(1, half, step, 0)
        fw_recv[local] = fw_send[local]

    def collect():
        wait(fw_recv.at[pl.ds(0, half - 1)], fw_got.at[0])

        def fold(o, carry):
            block = fw_recv[o].astype(f32)
            for e in range(elec):
                for h in range(halves):
                    low = e * orbitals + h * 128
                    fw_rows[h, pl.ds(o * elec + e, cap * half, stride=near), :] = block[
                        :, low : low + 128
                    ]
            return carry

        lax.fori_loop(0, half, fold, 0)
        wait(branch.at[:, pl.ds(0, half - 1 + half // 2)], br_got.at[0])

        def put(s, carry):
            for c in range(cap):
                at = pl.ds(pl.multiple_of((c * half + s) * near, near), near)
                value = jnp.concatenate([fw_rows[h, at, :] for h in range(halves)], axis=1)
                mine = pl.ds(pl.multiple_of(side * near, near), near)
                branch[c, away * half + s, mine] = value.astype(bf16)
            return carry

        lax.fori_loop(0, half, put, 0)

    wait(op_recv.at[:, pl.ds(0, blocks - 1), 0], op_got.at[cap])
    for c in range(cap):
        wait(op_recv.at[c, pl.ds(0, blocks - 1), pl.ds(1, pairs - 1)], op_got.at[c])
        taylor(c)
    for c in range(cap):
        send_walkers(c)
    for c in range(cap):
        wait(nw_recv.at[c, pl.ds(0, blocks - 1)], nw_got.at[c])
        bias(c)
        if c == cap - 1:
            forward()
        reduce(c)
        spread(c)
    collect()
    for c in range(cap):
        finish(c)

    wait(all_fields.at[:, 0], field_send.at[0])
    wait(all_fields.at[pl.ds(0, lines), 0], field_send.at[1])

    @pl.when(rank == 0)
    def _():
        wait(all_fields.at[pl.ds(0, 4), 0], field_send.at[2])

    @pl.when(rank == 1)
    def _():
        wait(all_fields.at[pl.ds(0, 2), 0], field_send.at[2])

    wait(op_recv.at[:, pl.ds(0, blocks - 1), 0], op_sent.at[cap])
    wait(branch.at[:, pl.ds(0, half - 1 + half // 2)], br_sent.at[0])
    wait(fw_send.at[pl.ds(0, half - 1)], fw_sent.at[0])
    for c in range(cap):
        wait(op_recv.at[c, pl.ds(0, blocks - 1), pl.ds(1, pairs - 1)], op_sent.at[c])
        wait(nw_send.at[c, pl.ds(0, blocks - 1)], nw_sent.at[c])
        wait(pair_recv.at[c], pair_sent.at[c])
        wait(row_send.at[c], row_sent.at[c])
        wait(fb_send.at[c, pl.ds(0, lines - 1)], fb_sent.at[c])


def place_kernel(slot_row, branch, fb_total, new_walkers, force_bias):
    cap = branch.shape[0]

    @pl.loop(0, slot_row.shape[0])
    def _(p):
        entry = slot_row[p]
        c, s = lax.rem(entry, cap), entry // cap
        new_walkers[p] = branch[c, s]
        force_bias[pl.ds(p, 1), :] = fb_total[c, pl.ds(s, 1), :]


def parent_shards(blocks, walkers, fields, chol_vectors, rotated, send_walker, slot_row):
    slots, electrons, orbitals = walkers.shape
    nchol, rows, _ = chol_vectors.shape
    elec = rotated.shape[1]
    cap = send_walker.shape[-1]
    bf16, f32 = jnp.bfloat16, jnp.float32
    pairs, lines, half = blocks // 2, blocks // 4, blocks // 2
    halves, near = orbitals // 128, electrons // 2
    most = max(pairs // 2 * 2 * blocks, slots)
    wide = elec * orbitals
    vmem, smem, anywhere = (
        pl.BlockSpec(memory_space=m) for m in (pltpu.VMEM, pltpu.SMEM, pl.ANY)
    )
    dma = pltpu.SemaphoreType.DMA
    branch, fb_total = pl.pallas_call(
        functools.partial(parent_kernel, (blocks, cap, rows, elec)),
        out_shape=(
            jax.ShapeDtypeStruct((cap, blocks, electrons, orbitals), bf16),
            jax.ShapeDtypeStruct((cap, blocks, nchol), f32),
        ),
        in_specs=[smem, smem, vmem, anywhere, anywhere, anywhere],
        out_specs=(vmem, vmem),
        scratch_shapes=[
            pltpu.VMEM(walkers.shape, bf16),
            pltpu.VMEM(chol_vectors.shape, bf16),
            pltpu.VMEM((nchol, rows * orbitals), bf16),
            pltpu.VMEM(rotated.shape, bf16),
            pltpu.VMEM((nchol, wide), bf16),
            pltpu.VMEM((pairs, 2, slots, nchol), bf16),
            pltpu.VMEM((most, nchol), bf16),
            pltpu.VMEM((rows, most, orbitals), bf16),
            pltpu.VMEM((cap, blocks, pairs, 2, rows, orbitals), bf16),
            pltpu.VMEM((cap, blocks, pairs, 2, rows, orbitals), bf16),
            pltpu.VMEM((cap, blocks, electrons, orbitals), bf16),
            pltpu.VMEM((cap, blocks, blocks, wide), bf16),
            pltpu.VMEM((cap, blocks, blocks, wide), bf16),
            pltpu.VMEM((cap, 2, nchol // 128, blocks * pairs, 128), f32),
            pltpu.VMEM((cap, nchol // 128, blocks * pairs, 128), f32),
            pltpu.VMEM((cap, lines, blocks, nchol), bf16),
            pltpu.VMEM((cap, lines, blocks, nchol), bf16),
            pltpu.VMEM((cap, lines, blocks, nchol), bf16),
            pltpu.VMEM((cap, lines, blocks, nchol), bf16),
            pltpu.VMEM((wide // 128, cap * half * blocks, 128), f32),
            pltpu.VMEM((half, cap * half, wide), bf16),
            pltpu.VMEM((half, cap * half, wide), bf16),
            pltpu.VMEM((halves, cap * half * near, 128), f32),
            dma((6,)),
            dma((3,)),
            dma((3,)),
            dma((lines,)),
            dma((lines,)),
            dma((cap + 1,)),
            dma((cap + 1,)),
            dma((cap,)),
            dma((cap,)),
            dma((1,)),
            dma((1,)),
            dma((cap,)),
            dma((cap,)),
            dma((cap,)),
            dma((cap,)),
            dma((cap,)),
            dma((cap,)),
            dma((1,)),
            dma((1,)),
        ],
        compiler_params=pltpu.CompilerParams(
            collective_id=1, has_side_effects=True, vmem_limit_bytes=60 * 1024 * 1024
        ),
    )(
        jnp.transpose(send_walker, (0, 2, 1)).reshape(cap, blocks),
        slot_row,
        fields,
        walkers,
        chol_vectors,
        rotated,
    )
    return pl.pallas_call(
        place_kernel,
        out_shape=(
            jax.ShapeDtypeStruct(walkers.shape, bf16),
            jax.ShapeDtypeStruct((slots, nchol), f32),
        ),
        in_specs=[smem, vmem, vmem],
        out_specs=(vmem, vmem),
    )(slot_row, branch, fb_total)


def plan(blocks, walkers, fields, chol_vectors, rotated, send_walker, slot_row):
    every_entry = blocks * send_walker.shape[-1] == walkers.shape[0]
    step = parent_shards if every_entry and blocks == 4 * 2 * 2 else shards
    return step(blocks, walkers, fields, chol_vectors, rotated, send_walker, slot_row)


def solution(mesh):
    in_specs = (
        P(("grp", "chol"), None, None),
        P(("grp", "chol"), None),
        P(None, "chol", None),
        P(None, "chol", None),
        P(("grp", "chol"), None, None),
        P(("grp", "chol")),
    )
    out_specs = (P(("grp", "chol"), None, None), P(("grp", "chol"), None))
    return jax.shard_map(
        functools.partial(plan, mesh.shape["chol"]),
        mesh=mesh,
        in_specs=in_specs,
        out_specs=out_specs,
        check_vma=False,
    )
```

```python
import functools
import math

import jax
import jax.numpy as jnp
from jax import lax
from jax.experimental import pallas as pl
from jax.experimental.pallas import tpu as pltpu
from jax.sharding import PartitionSpec as P

field_scale = 1.5
chunk_slots = 16
degrees = 5
unfold_depth = 64
MESH = pl.DeviceIdType.MESH


def stride_of(blocks):
    return next(h for h in (7, 5, 3, 1) if math.gcd(h, blocks) == 1)


def unfold(source, scratch, target):
    depth, rows, orbitals = source.shape
    step = scratch.shape[1] // rows

    def body(b, carry):
        first = pl.multiple_of(b * step, step)
        block = source[pl.ds(first, step)].astype(jnp.float32).reshape(step * rows, orbitals)
        for h in range(orbitals // 128):
            scratch[h] = block[:, h * 128 : (h + 1) * 128]
        for r in range(rows):
            for h in range(orbitals // 128):
                low = r * orbitals + h * 128
                target[pl.ds(first, step), low : low + 128] = scratch[
                    h, pl.ds(r, step, stride=rows), :
                ].astype(jnp.bfloat16)
        return carry

    lax.fori_loop(0, depth // step, body, 0)


def exchange(me, blocks, send, recv, chunk, send_sem, recv_sem, place=lambda d: d, land=lambda d: d):
    hop = stride_of(blocks)

    def step(k, carry):
        peer = lax.rem(me + k * hop, blocks)
        pltpu.make_async_remote_copy(
            src_ref=send.at[chunk, place(peer)],
            dst_ref=recv.at[chunk, land(me)],
            send_sem=send_sem.at[chunk],
            recv_sem=recv_sem.at[chunk],
            device_id={"chol": peer},
            device_id_type=MESH,
        ).start()
        return carry

    lax.fori_loop(1, blocks, step, 0)
    recv[chunk, land(me)] = send[chunk, place(me)]


def arrived(blocks, recv, chunk, sem):
    whole = recv.at[chunk, pl.ds(0, blocks - 1)]
    pltpu.make_async_copy(whole, whole, sem.at[chunk]).wait()


def kernel(
    dims,
    send_walker,
    slot_row,
    walkers,
    fields,
    chol_hbm,
    rotated_raw,
    new_walkers,
    force_bias,
    chol_raw,
    chol_wide,
    chol,
    rotated_wide,
    rotated,
    all_fields,
    br_send,
    br_recv,
    op_send,
    op_recv,
    op_rows,
    totals,
    nw_send,
    nw_recv,
    pair_send,
    pair_recv,
    pair_own,
    fb_send,
    fb_recv,
    send_sems,
    recv_sems,
    field_sems,
    load_sem,
    op_sems,
):
    blocks, chunks, width, cap, rows, elec = dims
    slots, electrons, orbitals = walkers.shape
    nchol = rotated.shape[0]
    halves = orbitals // 128
    me = lax.axis_index("chol")
    pairs = blocks // 2
    core, pair = lax.rem(me, 2), me // 2
    groups = math.gcd(4, blocks)
    share_of = blocks // groups
    hop = stride_of(blocks)
    load = pltpu.make_async_copy(chol_hbm, chol_raw, load_sem)
    load.start()

    barrier = pltpu.get_barrier_semaphore()

    def greet(k, carry):
        pl.semaphore_signal(
            barrier, inc=1, device_id={"chol": lax.rem(me + k, blocks)}, device_id_type=MESH
        )
        return carry

    lax.fori_loop(1, blocks, greet, 0)

    def pick(d, carry):
        for c in range(cap):
            br_send[0, d, c] = walkers[jnp.maximum(send_walker[d * cap + c], 0)]
        return carry

    lax.fori_loop(0, blocks, pick, 0)
    pl.semaphore_wait(barrier, blocks - 1)

    def share(k, carry):
        pltpu.make_async_remote_copy(
            src_ref=fields,
            dst_ref=all_fields.at[core, pair],
            send_sem=field_sems.at[0],
            recv_sem=field_sems.at[1],
            device_id={"chol": lax.rem(pair + k, pairs) * 2 + core},
            device_id_type=MESH,
        ).start()
        return carry

    lax.fori_loop(1, pairs, share, 0)
    all_fields[core, pair] = fields[...]
    load.wait()
    unfold(chol_raw, chol_wide, chol)
    same_core = all_fields.at[core, pl.ds(0, pairs - 1)]
    pltpu.make_async_copy(same_core, same_core, field_sems.at[1]).wait()
    across = pltpu.make_async_remote_copy(
        src_ref=all_fields.at[core],
        dst_ref=all_fields.at[core],
        send_sem=field_sems.at[2],
        recv_sem=field_sems.at[3],
        device_id={"chol": pair * 2 + 1 - core},
        device_id_type=MESH,
    )
    across.start()
    exchange(me, blocks, br_send, br_recv, 0, send_sems.at[0], recv_sems.at[0])

    across.wait_recv()
    scale = field_scale / math.sqrt(nchol)
    cols = rows * orbitals
    tile = min(512, cols)

    @pl.loop(0, cols // tile)
    def _(n):
        at = pl.ds(pl.multiple_of(n * tile, tile), tile)
        left = all_fields[...].reshape(blocks * slots, nchol)
        part = jnp.dot(left, chol[:, at], preferred_element_type=jnp.float32) * scale
        part = part.astype(jnp.bfloat16).reshape(blocks, chunks, width, tile)
        for q in range(chunks):
            op_send[q, :, :, at] = part[:, q]

    def send_operators(q):
        for group in range(groups):
            def step(k, carry):
                peer = lax.rem(me + k * hop, blocks)
                pltpu.make_async_remote_copy(
                    src_ref=op_send.at[q, place(peer)],
                    dst_ref=op_recv.at[q, me],
                    send_sem=send_sems.at[1, q],
                    recv_sem=op_sems.at[q, group],
                    device_id={"chol": peer},
                    device_id_type=MESH,
                ).start()
                return carry

            lax.fori_loop(max(1, group * share_of), (group + 1) * share_of, step, 0)
        op_recv[q, me] = op_send[q, place(me)]

    def place(d):
        return lax.rem(d, 2) * pairs + d // 2

    def taylor(q):
        def spread(k, carry):
            s = lax.rem(me + (blocks - k) * hop, blocks)
            block = op_recv[q, s].astype(jnp.float32)
            for r in range(rows):
                for h in range(halves):
                    low = r * orbitals + h * 128
                    op_rows[h, pl.ds(s * rows + r, width, stride=orbitals), :] = block[
                        :, low : low + 128
                    ]
            return carry

        for group in range(groups):
            count = share_of - 1 if group == 0 else share_of
            whole = op_recv.at[q, pl.ds(0, count)]
            pltpu.make_async_copy(whole, whole, op_sems.at[q, group]).wait()
            lax.fori_loop(group * share_of, (group + 1) * share_of, spread, 0)
        group = 4

        @pl.loop(0, width // group)
        def _(g):
            ops, terms, sums = [], [], []
            for u in range(group):
                w = g * group + u
                first = pl.ds(pl.multiple_of(w * orbitals, orbitals), orbitals)
                ops.append(
                    jnp.concatenate([op_rows[h, first, :] for h in range(halves)], axis=1).astype(
                        jnp.bfloat16
                    )
                )
                row = slot_row[q * width + w]
                terms.append(br_recv[0, row // cap, row % cap])
                sums.append(terms[u].astype(jnp.float32))
            for degree in range(1, degrees + 1):
                for u in range(group):
                    product = lax.dot_general(
                        terms[u],
                        ops[u],
                        (((1,), (1,)), ((), ())),
                        preferred_element_type=jnp.float32,
                    )
                    terms[u] = (product * (1.0 / degree)).astype(jnp.bfloat16)
                    sums[u] = sums[u] + terms[u].astype(jnp.float32)
            for u in range(group):
                w = g * group + u
                new_walkers[q * width + w] = sums[u].astype(jnp.bfloat16)
                place = pl.ds(pl.multiple_of(w * electrons, electrons), electrons)
                for h in range(halves):
                    totals[h, place, :] = sums[u][:, h * 128 : (h + 1) * 128]

        def turn(d, carry):
            for e in range(elec):
                for h in range(halves):
                    low = e * orbitals + h * 128
                    nw_send[q, d, :, low : low + 128] = totals[
                        h, pl.ds(d * elec + e, width, stride=electrons), :
                    ].astype(jnp.bfloat16)
            return carry

        lax.fori_loop(0, blocks, turn, 0)
        exchange(me, blocks, nw_send, nw_recv, q, send_sems.at[2], recv_sems.at[2], land=place)

    def partial(q, half, target):
        left = nw_recv[q, pl.ds(half * pairs, pairs)].reshape(pairs * width, elec * orbitals)
        step = min(256, nchol)

        @pl.loop(0, nchol // step)
        def _(n):
            at = pl.ds(pl.multiple_of(n * step, step), step)
            target[:, at] = lax.dot_general(
                left, rotated[at, :], (((1,), (1,)), ((), ())), preferred_element_type=jnp.float32
            )

    def bias(q):
        partial(q, 1 - core, pair_send.at[q])
        across = pltpu.make_async_remote_copy(
            src_ref=pair_send.at[q],
            dst_ref=pair_recv.at[q],
            send_sem=send_sems.at[4, q],
            recv_sem=recv_sems.at[4, q],
            device_id={"chol": pair * 2 + 1 - core},
            device_id_type=MESH,
        )
        across.start()
        partial(q, core, pair_own)
        across.wait_recv()
        both = (pair_own[...] + pair_recv[q]).astype(jnp.bfloat16)
        fb_send[q] = both.reshape(pairs, width, nchol)

        def step(k, carry):
            peer = lax.rem(pair + k, pairs)
            pltpu.make_async_remote_copy(
                src_ref=fb_send.at[q, peer],
                dst_ref=fb_recv.at[q, pair],
                send_sem=send_sems.at[3, q],
                recv_sem=recv_sems.at[3, q],
                device_id={"chol": peer * 2 + core},
                device_id_type=MESH,
            ).start()
            return carry

        lax.fori_loop(1, pairs, step, 0)
        fb_recv[q, pair] = fb_send[q, pair]

    def finish(q):
        force_bias[q * width : (q + 1) * width, :] = lax.fori_loop(
            1,
            pairs,
            lambda s, acc: acc + fb_recv[q, s].astype(jnp.float32),
            fb_recv[q, 0].astype(jnp.float32),
        )

    for q in range(min(2, chunks)):
        send_operators(q)
    unfold(rotated_raw, rotated_wide, rotated)
    arrived(blocks, br_recv, 0, recv_sems.at[0])
    for q in range(chunks + 2):
        if q < chunks:
            if q + 2 < chunks:
                send_operators(q + 2)
            taylor(q)
        if 1 <= q <= chunks:
            arrived(blocks, nw_recv, q - 1, recv_sems.at[2])
            bias(q - 1)
        if q >= 2:
            arrived(pairs, fb_recv, q - 2, recv_sems.at[3])
            finish(q - 2)
    arrived(blocks, br_send, 0, send_sems.at[0])
    across.wait_send()
    pltpu.make_async_copy(same_core, same_core, field_sems.at[0]).wait()
    for q in range(chunks):
        arrived(blocks, op_send, q, send_sems.at[1])
        arrived(blocks, nw_send, q, send_sems.at[2])
        arrived(pairs, fb_send, q, send_sems.at[3])
        pltpu.make_async_copy(pair_send.at[q], pair_send.at[q], send_sems.at[4, q]).wait()


def shards(blocks, walkers, fields, chol_vectors, rotated, send_walker, slot_row):
    slots, electrons, orbitals = walkers.shape
    nchol, rows, _ = chol_vectors.shape
    elec = rotated.shape[1]
    cap = send_walker.shape[-1]
    width = min(chunk_slots, slots)
    chunks = slots // width
    dims = (blocks, chunks, width, cap, rows, elec)
    bf16, f32 = jnp.bfloat16, jnp.float32
    vmem, smem = (pl.BlockSpec(memory_space=m) for m in (pltpu.VMEM, pltpu.SMEM))
    return pl.pallas_call(
        functools.partial(kernel, dims),
        out_shape=(
            jax.ShapeDtypeStruct(walkers.shape, bf16),
            jax.ShapeDtypeStruct((slots, nchol), f32),
        ),
        in_specs=[smem, smem, vmem, vmem, pl.BlockSpec(memory_space=pl.ANY), vmem],
        out_specs=(vmem, vmem),
        scratch_shapes=[
            pltpu.VMEM(chol_vectors.shape, bf16),
            pltpu.VMEM((orbitals // 128, rows * unfold_depth, 128), f32),
            pltpu.VMEM((nchol, rows * orbitals), bf16),
            pltpu.VMEM((orbitals // 128, elec * unfold_depth, 128), f32),
            pltpu.VMEM((nchol, elec * orbitals), bf16),
            pltpu.VMEM((2, blocks // 2, slots, nchol), bf16),
            pltpu.VMEM((1, blocks, cap, electrons, orbitals), bf16),
            pltpu.VMEM((1, blocks, cap, electrons, orbitals), bf16),
            pltpu.VMEM((chunks, blocks, width, rows * orbitals), bf16),
            pltpu.VMEM((chunks, blocks, width, rows * orbitals), bf16),
            pltpu.VMEM((orbitals // 128, width * orbitals, 128), f32),
            pltpu.VMEM((orbitals // 128, width * electrons, 128), f32),
            pltpu.VMEM((chunks, blocks, width, elec * orbitals), bf16),
            pltpu.VMEM((chunks, blocks, width, elec * orbitals), bf16),
            pltpu.VMEM((chunks, blocks // 2 * width, nchol), f32),
            pltpu.VMEM((chunks, blocks // 2 * width, nchol), f32),
            pltpu.VMEM((blocks // 2 * width, nchol), f32),
            pltpu.VMEM((chunks, blocks // 2, width, nchol), bf16),
            pltpu.VMEM((chunks, blocks // 2, width, nchol), bf16),
            pltpu.SemaphoreType.DMA((5, chunks)),
            pltpu.SemaphoreType.DMA((5, chunks)),
            pltpu.SemaphoreType.DMA((4,)),
            pltpu.SemaphoreType.DMA,
            pltpu.SemaphoreType.DMA((chunks, math.gcd(4, blocks))),
        ],
        compiler_params=pltpu.CompilerParams(
            collective_id=0, has_side_effects=True, vmem_limit_bytes=60 * 1024 * 1024
        ),
    )(
        send_walker.reshape(-1),
        slot_row,
        walkers,
        fields,
        chol_vectors,
        rotated,
    )


def turned(source, target, start, count):
    rows, orbitals = source.shape[1:]
    step = 16

    def body(b, carry):
        first = pl.multiple_of(start + b * step, step)
        block = jnp.swapaxes(source[pl.ds(first, step)], 0, 1)
        for r in range(rows):
            target[pl.ds(first, step), r * orbitals : (r + 1) * orbitals] = block[r]
        return carry

    lax.fori_loop(0, count // step, body, 0)


def parent_kernel(
    dims,
    send_walker,
    slot_row,
    fields,
    walkers_hbm,
    chol_hbm,
    rotated_hbm,
    branch,
    fb_total,
    walkers,
    chol_raw,
    chol,
    rotated_raw,
    rotated,
    all_fields,
    left,
    op_rows,
    op_send,
    op_recv,
    nw_full,
    nw_send,
    nw_recv,
    part,
    pair_recv,
    row_send,
    row_recv,
    fb_send,
    fb_recv,
    fw_wide,
    fw_send,
    fw_recv,
    fw_rows,
    load_sems,
    field_send,
    field_core,
    field_line,
    field_row,
    op_sent,
    op_got,
    nw_sent,
    nw_got,
    br_sent,
    br_got,
    pair_sent,
    pair_got,
    row_sent,
    row_got,
    fb_sent,
    fb_got,
    fw_sent,
    fw_got,
):
    blocks, cap, rows, elec = dims
    slots, nchol = fields.shape
    electrons, orbitals = walkers.shape[1:]
    halves = orbitals // 128
    me = lax.axis_index("chol")
    pairs, lines, half = blocks // 2, blocks // 4, blocks // 2
    hop = stride_of(blocks)
    core, pair = lax.rem(me, 2), me // 2
    line, across = pair // 2, lax.rem(pair, 2)
    side, local = me // half, lax.rem(me, half)
    away = 1 - side
    near = electrons // 2
    bf16, f32 = jnp.bfloat16, jnp.float32

    def wait(ref, sem):
        pltpu.make_async_copy(ref, ref, sem).wait()

    def send(src, dst, sent, got, peer):
        pltpu.make_async_remote_copy(
            src_ref=src,
            dst_ref=dst,
            send_sem=sent,
            recv_sem=got,
            device_id={"chol": peer},
            device_id_type=MESH,
        ).start()

    def everyone(to):
        def step(t, carry):
            to(lax.rem(me + t * hop, blocks))
            return carry

        lax.fori_loop(1, blocks, step, 0)

    def chip_at(k):
        beyond = across if k < lines else 1 - across
        return lax.rem(line + k % lines, lines) * 2 + beyond

    def steps_from(o, chip):
        z, y = chip // 2, lax.rem(chip, 2)
        apart = y if o // 2 % 2 == 0 else 1 - y
        return lax.rem(z + lines - o // 4, lines) + apart * lines

    def row_of(d):
        return lax.rem(d, 2) * pairs + d // 2

    pieces = 4
    span = nchol // pieces
    chol_loads = [
        pltpu.make_async_copy(
            chol_hbm.at[pl.ds(p * span, span)], chol_raw.at[pl.ds(p * span, span)], load_sems.at[p]
        )
        for p in range(pieces)
    ]
    for load in chol_loads:
        load.start()
    walker_load = pltpu.make_async_copy(walkers_hbm, walkers, load_sems.at[pieces])
    rotated_load = pltpu.make_async_copy(rotated_hbm, rotated_raw, load_sems.at[pieces + 1])
    walker_load.start()
    rotated_load.start()

    barrier = pltpu.get_barrier_semaphore()

    def greet(k, carry):
        pl.semaphore_signal(
            barrier, inc=1, device_id={"chol": lax.rem(me + k, blocks)}, device_id_type=MESH
        )
        return carry

    lax.fori_loop(1, blocks, greet, 0)

    order = lax.broadcasted_iota(jnp.int32, (slots, slots), 0)
    place = lax.broadcasted_iota(jnp.int32, (slots, slots), 1)
    chosen = jnp.zeros((slots, slots), f32)
    for p in range(slots):
        entry = slot_row[p]
        target = lax.rem(entry, cap) * blocks + entry // cap
        chosen = jnp.where((place == p) & (order == target), 1.0, chosen)
    all_fields[pair, core] = jnp.dot(
        chosen.astype(bf16), fields[...], preferred_element_type=f32
    ).astype(bf16)

    for p in range(pieces):
        chol_loads[p].wait()
        turned(chol_raw, chol, p * span, span)

    scale = field_scale / math.sqrt(nchol)
    cols = rows * orbitals
    tile = min(2048, cols)
    deep = tile // orbitals

    def operators(m):
        @pl.loop(0, cols // tile)
        def _(n):
            at = pl.ds(pl.multiple_of(n * tile, tile), tile)
            out = jnp.dot(left[:m], chol[:, at], preferred_element_type=f32) * scale
            for i in range(deep):
                op_rows[n * deep + i, :m] = out[:, i * orbitals : (i + 1) * orbitals].astype(bf16)

    def packed(b):
        return jnp.swapaxes(op_rows[:, b * blocks : (b + 1) * blocks], 0, 1)

    def chip_operators(which):
        left[:slots] = all_fields[pair, which]
        operators(slots)
        for c in range(cap):
            op_send[c, :, 0, which] = packed(c)

    def send_chip_operators(which):
        def to(s):
            send(
                op_send.at[:, s, 0, which],
                op_recv.at[:, me, 0, which],
                op_sent.at[cap],
                op_got.at[cap],
                s,
            )

        everyone(to)
        for c in range(cap):
            op_recv[c, me, 0, which] = op_send[c, me, 0, which]

    def other_operators(c, first, count):
        for k in range(count):
            chip = chip_at(first + k)
            for q in range(2):
                low = (k * 2 + q) * blocks
                at = pl.ds(pl.multiple_of(c * blocks, blocks), blocks)
                left[low : low + blocks] = all_fields[chip, q, at]
        operators(count * 2 * blocks)

        for k in range(count):
            for q in range(2):
                op_send[c, :, first + k, q] = packed(k * 2 + q)

        def to(s):
            send(
                op_send.at[c, s, pl.ds(first, count)],
                op_recv.at[c, me, pl.ds(first, count)],
                op_sent.at[c],
                op_got.at[c],
                s,
            )

        everyone(to)
        for k in range(count):
            for q in range(2):
                op_recv[c, me, first + k, q] = op_send[c, me, first + k, q]

    partner = pair * 2 + 1 - core
    beside = (line * 2 + 1 - across) * 2 + core

    bank = lines // 2
    low_bank = line < bank
    outer = jnp.where(low_bank, line < bank - 1, line > bank)
    rank = jnp.where(outer, 1, 0)
    other_line = jnp.where(low_bank, bank - 1 - line, lines + bank - 1 - line)
    far_inner = jnp.where(low_bank, bank, bank - 1)
    far_outer = jnp.where(low_bank, lines - 1, 0)
    held_lines = (line, other_line, far_inner, far_outer)

    def line_at(j):
        return held_lines[j]

    def along(z):
        return (z * 2 + across) * 2 + core

    own, twin = all_fields.at[pair, core], all_fields.at[pair, 1 - core]
    pl.semaphore_wait(barrier, blocks - 1)
    send(own, own, field_send.at[0], field_core.at[0], partner)
    send(own, own, field_send.at[2], field_line.at[2 + rank], along(far_inner))
    send(own, own, field_send.at[2], field_line.at[1], along(other_line))
    send(own, own, field_send.at[1], field_row.at[0], beside)

    def hand_on(held, j):
        @pl.when(rank == 0)
        def _():
            send(held, held, field_send.at[2], field_line.at[j], along(other_line))

    @pl.loop(0, 2)
    def _(t):
        @pl.when(t == 1)
        def _():
            for j in range(1, lines):
                held = all_fields.at[line_at(j) * 2 + across, core]
                wait(held, field_line.at[j])
                if j > 1:
                    hand_on(held, j)
                send(held, held, field_send.at[1], field_row.at[j], beside)
                send(held, held, field_send.at[0], field_core.at[1], partner)
            wait(twin, field_core.at[0])

        which = lax.rem(core + t, 2)
        chip_operators(which)
        send_chip_operators(which)

    wait(all_fields.at[pl.ds(0, lines - 1), 0], field_core.at[1])

    @pl.loop(0, cap)
    def _(c):
        other_operators(c, 1, lines - 1)

        @pl.when(c == 0)
        def _():
            for j in range(lines):
                held = all_fields.at[line_at(j) * 2 + 1 - across, core]
                wait(held, field_row.at[j])
                send(held, held, field_send.at[0], field_core.at[2], partner)
            wait(all_fields.at[pl.ds(0, lines), 0], field_core.at[2])

        other_operators(c, lines, lines)

    rotated_load.wait()
    turned(rotated_raw, rotated, 0, nchol)
    walker_load.wait()

    def taylor(c):
        group = 4

        @pl.loop(0, blocks // group)
        def _(g):
            ops, terms, sums = [], [], []
            for u in range(group):
                r = g * group + u
                chip, q = lax.rem(r, pairs), r // pairs
                ops.append(
                    jnp.concatenate(
                        [
                            op_recv[c, o, steps_from(o, chip), q]
                            for o in range(blocks)
                        ],
                        axis=0,
                    )
                )
                entry = jnp.maximum(send_walker[c, chip * 2 + q], 0)
                terms.append(walkers[entry])
                sums.append(terms[u].astype(f32))
            for degree in range(1, degrees + 1):
                for u in range(group):
                    product = lax.dot_general(
                        terms[u], ops[u], (((1,), (1,)), ((), ())), preferred_element_type=f32
                    )
                    terms[u] = (product * (1.0 / degree)).astype(bf16)
                    sums[u] = sums[u] + terms[u].astype(f32)
            for u in range(group):
                r = g * group + u
                nw_full[c, r] = sums[u].astype(bf16)

        for o in range(0, blocks, 16 // elec):
            block = jnp.swapaxes(nw_full[c, :, o * elec : o * elec + 16], 0, 1)
            for e in range(16):
                low = e % elec * orbitals
                nw_send[c, o + e // elec, :, low : low + orbitals] = block[e]

        def to_owner(o):
            send(nw_send.at[c, o], nw_recv.at[c, me], nw_sent.at[c], nw_got.at[c], o)

        everyone(to_owner)
        nw_recv[c, me] = nw_send[c, me]

    def send_walkers(c):
        mine = pl.ds(pl.multiple_of(side * near, near), near)

        def to_slot(d):
            @pl.when(d // half != side)
            def _():
                send(
                    nw_full.at[c, row_of(d), mine],
                    branch.at[c, me, mine],
                    br_sent.at[0],
                    br_got.at[0],
                    d,
                )

            @pl.when(d // half == side)
            def _():
                send(nw_full.at[c, row_of(d)], branch.at[c, me], br_sent.at[0], br_got.at[0], d)

        everyone(to_slot)
        branch[c, me] = nw_full[c, row_of(me)]

    def bias(c):
        rows_in = nw_recv[c].reshape(blocks * blocks, elec * orbitals)
        step = min(256, nchol)

        @pl.loop(0, nchol // step)
        def _(n):
            at = pl.ds(pl.multiple_of(n * step, step), step)
            out = lax.dot_general(
                rows_in, rotated[at, :], (((1,), (1,)), ((), ())), preferred_element_type=f32
            ).reshape(blocks, 2, pairs, step)
            for q in range(2):
                mine = out[:, q].reshape(blocks * pairs, step)
                for h in range(step // 128):
                    part[c, q, n * (step // 128) + h] = mine[:, h * 128 : (h + 1) * 128]

        send(part.at[c, 1 - core], pair_recv.at[c], pair_sent.at[c], pair_got.at[c], partner)

    def reduced(c, chip, h):
        at = pl.ds(chip, blocks, stride=pairs)
        return part[c, core, h, at, :] + pair_recv[c, h, at, :]

    def reduce(c):
        wait(pair_recv.at[c], pair_got.at[c])

        def pick(z, carry):
            for h in range(nchol // 128):
                both = reduced(c, z * 2 + 1 - across, h)
                row_send[c, z, :, h * 128 : (h + 1) * 128] = both.astype(bf16)
            return carry

        lax.fori_loop(0, lines, pick, 0)
        send(row_send.at[c], row_recv.at[c], row_sent.at[c], row_got.at[c], beside)

    def spread(c):
        wait(row_recv.at[c], row_got.at[c])

        def pick(z, carry):
            for h in range(nchol // 128):
                low = h * 128
                both = reduced(c, z * 2 + across, h)
                both = both + row_recv[c, z, :, low : low + 128].astype(f32)
                fb_send[c, z, :, low : low + 128] = both.astype(bf16)
            return carry

        lax.fori_loop(0, lines, pick, 0)

        def step(k, carry):
            z = lax.rem(line + k, lines)
            send(
                fb_send.at[c, z],
                fb_recv.at[c, line],
                fb_sent.at[c],
                fb_got.at[c],
                (z * 2 + across) * 2 + core,
            )
            return carry

        lax.fori_loop(1, lines, step, 0)
        fb_recv[c, line] = fb_send[c, line]

    def finish(c):
        wait(fb_recv.at[c, pl.ds(0, lines - 1)], fb_got.at[c])
        fb_total[c] = lax.fori_loop(
            1,
            lines,
            lambda s, acc: acc + fb_recv[c, s].astype(f32),
            fb_recv[c, 0].astype(f32),
        )

    def forward():
        count = half * blocks
        for c in range(cap):
            block = nw_recv[c, pl.ds(away * half, half)].astype(f32)
            block = block.reshape(count, elec * orbitals)
            for h in range(elec * orbitals // 128):
                fw_wide[h, c * count : (c + 1) * count] = block[:, h * 128 : (h + 1) * 128]

        def gather(t, carry):
            at = pl.ds(row_of(side * half + t), cap * half, stride=blocks)
            for h in range(elec * orbitals // 128):
                fw_send[t, :, h * 128 : (h + 1) * 128] = fw_wide[h, at, :].astype(bf16)
            return carry

        lax.fori_loop(0, half, gather, 0)

        def step(k, carry):
            t = lax.rem(local + k, half)
            send(fw_send.at[t], fw_recv.at[local], fw_sent.at[0], fw_got.at[0], side * half + t)
            return carry

        lax.fori_loop(1, half, step, 0)
        fw_recv[local] = fw_send[local]

    def collect():
        wait(fw_recv.at[pl.ds(0, half - 1)], fw_got.at[0])

        def fold(o, carry):
            block = fw_recv[o].astype(f32)
            for e in range(elec):
                for h in range(halves):
                    low = e * orbitals + h * 128
                    fw_rows[h, pl.ds(o * elec + e, cap * half, stride=near), :] = block[
                        :, low : low + 128
                    ]
            return carry

        lax.fori_loop(0, half, fold, 0)
        wait(branch.at[:, pl.ds(0, half - 1 + half // 2)], br_got.at[0])

        def put(s, carry):
            for c in range(cap):
                at = pl.ds(pl.multiple_of((c * half + s) * near, near), near)
                value = jnp.concatenate([fw_rows[h, at, :] for h in range(halves)], axis=1)
                mine = pl.ds(pl.multiple_of(side * near, near), near)
                branch[c, away * half + s, mine] = value.astype(bf16)
            return carry

        lax.fori_loop(0, half, put, 0)

    wait(op_recv.at[:, pl.ds(0, blocks - 1), 0], op_got.at[cap])
    for c in range(cap):
        wait(op_recv.at[c, pl.ds(0, blocks - 1), pl.ds(1, pairs - 1)], op_got.at[c])
        taylor(c)
    for c in range(cap):
        send_walkers(c)
    for c in range(cap):
        wait(nw_recv.at[c, pl.ds(0, blocks - 1)], nw_got.at[c])
        bias(c)
        reduce(c)
        if c == cap - 1:
            forward()
        spread(c)
    collect()
    for c in range(cap):
        finish(c)

    wait(all_fields.at[:, 0], field_send.at[0])
    wait(all_fields.at[pl.ds(0, lines), 0], field_send.at[1])

    @pl.when(rank == 0)
    def _():
        wait(all_fields.at[pl.ds(0, 4), 0], field_send.at[2])

    @pl.when(rank == 1)
    def _():
        wait(all_fields.at[pl.ds(0, 2), 0], field_send.at[2])

    wait(op_recv.at[:, pl.ds(0, blocks - 1), 0], op_sent.at[cap])
    wait(branch.at[:, pl.ds(0, half - 1 + half // 2)], br_sent.at[0])
    wait(fw_send.at[pl.ds(0, half - 1)], fw_sent.at[0])
    for c in range(cap):
        wait(op_recv.at[c, pl.ds(0, blocks - 1), pl.ds(1, pairs - 1)], op_sent.at[c])
        wait(nw_send.at[c, pl.ds(0, blocks - 1)], nw_sent.at[c])
        wait(pair_recv.at[c], pair_sent.at[c])
        wait(row_send.at[c], row_sent.at[c])
        wait(fb_send.at[c, pl.ds(0, lines - 1)], fb_sent.at[c])


def place_kernel(slot_row, branch, fb_total, new_walkers, force_bias):
    cap = branch.shape[0]

    @pl.loop(0, slot_row.shape[0])
    def _(p):
        entry = slot_row[p]
        c, s = lax.rem(entry, cap), entry // cap
        new_walkers[p] = branch[c, s]
        force_bias[pl.ds(p, 1), :] = fb_total[c, pl.ds(s, 1), :]


def parent_shards(blocks, walkers, fields, chol_vectors, rotated, send_walker, slot_row):
    slots, electrons, orbitals = walkers.shape
    nchol, rows, _ = chol_vectors.shape
    elec = rotated.shape[1]
    cap = send_walker.shape[-1]
    bf16, f32 = jnp.bfloat16, jnp.float32
    pairs, lines, half = blocks // 2, blocks // 4, blocks // 2
    halves, near = orbitals // 128, electrons // 2
    most = max(pairs // 2 * 2 * blocks, slots)
    wide = elec * orbitals
    vmem, smem, anywhere = (
        pl.BlockSpec(memory_space=m) for m in (pltpu.VMEM, pltpu.SMEM, pl.ANY)
    )
    dma = pltpu.SemaphoreType.DMA
    branch, fb_total = pl.pallas_call(
        functools.partial(parent_kernel, (blocks, cap, rows, elec)),
        out_shape=(
            jax.ShapeDtypeStruct((cap, blocks, electrons, orbitals), bf16),
            jax.ShapeDtypeStruct((cap, blocks, nchol), f32),
        ),
        in_specs=[smem, smem, vmem, anywhere, anywhere, anywhere],
        out_specs=(vmem, vmem),
        scratch_shapes=[
            pltpu.VMEM(walkers.shape, bf16),
            pltpu.VMEM(chol_vectors.shape, bf16),
            pltpu.VMEM((nchol, rows * orbitals), bf16),
            pltpu.VMEM(rotated.shape, bf16),
            pltpu.VMEM((nchol, wide), bf16),
            pltpu.VMEM((pairs, 2, slots, nchol), bf16),
            pltpu.VMEM((most, nchol), bf16),
            pltpu.VMEM((rows, most, orbitals), bf16),
            pltpu.VMEM((cap, blocks, pairs, 2, rows, orbitals), bf16),
            pltpu.VMEM((cap, blocks, pairs, 2, rows, orbitals), bf16),
            pltpu.VMEM((cap, blocks, electrons, orbitals), bf16),
            pltpu.VMEM((cap, blocks, blocks, wide), bf16),
            pltpu.VMEM((cap, blocks, blocks, wide), bf16),
            pltpu.VMEM((cap, 2, nchol // 128, blocks * pairs, 128), f32),
            pltpu.VMEM((cap, nchol // 128, blocks * pairs, 128), f32),
            pltpu.VMEM((cap, lines, blocks, nchol), bf16),
            pltpu.VMEM((cap, lines, blocks, nchol), bf16),
            pltpu.VMEM((cap, lines, blocks, nchol), bf16),
            pltpu.VMEM((cap, lines, blocks, nchol), bf16),
            pltpu.VMEM((wide // 128, cap * half * blocks, 128), f32),
            pltpu.VMEM((half, cap * half, wide), bf16),
            pltpu.VMEM((half, cap * half, wide), bf16),
            pltpu.VMEM((halves, cap * half * near, 128), f32),
            dma((6,)),
            dma((3,)),
            dma((3,)),
            dma((lines,)),
            dma((lines,)),
            dma((cap + 1,)),
            dma((cap + 1,)),
            dma((cap,)),
            dma((cap,)),
            dma((1,)),
            dma((1,)),
            dma((cap,)),
            dma((cap,)),
            dma((cap,)),
            dma((cap,)),
            dma((cap,)),
            dma((cap,)),
            dma((1,)),
            dma((1,)),
        ],
        compiler_params=pltpu.CompilerParams(
            collective_id=1, has_side_effects=True, vmem_limit_bytes=60 * 1024 * 1024
        ),
    )(
        jnp.transpose(send_walker, (0, 2, 1)).reshape(cap, blocks),
        slot_row,
        fields,
        walkers,
        chol_vectors,
        rotated,
    )
    return pl.pallas_call(
        place_kernel,
        out_shape=(
            jax.ShapeDtypeStruct(walkers.shape, bf16),
            jax.ShapeDtypeStruct((slots, nchol), f32),
        ),
        in_specs=[smem, vmem, vmem],
        out_specs=(vmem, vmem),
    )(slot_row, branch, fb_total)


def plan(blocks, walkers, fields, chol_vectors, rotated, send_walker, slot_row):
    every_entry = blocks * send_walker.shape[-1] == walkers.shape[0]
    step = parent_shards if every_entry and blocks == 4 * 2 * 2 else shards
    return step(blocks, walkers, fields, chol_vectors, rotated, send_walker, slot_row)


def solution(mesh):
    in_specs = (
        P(("grp", "chol"), None, None),
        P(("grp", "chol"), None),
        P(None, "chol", None),
        P(None, "chol", None),
        P(("grp", "chol"), None, None),
        P(("grp", "chol")),
    )
    out_specs = (P(("grp", "chol"), None, None), P(("grp", "chol"), None))
    return jax.shard_map(
        functools.partial(plan, mesh.shape["chol"]),
        mesh=mesh,
        in_specs=in_specs,
        out_specs=out_specs,
        check_vma=False,
    )
```
